32 devices in a mesh: dp: 8 (over z, x), tensor: 4 (over y, core).
Axes of the slice: x: 2, y: 2, z: 4, core: 2. Of those that a mesh axis runs over, the one named last changes fastest.
Arguments:
- tokens: bfloat16 [16384, 768], P(('dp', 'tensor')), may hold values from -6 to 6
- w_query: bfloat16 [768, 768], P(None, 'tensor'), may hold values from -0.3125 to 0.3125
- w_key: bfloat16 [768, 768], P(None, 'tensor'), may hold values from -0.3125 to 0.3125
- w_value: bfloat16 [768, 768], P(None, 'tensor'), may hold values from -0.21875 to 0.21875
- b_query: bfloat16 [768], P('tensor'), may hold values from -3 to 3
- b_value: bfloat16 [768], P('tensor'), may hold values from -3 to 3
- w_output: bfloat16 [768, 768], P('tensor'), may hold values from -0.375 to 0.375
- b_output: bfloat16 [768], replicated, may hold values from -3 to 3
- first_gain: bfloat16 [768], replicated, may hold values from 0.5 to 1.5
- first_shift: bfloat16 [768], replicated, may hold values from -3 to 3
- w_up: bfloat16 [768, 3072], P(None, 'tensor'), may hold values from -0.21875 to 0.21875
- b_up: bfloat16 [3072], P('tensor'), may hold values from -3 to 3
- w_down: bfloat16 [3072, 768], P('tensor'), may hold values from -0.15625 to 0.15625
- b_down: bfloat16 [768], replicated, may hold values from -3 to 3
- second_gain: bfloat16 [768], replicated, may hold values from 0.5 to 1.5
- second_shift: bfloat16 [768], replicated, may hold values from -3 to 3
- cotangent: bfloat16 [16384, 768], P(('dp', 'tensor')), may hold values from -24 to 24, as said below
Outputs:
- layer_out: bfloat16 [16384, 768], P(('dp', 'tensor'))
- grad_tokens: bfloat16 [16384, 768], P(('dp', 'tensor'))
- grad_w_query: float32 [768, 768], P(None, 'tensor')
- grad_w_key: float32 [768, 768], P(None, 'tensor')
- grad_w_value: float32 [768, 768], P(None, 'tensor')
- grad_b_query: float32 [768], P('tensor')
- grad_b_value: float32 [768], P('tensor')
- grad_w_output: float32 [768, 768], P('tensor')
- grad_b_output: float32 [768], replicated
- grad_first_gain: float32 [768], replicated
- grad_first_shift: float32 [768], replicated
- grad_w_up: float32 [768, 3072], P(None, 'tensor')
- grad_b_up: float32 [3072], P('tensor')
- grad_w_down: float32 [3072, 768], P('tensor')
- grad_b_down: float32 [768], replicated
- grad_second_gain: float32 [768], replicated
- grad_second_shift: float32 [768], replicated
The draws below stay inside these ranges and needn't reach their ends.
Inputs may be any that keep to these rules, and one draw needn't show every extreme that they name: cotangent of the layer's output.
All inputs are finite; a program needn't handle non-finite values.
Results may differ from the reference program's by a relative error of at most 0.013.
The reference program's roundings to bfloat16 on the way count: a program that leaves them out, or rounds other values in their place, can miss the bound.
Values may be sent and summed in bfloat16 or wider, within the bound.
No kernel may reach another device: no remote copies, remote signals or barrier semaphores. Data moves between devices by JAX's collectives and lax.ppermute only.
A program may use at most 128 MiB of HBM per device.

```python
import jax
import jax.numpy as jnp
from jax import lax

D = 768
HEADS = 12
HEAD = 64
FF = 3072
SEQ_LEN = 512
TOKENS = 16384


def draw_cotangent(key, part):
    position = jnp.arange(TOKENS, dtype=jnp.float32)[:, None] / TOKENS
    growth = jnp.exp(jnp.log(3.0) * position)
    sample = jax.random.truncated_normal(key, -4.0, 4.0, (TOKENS, D), jnp.float32)
    return (sample * growth).astype(jnp.bfloat16)


def level_of(key, extent, shards, low, largest):
    loudness = 1.0
    for axis_at, shards_of in shards:
        steps = jax.random.uniform(jax.random.fold_in(jax.random.fold_in(key, 6), axis_at), (shards_of,), jnp.float32, low / len(shards), largest / len(shards))
        loudness = loudness * jnp.repeat(jnp.exp(steps), extent[axis_at] // shards_of).reshape((-1,) + (1,) * (len(extent) - 1 - axis_at))
    return loudness


def scatter_about(rng, shape, scale, most, pieces=(), held_as=jnp.bfloat16):
    factor_of = level_of(rng, shape, pieces, -0.22, 0.18) if pieces else 1.0
    entries = jax.random.normal(rng, shape, jnp.float32) * scale * factor_of
    return jnp.minimum(jnp.maximum(entries, -most), most).astype(held_as)


def setup_inputs(seed: int = 0) -> dict:
    streams_of = jax.random.split(jax.random.key(seed), 18)
    tokens = scatter_about(streams_of[0], (TOKENS, D), 1.0, 6.0, ((0, 32),))
    w_query = scatter_about(streams_of[1], (D, D), (D // 2) ** -0.5, 0.3125, ((1, 4),))
    w_key = scatter_about(streams_of[2], (D, D), (D // 2) ** -0.5, 0.3125, ((1, 4),))
    w_value = scatter_about(streams_of[3], (D, D), D ** -0.5, 0.21875, ((1, 4),))
    b_query = scatter_about(streams_of[4], (D,), 0.5, 3.0, ((0, 4),))
    b_value = scatter_about(streams_of[5], (D,), 0.5, 3.0, ((0, 4),))
    w_output = scatter_about(streams_of[6], (D, D), (D // 3) ** -0.5, 0.375, ((0, 4),))
    b_output = scatter_about(streams_of[7], (D,), 0.5, 3.0)
    first_gain = jnp.clip(1.0 + 0.1 * jax.random.normal(streams_of[8], (D,), jnp.float32), 0.5, 1.5).astype(jnp.bfloat16)
    first_shift = scatter_about(streams_of[9], (D,), 0.5, 3.0)
    w_up = scatter_about(streams_of[10], (D, FF), D ** -0.5, 0.21875, ((1, 4),))
    b_up = scatter_about(streams_of[11], (FF,), 0.5, 3.0, ((0, 4),))
    w_down = scatter_about(streams_of[12], (FF, D), (FF // 2) ** -0.5, 0.15625, ((0, 4),))
    b_down = scatter_about(streams_of[13], (D,), 0.5, 3.0)
    second_gain = jnp.clip(1.0 + 0.1 * jax.random.normal(streams_of[14], (D,), jnp.float32), 0.5, 1.5).astype(jnp.bfloat16)
    second_shift = scatter_about(streams_of[15], (D,), 0.5, 3.0)
    cotangent = draw_cotangent(jax.random.fold_in(streams_of[17], 71), 0)
    return {"tokens": tokens, "w_query": w_query, "w_key": w_key, "w_value": w_value, "b_query": b_query, "b_value": b_value, "w_output": w_output, "b_output": b_output, "first_gain": first_gain, "first_shift": first_shift, "w_up": w_up, "b_up": b_up, "w_down": w_down, "b_down": b_down, "second_gain": second_gain, "second_shift": second_shift, "cotangent": cotangent}


@jax.custom_vjp
def low(v):
    return lax.optimization_barrier(v.astype(jnp.bfloat16)).astype(jnp.float32)

@jax.custom_vjp
def low_back(v):
    return v

def low_keep(v):
    return (low(v), None)

def low_pass(kept, grad):
    return (grad,)

def back_keep(v):
    return (v, None)

def back_low(kept, grad):
    return (low(grad),)
low.defvjp(low_keep, low_pass)
low_back.defvjp(back_keep, back_low)

def matmul(left, right):
    return jnp.dot(left, right, precision=lax.Precision.HIGHEST, preferred_element_type=jnp.float32)

def layer_norm(values, gain_row, shift_row):
    center = values - lax.optimization_barrier(jnp.mean(values, axis=-1, keepdims=True))
    spread = lax.optimization_barrier(jnp.mean(center * center, axis=-1, keepdims=True))
    return center * lax.rsqrt(spread + 1e-12) * gain_row + shift_row

def encoder_layer(inputs, w_query, w_key, w_value, b_query, b_value, w_output, b_output, first_gain, first_shift, w_up, b_up, w_down, b_down, second_gain, second_shift):
    length = inputs.shape[0]
    queries = low(low_back(matmul(inputs, w_query) + b_query)).reshape(length, HEADS, HEAD)
    key_rows = low(low_back(matmul(inputs, w_key))).reshape(length, HEADS, HEAD)
    value_rows = low(low_back(matmul(inputs, w_value) + b_value)).reshape(length, HEADS, HEAD)
    scores = low_back(jnp.einsum('qhd,khd->hqk', queries, key_rows, precision=lax.Precision.HIGHEST) * 0.125)
    soft_probs = low(jax.nn.softmax(scores, axis=-1))
    attended = jnp.einsum('hqk,khd->qhd', soft_probs, value_rows, precision=lax.Precision.HIGHEST).reshape(length, D)
    attended = low(low_back(attended))
    first_sum = low_back(matmul(attended, w_output)) + b_output + inputs
    normed = layer_norm(first_sum, first_gain, first_shift)
    up_rows = low_back(matmul(low(normed), w_up) + b_up)
    active = low(jax.nn.gelu(up_rows, approximate=False))
    second_sum = low_back(matmul(active, w_down)) + b_down + normed
    return layer_norm(second_sum, second_gain, second_shift)

def reference(tokens, w_query, w_key, w_value, b_query, b_value, w_output, b_output, first_gain, first_shift, w_up, b_up, w_down, b_down, second_gain, second_shift, cotangent):
    weights = tuple((entry.astype(jnp.float32) for entry in (w_query, w_key, w_value, b_query, b_value, w_output, b_output, first_gain, first_shift, w_up, b_up, w_down, b_down, second_gain, second_shift)))
    seq_count = TOKENS // SEQ_LEN
    seq_inputs = tokens.astype(jnp.float32).reshape(seq_count, SEQ_LEN, D)
    seq_cots = cotangent.astype(jnp.float32).reshape(seq_count, SEQ_LEN, D)

    def one_step(totals, pair_rows):
        seq_in, seq_cot = pair_rows
        result, puller = jax.vjp(encoder_layer, seq_in, *weights)
        grad_list = puller(seq_cot)
        totals = tuple((total_sum + grad_part for total_sum, grad_part in zip(totals, grad_list[1:])))
        return (totals, (result.astype(jnp.bfloat16), grad_list[0].astype(jnp.bfloat16)))
    zero_grads = tuple((jnp.zeros_like(entry) for entry in weights))
    totals, (layer_rows, input_grads) = lax.scan(one_step, zero_grads, (seq_inputs, seq_cots))
    return (layer_rows.reshape(TOKENS, D), input_grads.reshape(TOKENS, D), totals[0], totals[1], totals[2], totals[3], totals[4], totals[5], totals[6], totals[7], totals[8], totals[9], totals[10], totals[11], totals[12], totals[13], totals[14])
```

```python
import jax
import jax.numpy as jnp
from jax import lax
from jax.sharding import PartitionSpec as P

HEAD = 64
SEQ_LEN = 512
BF = jnp.bfloat16
F32 = jnp.float32


def layer_norm(values, gain_row, shift_row):
    center = values - jnp.mean(values, axis=-1, keepdims=True)
    spread = jnp.mean(center * center, axis=-1, keepdims=True)
    return center * lax.rsqrt(spread + 1e-12) * gain_row + shift_row


def gelu_exact(values):
    return jax.nn.gelu(values, approximate=False)


def contract(left, right, dims):
    return lax.dot_general(left, right, (dims, ((), ())), preferred_element_type=F32)


def nn(left, right):
    return contract(left, right, ((1,), (0,)))


def nt(left, right):
    return contract(left, right, ((1,), (1,)))


def tn(left, right):
    return contract(left, right, ((0,), (0,)))


def swap(value, axis, bit):
    size = lax.axis_size(axis)
    return lax.ppermute(value, axis, [(i, i ^ bit) for i in range(size)])


def gather_shards(own):
    partner = swap(own, "tensor", 1)
    across = swap(own, "tensor", 2)
    across_partner = swap(across, "tensor", 1)
    return [own, partner, across, across_partner]


def half(value, which):
    rows = value.shape[0] // 2
    return lax.dynamic_slice_in_dim(value, which * rows, rows, 0)


def reduce_shards(parts):
    got = swap(jnp.stack([parts[1].astype(BF), parts[3].astype(BF)]), "tensor", 1)
    keep = parts[0] + got[0].astype(F32)
    send = (parts[2] + got[1].astype(F32)).astype(BF)
    keep = keep + swap(send, "tensor", 2).astype(F32)
    index = lax.axis_index("dp")
    bits = []
    bit = 1
    while bit < lax.axis_size("dp"):
        bits.append(bit)
        bit *= 2
    for bit in bits:
        mine = (index // bit) % 2
        got = swap(half(keep, 1 - mine).astype(BF), "dp", bit)
        keep = half(keep, mine) + got.astype(F32)
    full = keep.astype(BF)
    for bit in reversed(bits):
        mine = (index // bit) % 2
        got = swap(full, "dp", bit)
        low = jnp.where(mine == 0, full, got)
        high = jnp.where(mine == 0, got, full)
        full = jnp.concatenate([low, high], axis=0)
    return full.astype(F32)


def reduce_all(value):
    for axis in ("tensor", "dp"):
        bit = 1
        while bit < lax.axis_size(axis):
            value = value + swap(value, axis, bit)
            bit *= 2
    return value


def attend_forward(queries, key_rows, value_rows):
    scores = jnp.einsum("qhd,khd->hqk", queries, key_rows, preferred_element_type=F32) * 0.125
    highest = jnp.max(scores, axis=-1, keepdims=True)
    unnorm = jnp.exp(scores - highest)
    totals = jnp.sum(unnorm, axis=-1, keepdims=True)
    soft_probs = (unnorm / totals).astype(BF)
    attended = jnp.einsum("hqk,khd->qhd", soft_probs, value_rows, preferred_element_type=F32)
    return attended.astype(BF), highest + jnp.log(totals)


def attend_backward(queries, key_rows, value_rows, grad_att, log_total):
    scores = jnp.einsum("qhd,khd->hqk", queries, key_rows, preferred_element_type=F32) * 0.125
    soft_probs = jnp.exp(scores - log_total)
    grad_prob = jnp.einsum("qhd,khd->hqk", grad_att, value_rows, preferred_element_type=F32)
    inner_sum = jnp.sum(soft_probs * grad_prob, axis=-1, keepdims=True)
    grad_score = (soft_probs * (grad_prob - inner_sum)).astype(BF)
    grad_query = (
        jnp.einsum("hqk,khd->qhd", grad_score, key_rows, preferred_element_type=F32) * 0.125
    ).astype(BF)
    grad_key = (
        jnp.einsum("hqk,qhd->khd", grad_score, queries, preferred_element_type=F32) * 0.125
    ).astype(BF)
    grad_value = jnp.einsum(
        "hqk,qhd->khd", soft_probs.astype(BF), grad_att, preferred_element_type=F32
    ).astype(BF)
    return grad_query, grad_key, grad_value


def on_device(
    tokens,
    w_query,
    w_key,
    w_value,
    b_query,
    b_value,
    w_output,
    b_output,
    first_gain,
    first_shift,
    w_up,
    b_up,
    w_down,
    b_down,
    second_gain,
    second_shift,
    cotangent,
):
    rows, width = tokens.shape
    local = w_query.shape[1]
    heads = local // HEAD
    seqs = rows // SEQ_LEN
    assert seqs == 1
    hidden = w_up.shape[1]

    bias_rows = jnp.zeros((16, width), BF)
    bias_rows = bias_rows.at[0, :local].set(b_query).at[0, local : 2 * local].set(b_value)
    bias_rows = bias_rows.at[1, :hidden].set(b_up)
    pack = jnp.concatenate([w_query.T, w_key.T, w_value.T, w_output, bias_rows], axis=0)
    attn_w = gather_shards(pack)
    up_w = gather_shards(w_up)
    down_w = gather_shards(w_down)

    def split(block):
        return block.reshape(rows, heads, HEAD)

    saved = []
    attention = jnp.zeros((rows, width), F32)
    for shard in attn_w:
        bias = shard[4 * local].astype(F32)
        proj = nt(tokens, shard[: 3 * local])
        queries = split((proj[:, :local] + bias[:local]).astype(BF))
        key_rows = split(proj[:, local : 2 * local].astype(BF))
        value_rows = split((proj[:, 2 * local :] + bias[local : 2 * local]).astype(BF))
        attended, log_total = attend_forward(queries, key_rows, value_rows)
        attended = attended.reshape(rows, local)
        attention = attention + nn(attended, shard[3 * local : 4 * local])
        saved.append((queries, key_rows, value_rows, attended, log_total))
    first_sum = attention + b_output.astype(F32) + tokens.astype(F32)
    normed, first_pull = jax.vjp(
        layer_norm, first_sum, first_gain.astype(F32), first_shift.astype(F32)
    )
    normed_low = normed.astype(BF)

    feed = jnp.zeros((rows, width), F32)
    acts = []
    for shard, up_s, down_s in zip(attn_w, up_w, down_w):
        up_rows = nn(normed_low, up_s) + shard[4 * local + 1, :hidden].astype(F32)
        active, pull = jax.vjp(gelu_exact, up_rows)
        active = active.astype(BF)
        feed = feed + nn(active, down_s)
        acts.append((active, pull))
    second_sum = feed + b_down.astype(F32) + normed
    layer_out, second_pull = jax.vjp(
        layer_norm, second_sum, second_gain.astype(F32), second_shift.astype(F32)
    )
    grad_second, grad_second_gain, grad_second_shift = second_pull(cotangent.astype(F32))
    grad_b_down = jnp.sum(grad_second, axis=0)
    down_low = grad_second.astype(BF)

    down_grads = [tn(active, down_low) for active, _ in acts]
    grad_w_down = reduce_shards(down_grads)
    grad_normed = grad_second
    up_grads, grad_b_up = [], []
    for (active, pull), up_s, down_s in zip(acts, up_w, down_w):
        grad_up = pull(nt(down_low, down_s))[0].astype(BF)
        grad_b_up.append(jnp.sum(grad_up, axis=0, dtype=F32))
        up_grads.append(tn(normed_low, grad_up))
        grad_normed = grad_normed + nt(grad_up, up_s)
    grad_w_up = reduce_shards(up_grads)

    grad_first, grad_first_gain, grad_first_shift = first_pull(grad_normed)
    grad_b_output = jnp.sum(grad_first, axis=0)
    first_low = grad_first.astype(BF)

    grad_tokens = grad_first
    attn_grads, grad_b_query, grad_b_value = [], [], []
    for shard, (queries, key_rows, value_rows, attended, log_total) in zip(attn_w, saved):
        grad_wo = tn(attended, first_low)
        grad_att = split(nt(first_low, shard[3 * local : 4 * local]).astype(BF))
        pieces = attend_backward(queries, key_rows, value_rows, grad_att, log_total)
        joined = jnp.concatenate([p.reshape(rows, local) for p in pieces], axis=1)
        grad_b_query.append(jnp.sum(joined[:, :local], axis=0, dtype=F32))
        grad_b_value.append(jnp.sum(joined[:, 2 * local :], axis=0, dtype=F32))
        attn_grads.append(jnp.concatenate([tn(joined, tokens), grad_wo], axis=0))
        grad_tokens = grad_tokens + nn(joined, shard[: 3 * local])
    grad_attn = reduce_shards(attn_grads)

    mine = lax.axis_index("tensor")

    def natural(pieces):
        laid = [None] * 4
        stacked = jnp.stack(pieces)
        for t in range(4):
            laid[t] = lax.dynamic_index_in_dim(stacked, mine ^ t, 0, keepdims=False)
        return jnp.concatenate(laid)

    small = [
        natural(grad_b_query),
        natural(grad_b_value),
        natural(grad_b_up),
        grad_b_output,
        grad_first_gain,
        grad_first_shift,
        grad_b_down,
        grad_second_gain,
        grad_second_shift,
    ]
    sizes = [s.shape[0] for s in small]
    total = reduce_all(jnp.concatenate(small).reshape(-1, 128)).reshape(-1)
    out, at = [], 0
    for size in sizes:
        out.append(total[at : at + size])
        at += size
    g_bq, g_bv, g_bup, g_bo, g_fg, g_fs, g_bd, g_sg, g_ss = out

    def own(vector):
        size = vector.shape[0] // 4
        return lax.dynamic_slice_in_dim(vector, mine * size, size, 0)

    return (
        layer_out.astype(BF),
        grad_tokens.astype(BF),
        grad_attn[:local].T,
        grad_attn[local : 2 * local].T,
        grad_attn[2 * local : 3 * local].T,
        own(g_bq),
        own(g_bv),
        grad_attn[3 * local :],
        g_bo,
        g_fg,
        g_fs,
        grad_w_up,
        own(g_bup),
        grad_w_down,
        g_bd,
        g_sg,
        g_ss,
    )


def solution(mesh):
    rows = P(("dp", "tensor"), None)
    col, row, vec, rep = P(None, "tensor"), P("tensor", None), P("tensor"), P()
    return jax.shard_map(
        on_device,
        mesh=mesh,
        in_specs=(
            rows, col, col, col, vec, vec, row, rep, rep, rep, col, vec, row, rep, rep, rep, rows,
        ),
        out_specs=(
            rows, rows, col, col, col, vec, vec, row, rep, rep, rep, col, vec, row, rep, rep, rep,
        ),
        check_vma=False,
    )
```

```python
import functools

import jax
import jax.numpy as jnp
from jax import lax
from jax.experimental import pallas as pl
from jax.experimental.pallas import tpu as pltpu
from jax.sharding import PartitionSpec as P

HEAD = 64
SEQ_LEN = 512
BIAS_ROWS = 16
BF = jnp.bfloat16
F32 = jnp.float32
ANY = pl.BlockSpec(memory_space=pl.ANY)
VMEM_BYTES = 60 << 20


def dot(left, right, left_dim, right_dim):
    return lax.dot_general(
        left, right, (((left_dim,), (right_dim,)), ((), ())), preferred_element_type=F32
    )


def whole(shape):
    return pl.BlockSpec(shape, lambda *_: (0,) * len(shape))


def pair(shape):
    return pl.BlockSpec((1, *shape), lambda s, *_: (s, *(0,) * len(shape)))


def params():
    return pltpu.CompilerParams(vmem_limit_bytes=VMEM_BYTES)


def cost(flops, moved):
    return pl.CostEstimate(flops=int(flops), bytes_accessed=int(moved), transcendentals=0)


class Quarters:
    def __init__(self, source, target, order, sem):
        rows = target.shape[0] // 4
        self.copies = [
            pltpu.make_async_copy(
                source.at[pl.ds(i * rows, rows)],
                target.at[pl.ds(pl.multiple_of((order ^ i) * rows, rows), rows)],
                sem,
            )
            for i in range(4)
        ]

    def start(self):
        for copy in self.copies:
            copy.start()

    def wait(self):
        for copy in self.copies:
            copy.wait()


def pack_kernel(wq, wk, wv, wo, bq, bv, bu, out):
    local = wq.shape[1]
    for at, ref in enumerate((wq, wk, wv)):
        out[at * local : (at + 1) * local, :] = jnp.transpose(ref[...].astype(F32)).astype(BF)
    out[3 * local : 4 * local, :] = wo[...]
    out[4 * local :, :] = jnp.zeros((out.shape[0] - 4 * local, out.shape[1]), BF)
    out[4 * local : 4 * local + 1, 0:local] = bq[...]
    out[4 * local : 4 * local + 1, local : 2 * local] = bv[...]
    out[4 * local + 1 : 4 * local + 2, 0 : bu.shape[1]] = bu[...]


def pack_attention(w_query, w_key, w_value, w_output, b_query, b_value, b_up):
    width, local = w_query.shape
    return pl.pallas_call(
        pack_kernel,
        out_shape=jax.ShapeDtypeStruct((4 * local + BIAS_ROWS, width), BF),
        name="pack_attention",
    )(w_query, w_key, w_value, w_output, b_query[None], b_value[None], b_up[None])


def normalize(rows):
    center = rows - jnp.mean(rows, axis=-1, keepdims=True)
    scale = lax.rsqrt(jnp.mean(center * center, axis=-1, keepdims=True) + 1e-12)
    return center * scale, scale


def norm_back(grad, unit, scale):
    return scale * (
        grad
        - jnp.mean(grad, axis=-1, keepdims=True)
        - unit * jnp.mean(grad * unit, axis=-1, keepdims=True)
    )


def attention_kernel(last, *refs):
    if last:
        (order, tok, pa, pb, part_in, b_out, gain, shift,
         qkv, probs, att, normed_low, unit, scale, pack, part, sem) = refs
    else:
        order, tok, pa, pb, qkv, probs, att, part, pack, sem = refs
    step = pl.program_id(0)
    local = att.shape[1]
    at = order[0]
    body = 4 * local
    copies = []
    for i, ref in enumerate((pa, pb)):
        copies.append(
            (
                Quarters(ref.at[pl.ds(0, body)], pack.at[i, pl.ds(0, body)], at, sem.at[i]),
                pltpu.make_async_copy(
                    ref.at[pl.ds(body, BIAS_ROWS)], pack.at[i, pl.ds(body, BIAS_ROWS)], sem.at[i]
                ),
            )
        )

    @pl.when(step == 0)
    def _():
        for quarters, rest in copies:
            quarters.start()
            rest.start()
        for copy in copies[0]:
            copy.wait()

    @pl.when(step == 1)
    def _():
        for copy in copies[1]:
            copy.wait()

    weights = pack.at[step]
    bias = jnp.transpose(weights[body : body + BIAS_ROWS, :].astype(F32))
    tokens = tok[...]
    qkv[0, 0:local, :] = (
        dot(weights[0:local, :], tokens, 1, 1) + bias[0:local, 0:1]
    ).astype(BF) * BF(0.125)
    qkv[0, local : 2 * local, :] = dot(weights[local : 2 * local, :], tokens, 1, 1).astype(BF)
    qkv[0, 2 * local : 3 * local, :] = (
        dot(weights[2 * local : 3 * local, :], tokens, 1, 1) + bias[local : 2 * local, 0:1]
    ).astype(BF)
    for head in range(local // HEAD):
        here = head * HEAD
        queries = qkv[0, here : here + HEAD, :]
        keys = qkv[0, local + here : local + here + HEAD, :]
        values = qkv[0, 2 * local + here : 2 * local + here + HEAD, :]
        scores = dot(keys, queries, 0, 0)
        unnorm = jnp.exp(scores - jnp.max(scores, axis=0, keepdims=True))
        prob = (unnorm * (1.0 / jnp.sum(unnorm, axis=0, keepdims=True))).astype(BF)
        probs[0, head] = prob
        att[0, here : here + HEAD, :] = dot(values, prob, 1, 0).astype(BF)
    out = dot(att[0], weights[3 * local : 4 * local, :], 0, 0)

    @pl.when(step == 0)
    def _():
        part[...] = out + part_in[...] if last else out

    @pl.when(step > 0)
    def _():
        part[...] += out

    if last:

        @pl.when(step == 1)
        def _():
            block = 128

            def rows(i, carry):
                r = pl.ds(pl.multiple_of(i * block, block), block)
                total = part[r, :] + b_out[...].astype(F32) + tok[r, :].astype(F32)
                unit_rows, scale_rows = normalize(total)
                unit[r, :] = unit_rows
                scale[r, :] = scale_rows
                normed = unit_rows * gain[...].astype(F32) + shift[...].astype(F32)
                normed_low[r, :] = normed.astype(BF)
                return carry

            lax.fori_loop(0, tok.shape[0] // block, rows, 0)


def attention(order, tokens, packs, extra=None):
    rows, width = tokens.shape
    local = (packs[0].shape[0] - BIAS_ROWS) // 4
    heads = local // HEAD
    last = extra is not None
    ops = [tokens, *packs]
    in_specs = [whole((rows, width)), ANY, ANY]
    out_specs = [pair((3 * local, rows)), pair((heads, rows, rows)), pair((local, rows))]
    out_shape = [
        jax.ShapeDtypeStruct((2, 3 * local, rows), BF),
        jax.ShapeDtypeStruct((2, heads, rows, rows), BF),
        jax.ShapeDtypeStruct((2, local, rows), BF),
    ]
    scratch = [pltpu.VMEM((2, *packs[0].shape), BF)]
    if last:
        ops += extra
        in_specs += [whole((rows, width))] + [whole((1, width))] * 3
        out_specs += [whole((rows, width)), whole((rows, width)), whole((rows, 1))]
        out_shape += [
            jax.ShapeDtypeStruct((rows, width), BF),
            jax.ShapeDtypeStruct((rows, width), F32),
            jax.ShapeDtypeStruct((rows, 1), F32),
        ]
        scratch += [pltpu.VMEM((rows, width), F32)]
    else:
        out_specs += [whole((rows, width))]
        out_shape += [jax.ShapeDtypeStruct((rows, width), F32)]
    scratch += [pltpu.SemaphoreType.DMA((2,))]
    return pl.pallas_call(
        functools.partial(attention_kernel, last),
        grid_spec=pltpu.PrefetchScalarGridSpec(
            num_scalar_prefetch=1,
            grid=(2,),
            in_specs=in_specs,
            out_specs=out_specs,
            scratch_shapes=scratch,
        ),
        out_shape=out_shape,
        compiler_params=params(),
        cost_estimate=cost(5e9, 8e6),
        name="attention_last" if last else "attention",
    )(order, *ops)


def feed_kernel(last, *refs):
    if last:
        (order, low, ua, ub, da, db, ba, bb, part_in, unit, gain, shift, b_down, gain2, shift2, cot,
         act, slope, layer_out, down_low, grad_second, small, ga, gb,
         up, down, part, grads, kept, sem) = refs
    else:
        order, low, ua, ub, da, db, ba, bb, act, slope, part, up, down, sem = refs
    step = pl.program_id(0)
    at = order[0]
    copies = []
    for i, (u, d) in enumerate(((ua, da), (ub, db))):
        copies.append(
            (
                Quarters(u, up.at[i], at, sem.at[2 * i]),
                Quarters(d, down.at[i], at, sem.at[2 * i + 1]),
            )
        )

    @pl.when(step == 0)
    def _():
        for group in copies:
            for copy in group:
                copy.start()
        for copy in copies[0]:
            copy.wait()

    @pl.when(step == 1)
    def _():
        for copy in copies[1]:
            copy.wait()

    hidden = up.shape[2]
    bias = jnp.where(step == 0, ba[1:2, 0:hidden], bb[1:2, 0:hidden]).astype(F32)
    rows = dot(low[...], up[step], 1, 0) + bias
    cdf = 0.5 * (1.0 + lax.erf(rows * 0.7071067811865476))
    active = (rows * cdf).astype(BF)
    act[0] = active
    slope[0] = (cdf + (rows * 0.3989422804014327) * jnp.exp(-0.5 * rows * rows)).astype(BF)
    if last:
        kept[step] = active
    out = dot(active, down[step], 1, 0)

    @pl.when(step == 0)
    def _():
        part[...] = out + part_in[...] if last else out

    @pl.when(step > 0)
    def _():
        part[...] += out

    if last:

        @pl.when(step == 1)
        def _():
            block = 128
            small[...] = jnp.zeros_like(small)

            def body(i, carry):
                r = pl.ds(pl.multiple_of(i * block, block), block)
                normed = unit[r, :] * gain[...].astype(F32) + shift[...].astype(F32)
                unit2, scale2 = normalize(part[r, :] + b_down[...].astype(F32) + normed)
                layer_out[r, :] = (
                    unit2 * gain2[...].astype(F32) + shift2[...].astype(F32)
                ).astype(BF)
                cots = cot[r, :].astype(F32)
                grad = norm_back(cots * gain2[...].astype(F32), unit2, scale2)
                grad_second[r, :] = grad
                down_low[r, :] = grad.astype(BF)
                small[0:1, :] += jnp.sum(grad, axis=0, keepdims=True)
                small[1:2, :] += jnp.sum(cots * unit2, axis=0, keepdims=True)
                small[2:3, :] += jnp.sum(cots, axis=0, keepdims=True)
                return carry

            lax.fori_loop(0, low.shape[0] // block, body, 0)
            for i, ref in enumerate((ga, gb)):
                grads[i] = dot(kept[i], down_low[...], 0, 0).astype(BF)
                pltpu.make_async_copy(grads.at[i], ref, sem.at[4 + i]).start()
            for i, ref in enumerate((ga, gb)):
                pltpu.make_async_copy(grads.at[i], ref, sem.at[4 + i]).wait()


def feed(order, low, ups, downs, packs, extra=None):
    rows, width = low.shape
    hidden = ups[0].shape[1]
    last = extra is not None
    bias_at = packs[0].shape[0] // BIAS_ROWS - 1
    bias_spec = pl.BlockSpec((BIAS_ROWS, width), lambda s, *_: (bias_at, 0))
    row_spec = whole((rows, width))
    ops = [low, *ups, *downs, *packs]
    in_specs = [row_spec, ANY, ANY, ANY, ANY, bias_spec, bias_spec]
    out_specs = [pair((rows, hidden))] * 2
    out_shape = [jax.ShapeDtypeStruct((2, rows, hidden), BF)] * 2
    scratch = [pltpu.VMEM((2, width, hidden), BF), pltpu.VMEM((2, hidden, width), BF)]
    if last:
        ops += extra
        in_specs += [row_spec, row_spec] + [whole((1, width))] * 5 + [row_spec]
        out_specs += [row_spec] * 3 + [whole((8, width)), ANY, ANY]
        out_shape += [
            jax.ShapeDtypeStruct((rows, width), BF),
            jax.ShapeDtypeStruct((rows, width), BF),
            jax.ShapeDtypeStruct((rows, width), F32),
            jax.ShapeDtypeStruct((8, width), F32),
        ] + [jax.ShapeDtypeStruct((hidden, width), BF)] * 2
        scratch += [
            pltpu.VMEM((rows, width), F32),
            pltpu.VMEM((2, hidden, width), BF),
            pltpu.VMEM((2, rows, hidden), BF),
            pltpu.SemaphoreType.DMA((6,)),
        ]
    else:
        out_specs += [row_spec]
        out_shape += [jax.ShapeDtypeStruct((rows, width), F32)]
        scratch += [pltpu.SemaphoreType.DMA((4,))]
    return pl.pallas_call(
        functools.partial(feed_kernel, last),
        grid_spec=pltpu.PrefetchScalarGridSpec(
            num_scalar_prefetch=1,
            grid=(2,),
            in_specs=in_specs,
            out_specs=out_specs,
            scratch_shapes=scratch,
        ),
        out_shape=out_shape,
        compiler_params=params(),
        cost_estimate=cost(5e9 if last else 3e9, 8e6),
        name="feed_last" if last else "feed",
    )(order, *ops)


def down_grad_kernel(act, low, out_a, out_b, grads, sem):
    step = pl.program_id(0)
    grads[step] = dot(act[0], low[...], 0, 0).astype(BF)
    copies = [
        pltpu.make_async_copy(grads.at[i], ref, sem.at[i]) for i, ref in enumerate((out_a, out_b))
    ]

    @pl.when(step == 0)
    def _():
        copies[0].start()

    @pl.when(step == 1)
    def _():
        copies[1].start()
        copies[0].wait()
        copies[1].wait()


def down_grad(act, low):
    _, rows, hidden = act.shape
    width = low.shape[1]
    return pl.pallas_call(
        down_grad_kernel,
        grid=(2,),
        in_specs=[pair((rows, hidden)), whole((rows, width))],
        out_specs=[ANY, ANY],
        out_shape=[jax.ShapeDtypeStruct((hidden, width), BF)] * 2,
        scratch_shapes=[pltpu.VMEM((2, hidden, width), BF), pltpu.SemaphoreType.DMA((2,))],
        compiler_params=params(),
        cost_estimate=cost(1.2e9, 4e6),
        name="down_grad",
    )(act, low)


def feed_back_kernel(last, *refs):
    if last:
        (order, slope, down_low, normed_low, grad_in, ua, ub, da, db, unit, scale, gain,
         ga, gb, bias, grad_first, first_low, small, up, down, grads, part, sem) = refs
    else:
        (order, slope, down_low, normed_low, grad_in, ua, ub, da, db,
         ga, gb, bias, part, up, down, grads, sem) = refs
    step = pl.program_id(0)
    at = order[0]
    copies = []
    for i, (u, d) in enumerate(((ua, da), (ub, db))):
        copies.append(
            (
                Quarters(d, down.at[i], at, sem.at[2 * i + 1]),
                Quarters(u, up.at[i], at, sem.at[2 * i]),
            )
        )

    @pl.when(step == 0)
    def _():
        for group in copies:
            for copy in group:
                copy.start()
        for copy in copies[0]:
            copy.wait()

    @pl.when(step == 1)
    def _():
        for copy in copies[1]:
            copy.wait()

    grad_up = (dot(down_low[...], down[step], 1, 1) * slope[0].astype(F32)).astype(BF)
    bias[0] = jnp.broadcast_to(
        jnp.sum(grad_up.astype(F32), axis=0, keepdims=True), bias.shape[1:]
    )
    grads[step] = dot(normed_low[...], grad_up, 0, 0).astype(BF)
    outs = [pltpu.make_async_copy(grads.at[i], ref, sem.at[4 + i]) for i, ref in enumerate((ga, gb))]

    @pl.when(step == 0)
    def _():
        outs[0].start()

    @pl.when(step == 1)
    def _():
        outs[1].start()

    out = dot(grad_up, up[step], 1, 1)

    @pl.when(step == 0)
    def _():
        part[...] = out + grad_in[...]

    @pl.when(step > 0)
    def _():
        part[...] += out

    @pl.when(step == 1)
    def _():
        if last:
            block = 128
            small[...] = jnp.zeros_like(small)

            def body(i, carry):
                r = pl.ds(pl.multiple_of(i * block, block), block)
                grad = part[r, :]
                units = unit[r, :]
                first = norm_back(grad * gain[...].astype(F32), units, scale[r, :])
                grad_first[r, :] = first
                first_low[r, :] = first.astype(BF)
                small[0:1, :] += jnp.sum(first, axis=0, keepdims=True)
                small[1:2, :] += jnp.sum(grad * units, axis=0, keepdims=True)
                small[2:3, :] += jnp.sum(grad, axis=0, keepdims=True)
                return carry

            lax.fori_loop(0, part.shape[0] // block, body, 0)
        outs[0].wait()
        outs[1].wait()


def feed_back(order, slope, down_low, normed_low, grad_in, ups, downs, extra=None):
    rows, width = down_low.shape
    hidden = ups[0].shape[1]
    last = extra is not None
    row_spec = whole((rows, width))
    ops = [slope, down_low, normed_low, grad_in, *ups, *downs]
    in_specs = [pair((rows, hidden)), row_spec, row_spec, row_spec, ANY, ANY, ANY, ANY]
    out_specs = [ANY, ANY, pair((8, hidden))]
    out_shape = [jax.ShapeDtypeStruct((width, hidden), BF)] * 2 + [
        jax.ShapeDtypeStruct((2, 8, hidden), F32)
    ]
    scratch = [
        pltpu.VMEM((2, width, hidden), BF),
        pltpu.VMEM((2, hidden, width), BF),
        pltpu.VMEM((2, width, hidden), BF),
    ]
    if last:
        ops += extra
        in_specs += [row_spec, whole((rows, 1)), whole((1, width))]
        out_specs += [row_spec, row_spec, whole((8, width))]
        out_shape += [
            jax.ShapeDtypeStruct((rows, width), F32),
            jax.ShapeDtypeStruct((rows, width), BF),
            jax.ShapeDtypeStruct((8, width), F32),
        ]
        scratch += [pltpu.VMEM((rows, width), F32)]
    else:
        out_specs += [row_spec]
        out_shape += [jax.ShapeDtypeStruct((rows, width), F32)]
    scratch += [pltpu.SemaphoreType.DMA((6,))]
    return pl.pallas_call(
        functools.partial(feed_back_kernel, last),
        grid_spec=pltpu.PrefetchScalarGridSpec(
            num_scalar_prefetch=1,
            grid=(2,),
            in_specs=in_specs,
            out_specs=out_specs,
            scratch_shapes=scratch,
        ),
        out_shape=out_shape,
        compiler_params=params(),
        cost_estimate=cost(4e9, 8e6),
        name="feed_back_last" if last else "feed_back",
    )(order, *ops)


def attention_back_kernel(
    order, qkv, probs, att, first_low, tok, grad_in, pa, pb,
    ga, gb, bias, grad_out, pack, grads, work, part, sem,
):
    step = pl.program_id(0)
    local = att.shape[1]
    at = order[0]
    body = 4 * local
    copies = [
        Quarters(ref.at[pl.ds(0, body)], pack.at[i], at, sem.at[i])
        for i, ref in enumerate((pa, pb))
    ]

    @pl.when(step == 0)
    def _():
        copies[0].start()
        copies[1].start()
        copies[0].wait()

    @pl.when(step == 1)
    def _():
        copies[1].wait()

    weights = pack.at[step]
    firsts = first_low[...]
    grads[step, 3 * local : 4 * local, :] = dot(att[0], firsts, 1, 0).astype(BF)
    work[3 * local : 4 * local, :] = dot(weights[3 * local : 4 * local, :], firsts, 1, 1).astype(BF)
    for head in range(local // HEAD):
        here = head * HEAD
        spans = [pl.ds(i * local + here, HEAD) for i in range(4)]
        queries, keys, values = (qkv[0, span, :] for span in spans[:3])
        grad_att = work[spans[3], :]
        prob = probs[0, head]
        grad_prob = dot(values, grad_att, 0, 0)
        wide = prob.astype(F32)
        inner = jnp.sum(wide * grad_prob, axis=0, keepdims=True)
        grad_score = (wide * (grad_prob - inner)).astype(BF)
        work[spans[0], :] = (dot(keys, grad_score, 1, 0) * 0.125).astype(BF)
        work[spans[1], :] = dot(queries, grad_score, 1, 1).astype(BF)
        work[spans[2], :] = dot(grad_att, prob, 1, 1).astype(BF)
    joined = work[0 : 3 * local, :]
    grads[step, 0 : 3 * local, :] = dot(joined, tok[...], 1, 0).astype(BF)
    outs = [pltpu.make_async_copy(grads.at[i], ref, sem.at[2 + i]) for i, ref in enumerate((ga, gb))]

    @pl.when(step == 0)
    def _():
        outs[0].start()

    @pl.when(step == 1)
    def _():
        outs[1].start()

    bias[0] = dot(jnp.ones((8, joined.shape[1]), BF), joined, 1, 1)
    out = dot(joined, weights[0 : 3 * local, :], 0, 0)

    @pl.when(step == 0)
    def _():
        part[...] = grad_in[...] + out

    @pl.when(step == 1)
    def _():
        grad_out[...] = (part[...] + out).astype(grad_out.dtype)
        outs[0].wait()
        outs[1].wait()


def attention_back(order, saved, first_low, tokens, grad_in, packs, out_dtype):
    qkv, probs, att = saved
    rows, width = tokens.shape
    local = att.shape[1]
    row_spec = whole((rows, width))
    return pl.pallas_call(
        attention_back_kernel,
        grid_spec=pltpu.PrefetchScalarGridSpec(
            num_scalar_prefetch=1,
            grid=(2,),
            in_specs=[
                pair(qkv.shape[1:]), pair(probs.shape[1:]), pair(att.shape[1:]),
                row_spec, row_spec, row_spec, ANY, ANY,
            ],
            out_specs=[ANY, ANY, pair((8, 3 * local)), row_spec],
            scratch_shapes=[
                pltpu.VMEM((2, 4 * local, width), BF),
                pltpu.VMEM((2, 4 * local, width), BF),
                pltpu.VMEM((4 * local, rows), BF),
                pltpu.VMEM((rows, width), F32),
                pltpu.SemaphoreType.DMA((4,)),
            ],
        ),
        out_shape=[jax.ShapeDtypeStruct((4 * local, width), BF)] * 2
        + [
            jax.ShapeDtypeStruct((2, 8, 3 * local), F32),
            jax.ShapeDtypeStruct((rows, width), out_dtype),
        ],
        compiler_params=params(),
        cost_estimate=cost(7e9, 1.2e7),
        name="attention_back",
    )(order, qkv, probs, att, first_low, tokens, grad_in, *packs)


def finish_kernel(bit, mine, theirs, gq, gk, gv, go):
    local = gq.shape[1]
    low = jnp.where(bit[0] == 0, mine[...], theirs[...]).astype(F32)
    high = jnp.where(bit[0] == 0, theirs[...], mine[...]).astype(F32)
    gq[...] = jnp.transpose(low[0:local, :])
    gk[...] = jnp.transpose(low[local : 2 * local, :])
    gv[...] = jnp.transpose(high[0:local, :])
    go[...] = high[local : 2 * local, :]


def finish_attention(bit, mine, theirs):
    half, width = mine.shape
    local = half // 2
    return pl.pallas_call(
        finish_kernel,
        grid_spec=pltpu.PrefetchScalarGridSpec(
            num_scalar_prefetch=1,
            grid=(1,),
            in_specs=[whole((half, width))] * 2,
            out_specs=[whole((width, local))] * 3 + [whole((local, width))],
        ),
        out_shape=[jax.ShapeDtypeStruct((width, local), F32)] * 3
        + [jax.ShapeDtypeStruct((local, width), F32)],
        compiler_params=params(),
        name="finish_attention",
    )(bit, mine, theirs)


def swap(value, axis, bit):
    size = lax.axis_size(axis)
    return lax.ppermute(value, axis, [(i, i ^ bit) for i in range(size)])


def cross(value):
    return swap(value, "tensor", 2)


def partner(value):
    return swap(value, "tensor", 1)


def fetch_across(own, order, tail=0):
    rows = (own.shape[0] - tail) // 4
    send = lax.dynamic_slice_in_dim(own, order * rows, rows, 0)
    if tail:
        send = jnp.concatenate([send, own[4 * rows :]], axis=0)
    first = cross(send)
    by_x = swap(first, "dp", 1)
    by_z = swap(first, "dp", 2)
    mid = rows // 2
    last_x = swap(by_z[:mid], "dp", 1)
    last_z = swap(by_x[mid:rows], "dp", 2)
    pieces = [first[:rows], by_x[:rows], by_z[:rows], last_x, last_z]
    if tail:
        pieces.append(first[rows:])
    return jnp.concatenate(pieces, axis=0)


def half(value, which):
    rows = value.shape[0] // 2
    return lax.dynamic_slice_in_dim(value, which * rows, rows, 0)


def add(left, right):
    return left.astype(F32) + right.astype(F32)


def dp_bits():
    bits, bit = [], 1
    while bit < lax.axis_size("dp"):
        bits.append(bit)
        bit *= 2
    return bits


def scatter_dp(keep):
    index = lax.axis_index("dp")
    for bit in dp_bits():
        mine = (index // bit) % 2
        got = swap(half(keep, 1 - mine).astype(BF), "dp", bit)
        keep = add(half(keep, mine), got)
    return keep.astype(BF)


def gather_dp(full, bits):
    index = lax.axis_index("dp")
    for bit in reversed(bits):
        mine = (index // bit) % 2
        got = swap(full, "dp", bit)
        low = jnp.where(mine == 0, full, got)
        high = jnp.where(mine == 0, got, full)
        full = jnp.concatenate([low, high], axis=0)
    return full


def sum_groups(first, second, third, fourth):
    send = add(second, partner(first)).astype(BF)
    keep = add(fourth, partner(third))
    return add(keep, cross(send))


def on_device(
    tokens,
    w_query,
    w_key,
    w_value,
    b_query,
    b_value,
    w_output,
    b_output,
    first_gain,
    first_shift,
    w_up,
    b_up,
    w_down,
    b_down,
    second_gain,
    second_shift,
    cotangent,
):
    rows, width = tokens.shape
    local = w_query.shape[1]
    assert rows == SEQ_LEN and width == 4 * local and w_up.shape == (width, width)
    index = lax.axis_index("dp")
    quarter = index % 4
    natural = jnp.zeros((1,), jnp.int32)
    order = quarter.astype(jnp.int32).reshape(1)

    pack = pack_attention(w_query, w_key, w_value, w_output, b_query, b_value, b_up)
    attn_own = [partner(pack), pack]
    attn_far = fetch_across(pack, quarter, BIAS_ROWS)
    up_own, down_own = [partner(w_up), w_up], [partner(w_down), w_down]
    attn_other = [partner(attn_far), attn_far]
    up_far = fetch_across(w_up, quarter)
    up_other = [partner(up_far), up_far]
    down_far = fetch_across(w_down, quarter)
    down_other = [partner(down_far), down_far]

    *saved_own, part = attention(natural, tokens, attn_own)
    *saved_other, normed_low, unit, scale = attention(
        order, tokens, attn_other, [part, b_output[None], first_gain[None], first_shift[None]]
    )
    act_own, slope_own, part = feed(natural, normed_low, up_own, down_own, attn_own)
    (_, slope_other, layer_out, down_low, grad_second, small_second, down_a, down_b) = feed(
        order, normed_low, up_other, down_other, attn_other,
        [part, unit, first_gain[None], first_shift[None], b_down[None], second_gain[None],
         second_shift[None], cotangent],
    )

    down_c, down_d = down_grad(act_own, down_low)
    down_total = sum_groups(down_a, down_b, down_c, down_d)
    up_a, up_b, bias_up_other, part = feed_back(
        order, slope_other, down_low, normed_low, grad_second, up_other, down_other
    )
    up_c, up_d, bias_up_own, grad_first, first_low, small_first = feed_back(
        natural, slope_own, down_low, normed_low, part, up_own, down_own,
        [unit, scale, first_gain[None]],
    )
    up_total = sum_groups(up_a, up_b, up_c, up_d)
    attn_a, attn_b, bias_other, part = attention_back(
        order, saved_other, first_low, tokens, grad_first, attn_other, F32
    )
    attn_c, attn_d, bias_own, grad_tokens = attention_back(
        natural, saved_own, first_low, tokens, part, attn_own, BF
    )
    attn_total = sum_groups(attn_a, attn_b, attn_c, attn_d)

    bits = dp_bits()
    grad_w_down = gather_dp(scatter_dp(down_total), bits).astype(F32)
    grad_w_up = gather_dp(scatter_dp(up_total), bits).astype(F32)
    mine = gather_dp(scatter_dp(attn_total), bits[1:])
    grad_q, grad_k, grad_v, grad_o = finish_attention(
        (index % 2).astype(jnp.int32).reshape(1), mine, swap(mine, "dp", 1)
    )

    def of_shard(bias, bias_up, i):
        return jnp.concatenate([bias[i, 0], bias_up[i, 0]])

    common = jnp.concatenate([small_second[:3].reshape(-1), small_first[:3].reshape(-1)])
    send = jnp.concatenate(
        [of_shard(bias_other, bias_up_other, 0), of_shard(bias_own, bias_up_own, 0), common]
    )
    keep = jnp.concatenate(
        [of_shard(bias_other, bias_up_other, 1), of_shard(bias_own, bias_up_own, 1), common]
    )
    size = 3 * local + width
    keep = keep + partner(send)
    keep = keep[size:] + cross(jnp.concatenate([keep[:size], keep[2 * size :]]))
    for bit in bits:
        keep = keep + swap(keep, "dp", bit)
    vectors = keep[size:].reshape(6, width)

    return (
        layer_out,
        grad_tokens,
        grad_q,
        grad_k,
        grad_v,
        keep[:local],
        keep[2 * local : 3 * local],
        grad_o,
        vectors[3],
        vectors[4],
        vectors[5],
        grad_w_up,
        keep[3 * local : size],
        grad_w_down,
        vectors[0],
        vectors[1],
        vectors[2],
    )


def solution(mesh):
    rows = P(("dp", "tensor"), None)
    col, row, vec, rep = P(None, "tensor"), P("tensor", None), P("tensor"), P()
    return jax.shard_map(
        on_device,
        mesh=mesh,
        in_specs=(
            rows, col, col, col, vec, vec, row, rep, rep, rep, col, vec, row, rep, rep, rep, rows,
        ),
        out_specs=(
            rows, rows, col, col, col, vec, vec, row, rep, rep, rep, col, vec, row, rep, rep, rep,
        ),
        check_vma=False,
    )
```

```python
import functools

import jax
import jax.numpy as jnp
from jax import lax
from jax.experimental import pallas as pl
from jax.experimental.pallas import tpu as pltpu
from jax.sharding import PartitionSpec as P

HEAD = 64
SEQ_LEN = 512
BIAS_ROWS = 16
BF = jnp.bfloat16
F32 = jnp.float32
ANY = pl.BlockSpec(memory_space=pl.ANY)
VMEM_BYTES = 26 << 20
BY_B, BY_A, NATURAL, FIRST, SECOND, THIRD, FOURTH, PLACES, SIDE = 0, 4, 8, 12, 16, 18, 22, 24, 28
ALL_VMEM_BYTES = 60 << 20


def dot(left, right, left_dim, right_dim):
    return lax.dot_general(
        left, right, (((left_dim,), (right_dim,)), ((), ())), preferred_element_type=F32
    )


def whole(shape):
    return pl.BlockSpec(shape, lambda *_: (0,) * len(shape))


def pair(shape):
    return pl.BlockSpec((1, *shape), lambda s, *_: (s, *(0,) * len(shape)))


def params(limit=VMEM_BYTES):
    return pltpu.CompilerParams(vmem_limit_bytes=limit)


def cost(flops, moved):
    return pl.CostEstimate(flops=int(flops), bytes_accessed=int(moved), transcendentals=0)


class Quarters:
    def __init__(self, source, target, plan, base, sem):
        rows = target.shape[0] // 4
        self.copies = [
            pltpu.make_async_copy(
                source.at[pl.ds(i * rows, rows)],
                target.at[pl.ds(pl.multiple_of(plan[base + i] * rows, rows), rows)],
                sem,
            )
            for i in range(4)
        ]

    def start(self):
        for copy in self.copies:
            copy.start()

    def wait(self):
        for copy in self.copies:
            copy.wait()


def pack_kernel(plan, wq, wk, wv, wo, wu, wd, *refs):
    vectors, refs = refs[:9], refs[9:]
    out, near, far_up, far_down, table, packed, piece, lines, *lists, sem = refs
    local, width = wq.shape
    at = pl.multiple_of(plan[BY_B] * local, local)
    copies = [
        pltpu.make_async_copy(ref, packed.at[pl.ds(i * local, local)], sem.at[0])
        for i, ref in enumerate((wq, wk, wv, wo))
    ]
    copies += [
        pltpu.make_async_copy(ref, line, sem.at[0]) for ref, line in zip(vectors, lists)
    ]
    pieces = [
        pltpu.make_async_copy(ref.at[pl.ds(at, local)], piece.at[i], sem.at[1])
        for i, ref in enumerate((wu, wd))
    ]
    for copy in copies:
        copy.start()
    for copy in pieces:
        copy.start()
    packed[4 * local :, :] = jnp.zeros((BIAS_ROWS, width), BF)
    lines[...] = jnp.zeros_like(lines)
    for copy in copies:
        copy.wait()
    bq, bv, bu = lists[:3]
    packed[4 * local : 4 * local + 1, 0:local] = bq[...].reshape(1, local)
    packed[4 * local : 4 * local + 1, local : 2 * local] = bv[...].reshape(1, local)
    packed[4 * local + 1 : 4 * local + 2, :] = bu[...].reshape(1, width)
    outs = [
        pltpu.make_async_copy(
            packed.at[pl.ds(at, local)], near.at[pl.ds(0, local)], sem.at[2]
        ),
        pltpu.make_async_copy(
            packed.at[pl.ds(4 * local, BIAS_ROWS)], near.at[pl.ds(local, BIAS_ROWS)], sem.at[2]
        ),
        pltpu.make_async_copy(packed, out, sem.at[2]),
    ]
    for copy in outs:
        copy.start()
    for i, ref in enumerate(lists[3:]):
        lines[i : i + 1, :] = ref[...].astype(F32).reshape(1, width)
    outs.append(pltpu.make_async_copy(lines, table, sem.at[2]))
    outs[-1].start()
    for copy in pieces:
        copy.wait()
    for i, ref in enumerate((far_up, far_down)):
        outs.append(pltpu.make_async_copy(piece.at[i], ref, sem.at[2]))
        outs[-1].start()
    for copy in outs:
        copy.wait()


def pack_weights(plan, w_query, w_key, w_value, w_output, w_up, w_down, vectors):
    local, width = w_output.shape
    shapes = [
        jax.ShapeDtypeStruct((4 * local + BIAS_ROWS, width), BF),
        jax.ShapeDtypeStruct((local + BIAS_ROWS, width), BF),
        jax.ShapeDtypeStruct((local, width), BF),
        jax.ShapeDtypeStruct((local, width), BF),
        jax.ShapeDtypeStruct((8, width), F32),
    ]
    return pl.pallas_call(
        pack_kernel,
        grid_spec=pltpu.PrefetchScalarGridSpec(
            num_scalar_prefetch=1,
            grid=(1,),
            in_specs=[ANY] * 15,
            out_specs=[ANY] * 5,
            scratch_shapes=[
                pltpu.VMEM(shapes[0].shape, BF),
                pltpu.VMEM((2, *shapes[2].shape), BF),
                pltpu.VMEM(shapes[4].shape, F32),
                *[pltpu.VMEM(v.shape, BF) for v in vectors],
                pltpu.SemaphoreType.DMA((3,)),
            ],
        ),
        out_shape=shapes,
        compiler_params=params(ALL_VMEM_BYTES),
        name="pack_weights",
    )(plan, w_query.T, w_key.T, w_value.T, w_output, w_up, w_down, *vectors)


def normalize(rows):
    center = rows - jnp.mean(rows, axis=-1, keepdims=True)
    scale = lax.rsqrt(jnp.mean(center * center, axis=-1, keepdims=True) + 1e-12)
    return center * scale, scale


def norm_back(grad, unit, scale):
    return scale * (
        grad
        - jnp.mean(grad, axis=-1, keepdims=True)
        - unit * jnp.mean(grad * unit, axis=-1, keepdims=True)
    )


def start_and_wait(step, copies):
    @pl.when(step == 0)
    def _():
        for group in copies:
            for copy in group:
                copy.start()

    for i, group in enumerate(copies):

        @pl.when(step == i)
        def _(group=group):
            for copy in group:
                copy.wait()


def attention_kernel(base, first, last, *refs):
    count = 1
    plan, tok, *refs = refs
    packs, refs = refs[:count], refs[count:]
    if not first:
        part_in, *refs = refs
    if last:
        table, qkv, probs, att, normed_low, unit, scale, pack, part, sem = refs
    else:
        qkv, probs, att, part, pack, sem = refs
    step = pl.program_id(0)
    local = att.shape[1]
    body = 4 * local
    start_and_wait(
        step,
        [
            (
                Quarters(ref.at[pl.ds(0, body)], pack.at[i, pl.ds(0, body)], plan, base, sem.at[i]),
                pltpu.make_async_copy(
                    ref.at[pl.ds(body, BIAS_ROWS)], pack.at[i, pl.ds(body, BIAS_ROWS)], sem.at[i]
                ),
            )
            for i, ref in enumerate(packs)
        ],
    )
    weights = pack.at[step]
    bias = jnp.transpose(weights[body : body + BIAS_ROWS, :].astype(F32))
    tokens = tok[...]
    qkv[0, 0:local, :] = (
        dot(weights[0:local, :], tokens, 1, 1) + bias[0:local, 0:1]
    ).astype(BF) * BF(0.125)
    qkv[0, local : 2 * local, :] = dot(weights[local : 2 * local, :], tokens, 1, 1).astype(BF)
    qkv[0, 2 * local : 3 * local, :] = (
        dot(weights[2 * local : 3 * local, :], tokens, 1, 1) + bias[local : 2 * local, 0:1]
    ).astype(BF)
    for head in range(local // HEAD):
        here = head * HEAD
        queries = qkv[0, here : here + HEAD, :]
        keys = qkv[0, local + here : local + here + HEAD, :]
        values = qkv[0, 2 * local + here : 2 * local + here + HEAD, :]
        scores = dot(keys, queries, 0, 0)
        unnorm = jnp.exp(scores - jnp.max(scores, axis=0, keepdims=True))
        prob = (unnorm * (1.0 / jnp.sum(unnorm, axis=0, keepdims=True))).astype(BF)
        probs[0, head] = prob
        att[0, here : here + HEAD, :] = dot(values, prob, 1, 0).astype(BF)
    out = dot(att[0], weights[3 * local : 4 * local, :], 0, 0)

    @pl.when(step == 0)
    def _():
        part[...] = out if first else out + part_in[...]

    @pl.when(step > 0)
    def _():
        part[...] += out

    if last:

        @pl.when(step == count - 1)
        def _():
            block = 128

            def rows(i, carry):
                r = pl.ds(pl.multiple_of(i * block, block), block)
                total = part[r, :] + table[0:1, :] + tok[r, :].astype(F32)
                unit_rows, scale_rows = normalize(total)
                unit[r, :] = unit_rows
                scale[r, :] = scale_rows
                normed_low[r, :] = (unit_rows * table[1:2, :] + table[2:3, :]).astype(BF)
                return carry

            lax.fori_loop(0, tok.shape[0] // block, rows, 0)


def attention(plan, base, tokens, packs, part=None, table=None):
    rows, width = tokens.shape
    count = len(packs)
    local = (packs[0].shape[0] - BIAS_ROWS) // 4
    heads = local // HEAD
    first, last = part is None, table is not None
    row_spec = whole((rows, width))
    ops = [tokens, *packs]
    in_specs = [row_spec] + [ANY] * count
    if not first:
        ops.append(part)
        in_specs.append(row_spec)
    out_specs = [pair((3 * local, rows)), pair((heads, rows, rows)), pair((local, rows))]
    out_shape = [
        jax.ShapeDtypeStruct((count, 3 * local, rows), BF),
        jax.ShapeDtypeStruct((count, heads, rows, rows), BF),
        jax.ShapeDtypeStruct((count, local, rows), BF),
    ]
    scratch = [pltpu.VMEM((count, *packs[0].shape), BF)]
    if last:
        ops.append(table)
        in_specs.append(whole((8, width)))
        out_specs += [row_spec, row_spec, whole((rows, 1))]
        out_shape += [
            jax.ShapeDtypeStruct((rows, width), BF),
            jax.ShapeDtypeStruct((rows, width), F32),
            jax.ShapeDtypeStruct((rows, 1), F32),
        ]
        scratch += [pltpu.VMEM((rows, width), F32)]
    else:
        out_specs += [row_spec]
        out_shape += [jax.ShapeDtypeStruct((rows, width), F32)]
    scratch += [pltpu.SemaphoreType.DMA((count,))]
    return pl.pallas_call(
        functools.partial(attention_kernel, base, first, last),
        grid_spec=pltpu.PrefetchScalarGridSpec(
            num_scalar_prefetch=1,
            grid=(count,),
            in_specs=in_specs,
            out_specs=out_specs,
            scratch_shapes=scratch,
        ),
        out_shape=out_shape,
        compiler_params=params(),
        cost_estimate=cost(2.5e9 * count, 4e6 * count),
        name="attention_last" if last else "attention",
    )(plan, *ops)


def feed_kernel(base, first, last, *refs):
    count = 1
    plan, low, *refs = refs
    weights, refs = refs[: 2 * count], refs[2 * count :]
    biases, refs = refs[:count], refs[count:]
    if not first:
        part_in, *refs = refs
    if last:
        unit, table, cot, act, slope, layer_out, down_low, grad_second, small, *refs = refs
        up, down, part, sem = refs
    else:
        act, slope, part, up, down, sem = refs
    step = pl.program_id(0)
    start_and_wait(
        step,
        [
            (
                Quarters(weights[i], up.at[i], plan, base, sem.at[i]),
                Quarters(weights[count + i], down.at[i], plan, base, sem.at[i]),
            )
            for i in range(count)
        ],
    )
    hidden = up.shape[2]
    bias = biases[0][1:2, 0:hidden].astype(F32)
    if count > 1:
        bias = jnp.where(step == 0, bias, biases[1][1:2, 0:hidden].astype(F32))
    rows = dot(low[...], up[step], 1, 0) + bias
    cdf = 0.5 * (1.0 + lax.erf(rows * 0.7071067811865476))
    active = (rows * cdf).astype(BF)
    act[0] = active
    slope[0] = (cdf + (rows * 0.3989422804014327) * jnp.exp(-0.5 * rows * rows)).astype(BF)
    out = dot(active, down[step], 1, 0)

    @pl.when(step == 0)
    def _():
        part[...] = out if first else out + part_in[...]

    @pl.when(step > 0)
    def _():
        part[...] += out

    if last:

        @pl.when(step == count - 1)
        def _():
            block = 128
            small[...] = jnp.zeros_like(small)

            def body(i, carry):
                r = pl.ds(pl.multiple_of(i * block, block), block)
                normed = unit[r, :] * table[1:2, :] + table[2:3, :]
                unit2, scale2 = normalize(part[r, :] + table[3:4, :] + normed)
                layer_out[r, :] = (unit2 * table[4:5, :] + table[5:6, :]).astype(BF)
                cots = cot[r, :].astype(F32)
                grad = norm_back(cots * table[4:5, :], unit2, scale2)
                grad_second[r, :] = grad
                down_low[r, :] = grad.astype(BF)
                small[0:1, :] += jnp.sum(grad, axis=0, keepdims=True)
                small[1:2, :] += jnp.sum(cots * unit2, axis=0, keepdims=True)
                small[2:3, :] += jnp.sum(cots, axis=0, keepdims=True)
                return carry

            lax.fori_loop(0, low.shape[0] // block, body, 0)


def feed(plan, base, low, ups, downs, packs, part=None, extra=None):
    rows, width = low.shape
    count = len(ups)
    hidden = ups[0].shape[1]
    first, last = part is None, extra is not None
    bias_at = packs[0].shape[0] // BIAS_ROWS - 1
    bias_spec = pl.BlockSpec((BIAS_ROWS, width), lambda s, *_: (bias_at, 0))
    row_spec = whole((rows, width))
    ops = [low, *ups, *downs, *packs]
    in_specs = [row_spec] + [ANY] * (2 * count) + [bias_spec] * count
    if not first:
        ops.append(part)
        in_specs.append(row_spec)
    out_specs = [pair((rows, hidden))] * 2
    out_shape = [jax.ShapeDtypeStruct((count, rows, hidden), BF)] * 2
    scratch = [pltpu.VMEM((count, width, hidden), BF), pltpu.VMEM((count, hidden, width), BF)]
    if last:
        ops += extra
        in_specs += [row_spec, whole((8, width)), row_spec]
        out_specs += [row_spec] * 3 + [whole((8, width))]
        out_shape += [
            jax.ShapeDtypeStruct((rows, width), BF),
            jax.ShapeDtypeStruct((rows, width), BF),
            jax.ShapeDtypeStruct((rows, width), F32),
            jax.ShapeDtypeStruct((8, width), F32),
        ]
        scratch += [pltpu.VMEM((rows, width), F32)]
    else:
        out_specs += [row_spec]
        out_shape += [jax.ShapeDtypeStruct((rows, width), F32)]
    scratch += [pltpu.SemaphoreType.DMA((count,))]
    return pl.pallas_call(
        functools.partial(feed_kernel, base, first, last),
        grid_spec=pltpu.PrefetchScalarGridSpec(
            num_scalar_prefetch=1,
            grid=(count,),
            in_specs=in_specs,
            out_specs=out_specs,
            scratch_shapes=scratch,
        ),
        out_shape=out_shape,
        compiler_params=params(),
        cost_estimate=cost(1.5e9 * count + 1e9 * last, 4e6 * count),
        name="feed_last" if last else "feed",
    )(plan, *ops)


def down_grad_kernel(count, *refs):
    acts, low = refs[:count], refs[count]
    targets, (grads, sem) = refs[count + 1 : -2], refs[-2:]
    copies = []
    for i in range(count):
        grads[i] = dot(acts[i][0], low[...], 0, 0).astype(BF)
        copies.append(pltpu.make_async_copy(grads.at[i], targets[i], sem))
        copies[-1].start()
    for copy in copies:
        copy.wait()


def down_grad(acts, low):
    count = len(acts)
    _, rows, hidden = acts[0].shape
    width = low.shape[1]
    return pl.pallas_call(
        functools.partial(down_grad_kernel, count),
        grid=(1,),
        in_specs=[whole((1, rows, hidden))] * count + [whole((rows, width))],
        out_specs=[ANY] * count,
        out_shape=[jax.ShapeDtypeStruct((hidden, width), BF)] * count,
        scratch_shapes=[pltpu.VMEM((count, hidden, width), BF), pltpu.SemaphoreType.DMA(())],
        compiler_params=params(),
        cost_estimate=cost(6e8 * count, 2e6 * count),
        name="down_grad",
    )(*acts, low)


def feed_back_kernel(base, last, *refs):
    if last:
        (plan, slope, down_low, normed_low, grad_in, u, d, unit, scale, table,
         target, bias, grad_first, first_low, small, up, down, grads, part, sem) = refs
    else:
        (plan, slope, down_low, normed_low, grad_in, u, d,
         target, bias, part, up, down, grads, sem) = refs
    copies = [Quarters(d, down, plan, base, sem.at[0]), Quarters(u, up, plan, base, sem.at[1])]
    for copy in copies:
        copy.start()
    copies[0].wait()
    grad_up = (dot(down_low[...], down[...], 1, 1) * slope[0].astype(F32)).astype(BF)
    bias[...] = jnp.broadcast_to(jnp.sum(grad_up.astype(F32), axis=0, keepdims=True), bias.shape)
    grads[...] = dot(normed_low[...], grad_up, 0, 0).astype(BF)
    out = pltpu.make_async_copy(grads, target, sem.at[2])
    out.start()
    copies[1].wait()
    part[...] = grad_in[...] + dot(grad_up, up[...], 1, 1)
    if last:
        block = 128
        small[...] = jnp.zeros_like(small)

        def body(i, carry):
            r = pl.ds(pl.multiple_of(i * block, block), block)
            grad = part[r, :]
            units = unit[r, :]
            first = norm_back(grad * table[1:2, :], units, scale[r, :])
            grad_first[r, :] = first
            first_low[r, :] = first.astype(BF)
            small[0:1, :] += jnp.sum(first, axis=0, keepdims=True)
            small[1:2, :] += jnp.sum(grad * units, axis=0, keepdims=True)
            small[2:3, :] += jnp.sum(grad, axis=0, keepdims=True)
            return carry

        lax.fori_loop(0, part.shape[0] // block, body, 0)
    out.wait()


def feed_back(plan, base, slope, down_low, normed_low, grad_in, up, down, extra=None):
    rows, width = down_low.shape
    hidden = up.shape[1]
    last = extra is not None
    row_spec = whole((rows, width))
    ops = [slope, down_low, normed_low, grad_in, up, down]
    in_specs = [whole((1, rows, hidden)), row_spec, row_spec, row_spec, ANY, ANY]
    out_specs = [ANY, whole((8, hidden))]
    out_shape = [
        jax.ShapeDtypeStruct((width, hidden), BF),
        jax.ShapeDtypeStruct((8, hidden), F32),
    ]
    scratch = [
        pltpu.VMEM((width, hidden), BF),
        pltpu.VMEM((hidden, width), BF),
        pltpu.VMEM((width, hidden), BF),
    ]
    if last:
        ops += extra
        in_specs += [row_spec, whole((rows, 1)), whole((8, width))]
        out_specs += [row_spec, row_spec, whole((8, width))]
        out_shape += [
            jax.ShapeDtypeStruct((rows, width), F32),
            jax.ShapeDtypeStruct((rows, width), BF),
            jax.ShapeDtypeStruct((8, width), F32),
        ]
        scratch += [pltpu.VMEM((rows, width), F32)]
    else:
        out_specs += [row_spec]
        out_shape += [jax.ShapeDtypeStruct((rows, width), F32)]
    scratch += [pltpu.SemaphoreType.DMA((3,))]
    return pl.pallas_call(
        functools.partial(feed_back_kernel, base, last),
        grid_spec=pltpu.PrefetchScalarGridSpec(
            num_scalar_prefetch=1,
            grid=(1,),
            in_specs=in_specs,
            out_specs=out_specs,
            scratch_shapes=scratch,
        ),
        out_shape=out_shape,
        compiler_params=params(),
        cost_estimate=cost(2.5e9 if last else 2e9, 5e6),
        name="feed_back_last" if last else "feed_back",
    )(plan, *ops)


def attention_back_kernel(base, *refs):
    count = 1
    plan, qkv, probs, first_low, tok, grad_in, *refs = refs
    packs, refs = refs[:count], refs[count:]
    targets, refs = refs[:count], refs[count:]
    bias, grad_out, pack, grads, work, part, sem = refs
    step = pl.program_id(0)
    local = pack.shape[1] // 4
    body = 4 * local
    start_and_wait(
        step,
        [
            (Quarters(ref.at[pl.ds(0, body)], pack.at[i], plan, base, sem.at[i]),)
            for i, ref in enumerate(packs)
        ],
    )
    weights = pack.at[step]
    firsts = first_low[...]
    work[3 * local : 4 * local, :] = dot(weights[3 * local : 4 * local, :], firsts, 1, 1).astype(BF)
    for head in range(local // HEAD):
        here = head * HEAD
        spans = [pl.ds(i * local + here, HEAD) for i in range(4)]
        queries, keys, values = (qkv[0, span, :] for span in spans[:3])
        grad_att = work[spans[3], :]
        prob = probs[0, head]
        grad_prob = dot(values, grad_att, 0, 0)
        wide = prob.astype(F32)
        inner = jnp.sum(wide * grad_prob, axis=0, keepdims=True)
        grad_score = (wide * (grad_prob - inner)).astype(BF)
        work[spans[0], :] = (dot(keys, grad_score, 1, 0) * 0.125).astype(BF)
        work[spans[1], :] = dot(queries, grad_score, 1, 1).astype(BF)
        work[spans[2], :] = dot(grad_att, prob, 1, 1).astype(BF)
    joined = work[0 : 3 * local, :]
    grads[step, 0 : 3 * local, :] = dot(joined, tok[...], 1, 0).astype(BF)
    outs = [
        [pltpu.make_async_copy(grads.at[i], targets[i], sem.at[count + i])]
        for i in range(count)
    ]
    for i in range(count):

        @pl.when(step == i)
        def _(i=i):
            for copy in outs[i]:
                copy.start()

    bias[0] = dot(jnp.ones((8, joined.shape[1]), BF), joined, 1, 1)
    out = dot(joined, weights[0 : 3 * local, :], 0, 0)
    before = part if count > 1 else grad_in
    if count > 1:

        @pl.when(step == 0)
        def _():
            part[...] = grad_in[...] + out

    @pl.when(step == count - 1)
    def _():
        grad_out[...] = (before[...] + out).astype(grad_out.dtype)
        for group in outs:
            for copy in group:
                copy.wait()


def attention_back(plan, base, saved, first_low, tokens, grad_in, packs, out_dtype):
    qkv, probs, _ = saved
    count = len(packs)
    rows, width = tokens.shape
    local = qkv.shape[1] // 3
    row_spec = whole((rows, width))
    return pl.pallas_call(
        functools.partial(attention_back_kernel, base),
        grid_spec=pltpu.PrefetchScalarGridSpec(
            num_scalar_prefetch=1,
            grid=(count,),
            in_specs=[
                pair(qkv.shape[1:]), pair(probs.shape[1:]),
                row_spec, row_spec, row_spec, *[ANY] * count,
            ],
            out_specs=[ANY] * count + [pair((8, 3 * local)), row_spec],
            scratch_shapes=[
                pltpu.VMEM((count, 4 * local, width), BF),
                pltpu.VMEM((count, 3 * local, width), BF),
                pltpu.VMEM((4 * local, rows), BF),
                pltpu.VMEM((rows, width) if count > 1 else (8, width), F32),
                pltpu.SemaphoreType.DMA((2 * count,)),
            ],
        ),
        out_shape=[jax.ShapeDtypeStruct((3 * local, width), BF)] * count
        + [
            jax.ShapeDtypeStruct((count, 8, 3 * local), F32),
            jax.ShapeDtypeStruct((rows, width), out_dtype),
        ],
        compiler_params=params(),
        cost_estimate=cost(3.5e9 * count, 6e6 * count),
        name="attention_back",
    )(plan, qkv, probs, first_low, tokens, grad_in, *packs)


def out_grad_kernel(a, b, c, d, low, send, keep):
    for ref, pair_of in ((send, (a, c)), (keep, (b, d))):
        for i, att in enumerate(pair_of):
            ref[i] = dot(att[0], low[...], 1, 0).astype(BF)


def out_grad(atts, low):
    _, local, rows = atts[0].shape
    width = low.shape[1]
    return pl.pallas_call(
        out_grad_kernel,
        grid=(1,),
        in_specs=[whole((1, local, rows))] * 4 + [whole((rows, width))],
        out_specs=[whole((2, local, width))] * 2,
        out_shape=[jax.ShapeDtypeStruct((2, local, width), BF)] * 2,
        compiler_params=params(),
        cost_estimate=cost(6e8, 3e6),
        name="out_grad",
    )(*atts, low)


def choose(total, plan, base, count, sent, keep):
    rows = sent.shape[0] // count
    for i in range(count):
        for ref, at in ((sent, base + i), (keep, base + count + i)):
            block = total[pl.ds(pl.multiple_of(plan[at] * rows, rows), rows), :]
            ref[i * rows : (i + 1) * rows, :] = block.astype(ref.dtype)


def first_kernel(stacked, plan, *refs):
    *parts, sent, keep, total = refs
    rows = sent.shape[0]
    at = 0
    for other, core_other, own, core_own in zip(*[iter(parts)] * 4):
        size = other.shape[0]
        total[at : at + size, :] = other[...].astype(F32) + core_other[...].astype(F32)
        total[rows + at : rows + at + size, :] = own[...].astype(F32) + core_own[...].astype(F32)
        at += size
    if stacked:
        mine, theirs = parts[-2:]
        size = mine.shape[1]
        total[at : at + size, :] = mine[0].astype(F32) + theirs[0].astype(F32)
        total[rows + at : rows + at + size, :] = mine[1].astype(F32) + theirs[1].astype(F32)
    choose(total, plan, FIRST, 2, sent, keep)


def first_stage(plan, parts, stacked):
    width = parts[0].shape[-1]
    rows = parts[0].shape[0] + (stacked[0].shape[1] if stacked else 0)
    ops = [*parts, *stacked]
    return pl.pallas_call(
        functools.partial(first_kernel, bool(stacked)),
        grid_spec=pltpu.PrefetchScalarGridSpec(
            num_scalar_prefetch=1,
            grid=(1,),
            in_specs=[whole(p.shape) for p in ops],
            out_specs=[whole((rows, width))] * 2,
            scratch_shapes=[pltpu.VMEM((2 * rows, width), F32)],
        ),
        out_shape=[
            jax.ShapeDtypeStruct((rows, width), BF),
            jax.ShapeDtypeStruct((rows, width), F32),
        ],
        compiler_params=params(),
        cost_estimate=cost(1e6, 5e6),
        name="first_stage",
    )(plan, *ops)


def next_kernel(base, count, plan, kept, got, sent, keep, total):
    total[...] = kept[...] + got[...].astype(F32)
    choose(total, plan, base, count, sent, keep)


def next_stage(plan, base, count, kept, got):
    rows, width = kept.shape
    return pl.pallas_call(
        functools.partial(next_kernel, base, count),
        grid_spec=pltpu.PrefetchScalarGridSpec(
            num_scalar_prefetch=1,
            grid=(1,),
            in_specs=[whole((rows, width))] * 2,
            out_specs=[whole((rows // 2, width))] * 2,
            scratch_shapes=[pltpu.VMEM((rows, width), F32)],
        ),
        out_shape=[
            jax.ShapeDtypeStruct((rows // 2, width), BF),
            jax.ShapeDtypeStruct((rows // 2, width), F32),
        ],
        compiler_params=params(),
        cost_estimate=cost(1e6, 3e6),
        name="next_stage",
    )(plan, kept, got)


def finish_kernel(sizes, plan, mine, theirs, *refs):
    outs, (sums, sem) = refs[:-2], refs[-2:]
    rows = mine.shape[0] // 4
    for h in range(2):
        for i in range(4):
            where = pl.ds(pl.multiple_of(plan[PLACES + i] * rows, rows), rows)
            at = (4 * h + i) * rows
            sums[at : at + rows, :] = jnp.where(
                plan[SIDE] == h, mine[where, :], theirs[where, :]
            ).astype(F32)
    copies, at = [], 0
    for ref, size in zip(outs, sizes):
        copies.append(pltpu.make_async_copy(sums.at[pl.ds(at, size)], ref, sem))
        copies[-1].start()
        at += size
    for copy in copies:
        copy.wait()


def finish(plan, mine, theirs, sizes):
    half, width = mine.shape
    return pl.pallas_call(
        functools.partial(finish_kernel, sizes),
        grid_spec=pltpu.PrefetchScalarGridSpec(
            num_scalar_prefetch=1,
            grid=(1,),
            in_specs=[whole((half, width))] * 2,
            out_specs=[ANY] * len(sizes),
            scratch_shapes=[pltpu.VMEM((2 * half, width), F32), pltpu.SemaphoreType.DMA(())],
        ),
        out_shape=[jax.ShapeDtypeStruct((size, width), F32) for size in sizes],
        compiler_params=params(),
        cost_estimate=cost(1e6, 5e6),
        name="finish",
    )(plan, mine, theirs)


def collect_kernel(*refs):
    attn, up, (second, first, send, keep) = refs[:4], refs[4:8], refs[8:]
    span = attn[0].shape[2]
    for ref, other, own in ((send, 0, 2), (keep, 1, 3)):
        ref[...] = jnp.zeros_like(ref)
        ref[0:1, 0:span] = attn[other][0, 0:1, :]
        ref[1:2, :] = up[other][0:1, :]
        ref[8:9, 0:span] = attn[own][0, 0:1, :]
        ref[9:10, :] = up[own][0:1, :]
        ref[16:19, :] = second[0:3, :]
        ref[19:22, :] = first[0:3, :]


def collect(*parts):
    width = parts[-1].shape[1]
    return pl.pallas_call(
        collect_kernel,
        grid=(1,),
        in_specs=[whole(p.shape) for p in parts],
        out_specs=[whole((24, width))] * 2,
        out_shape=[jax.ShapeDtypeStruct((24, width), F32)] * 2,
        compiler_params=params(),
        name="collect",
    )(*parts)


Y, X, Z_NEAR, Z_FAR = ("tensor", 2), ("dp", 1), ("dp", 2), ("dp", 4)


def tie(value, *others):
    return lax.optimization_barrier((value, others))[0]


def swap(value, even, odd=None):
    groups, width = lax.axis_size("dp"), lax.axis_size("tensor")
    pairs = []
    for group in range(groups):
        for t in range(width):
            axis, bit = even if odd is None or t % 2 == 0 else odd
            to = (group ^ bit, t) if axis == "dp" else (group, t ^ bit)
            pairs.append((group * width + t, to[0] * width + to[1]))
    return lax.ppermute(value, ("dp", "tensor"), pairs)


def partner(value):
    return swap(value, ("tensor", 1))


def make_plan():
    index, t = lax.axis_index("dp"), lax.axis_index("tensor")
    x, near, far, core = index % 2, index // 2 % 2, index // 4 % 2, t % 2
    quarter, place = x + 2 * near, near + 2 * far
    even = [quarter, quarter ^ 1, quarter ^ 2, quarter ^ 3]
    odd = [quarter, quarter ^ 2, quarter ^ 1, quarter ^ 3]
    even += odd + [0, 1, 2, 3]
    odd += even[:4] + [0, 1, 2, 3]
    even += [0, 1, 2, 3]
    odd += [1 - x, 3 - x, x, 2 + x]
    even += [1 - x, x]
    odd += [0, 1]
    even += [1 - near, 3 - near, near, 2 + near]
    odd += [2 - 2 * far, 3 - 2 * far, 2 * far, 2 * far + 1]
    even += [1 - far, far]
    odd += [1 - near, near]
    apart = [i ^ place for i in range(4)]
    even += [i // 2 + 2 * (i % 2) for i in apart]
    odd += apart
    even += [x]
    odd += [x]
    both = [jnp.stack([jnp.asarray(i, jnp.int32) for i in plan]) for plan in (even, odd)]
    return jnp.where(core == 0, *both)


class Gather:
    def __init__(self, sent, tail=0):
        self.tail = tail
        self.got = swap(sent, Y)

    def after(self, *values):
        self.got = tie(self.got, *values)

    def second(self):
        rows = self.got.shape[0] - self.tail
        self.rest = [self.got[rows:]] if self.tail else []
        self.held = self.got[:rows]
        self.got = swap(self.held, X, Z_NEAR)

    def third(self):
        self.held = jnp.concatenate([self.held, self.got], axis=0)
        self.got = swap(self.held, Z_NEAR, X)

    def result(self):
        return jnp.concatenate([self.held, self.got, *self.rest], axis=0)


class Reduction:
    def __init__(self, plan):
        self.plan = plan

    def after(self, *values):
        self.got = tie(self.got, *values)

    def first(self, parts, stacked=()):
        self.sent, self.keep = first_stage(self.plan, parts, stacked)
        self.got = swap(self.sent, Y, X)

    def second(self):
        self.sent, self.keep = next_stage(self.plan, SECOND, 1, self.keep, self.got)
        self.got = swap(self.sent, X, Y)

    def third(self):
        self.sent, self.keep = next_stage(self.plan, THIRD, 2, self.keep, self.got)
        self.got = swap(self.sent, Z_NEAR, Z_FAR)

    def fourth(self):
        self.sent, self.keep = next_stage(self.plan, FOURTH, 1, self.keep, self.got)
        self.got = swap(self.sent, Z_FAR, Z_NEAR)

    def fifth(self):
        total = (self.keep + self.got.astype(F32)).astype(BF)
        bit = 8
        while bit < lax.axis_size("dp"):
            total = (total.astype(F32) + swap(total, ("dp", bit)).astype(F32)).astype(BF)
            bit *= 2
        self.sent = total
        self.got = swap(self.sent, Z_FAR, Z_NEAR)

    def sixth(self):
        self.sent = jnp.concatenate([self.sent, self.got], axis=0)
        self.got = swap(self.sent, Z_NEAR, Z_FAR)

    def seventh(self):
        self.sent = jnp.concatenate([self.sent, self.got], axis=0)
        self.got = swap(self.sent, X)

    def result(self, sizes):
        return finish(self.plan, self.sent, self.got, sizes)


def on_device(
    tokens,
    w_query,
    w_key,
    w_value,
    b_query,
    b_value,
    w_output,
    b_output,
    first_gain,
    first_shift,
    w_up,
    b_up,
    w_down,
    b_down,
    second_gain,
    second_shift,
    cotangent,
):
    rows, width = tokens.shape
    local = w_query.shape[1]
    assert rows == SEQ_LEN and width == 4 * local and w_up.shape == (width, width)
    plan = make_plan()
    pack_d, near, far_up, far_down, table = pack_weights(
        plan, w_query, w_key, w_value, w_output, w_up, w_down,
        (b_query, b_value, b_up, b_output, first_gain, first_shift, b_down, second_gain,
         second_shift),
    )

    pack_c = partner(pack_d)
    far_pack = Gather(near, BIAS_ROWS)
    *saved_d, part = attention(plan, NATURAL, tokens, [pack_d])
    *saved_c, part = attention(plan, NATURAL, tokens, [pack_c], part)
    far_pack.after(part)
    far_pack.second()
    up_far = Gather(tie(far_up, far_pack.held))
    far_pack.third()
    up_far.after(far_pack.held)
    up_far.second()
    down_far = Gather(tie(far_down, up_far.held))
    up_d, down_d = w_up, w_down
    up_c = partner(tie(w_up, far_pack.held))
    pack_b = far_pack.result()
    pack_a = partner(pack_b)
    up_far.after(pack_b)
    up_far.third()
    *saved_b, part = attention(tie(plan, up_far.held), BY_B, tokens, [pack_b], part)
    down_far.after(part)
    down_far.second()
    down_c = partner(tie(w_down, down_far.held))
    *saved_a, normed_low, unit, scale = attention(
        tie(plan, down_far.held), BY_A, tokens, [pack_a], part, table
    )
    down_far.after(normed_low)
    down_far.third()
    act_d, slope_d, part = feed(
        tie(plan, down_far.held), NATURAL, normed_low, [up_d], [down_d], [pack_d]
    )
    up_far.after(part)
    up_b = up_far.result()
    up_a = partner(up_b)
    act_c, slope_c, part = feed(
        tie(plan, up_b), NATURAL, normed_low, [up_c], [down_c], [pack_c], part
    )
    down_far.after(part)
    down_b = down_far.result()
    down_a = partner(down_b)
    act_b, slope_b, part = feed(plan, BY_B, normed_low, [up_b], [down_b], [pack_b], part)
    act_a, slope_a, layer_out, down_low, grad_second, small_second = feed(
        plan, BY_A, normed_low, [up_a], [down_a], [pack_a], part, [unit, table, cotangent]
    )

    down, up, attn = Reduction(plan), Reduction(plan), Reduction(plan)
    grad_a, grad_b = down_grad([act_a, act_b], down_low)
    core_other = partner(grad_a)
    grad_c, grad_d = down_grad([act_c, act_d], tie(down_low, grad_a))
    core_own = partner(grad_c)
    up_grad_a, bias_up_a, part = feed_back(
        tie(plan, grad_c), BY_A, slope_a, down_low, normed_low, grad_second, up_a, down_a
    )
    core_up_other = partner(up_grad_a)
    down.first([grad_b, *tie((core_other,), up_grad_a), grad_d, core_own])
    up_grad_b, bias_up_b, part = feed_back(
        tie(plan, down.sent), BY_B, slope_b, down_low, normed_low, part, up_b, down_b
    )
    up_grad_c, bias_up_c, part = feed_back(
        tie(plan, core_up_other), NATURAL, slope_c, down_low, normed_low, part, up_c, down_c
    )
    core_up_own = partner(up_grad_c)
    up_grad_d, bias_up_d, grad_first, first_low, small_first = feed_back(
        plan, NATURAL, slope_d, down_low, normed_low, part, up_d, down_d, [unit, scale, table]
    )
    out_send, out_keep = out_grad([s[2] for s in (saved_a, saved_b, saved_c, saved_d)], first_low)
    core_out = partner(out_send)
    down.after(out_keep)
    down.second()
    grad_a, bias_a, part = attention_back(
        tie(plan, down.sent), BY_A, saved_a, first_low, tokens, grad_first, [pack_a], F32
    )
    core_other = partner(grad_a)
    up.first([up_grad_b, core_up_other, up_grad_d, core_up_own], [out_keep, tie(core_out, grad_a)])
    down.after(up.sent)
    down.third()
    grad_b, bias_b, part = attention_back(
        tie(plan, down.sent), BY_B, saved_b, first_low, tokens, part, [pack_b], F32
    )
    down.after(grad_b)
    down.fourth()
    grad_c, bias_c, part = attention_back(
        tie(plan, down.sent, core_other), NATURAL, saved_c, first_low, tokens, part, [pack_c], F32
    )
    core_own = partner(grad_c)
    down.after(grad_c)
    down.fifth()
    grad_d, bias_d, grad_tokens = attention_back(
        tie(plan, down.sent), NATURAL, saved_d, first_low, tokens, part, [pack_d], BF
    )
    attn.first([grad_b, core_other, grad_d, tie(core_own, grad_d)])
    down.after(attn.sent)
    down.sixth()
    up.after(down.sent)
    up.second()
    down.after(up.sent)
    down.seventh()
    up.after(down.sent)
    up.third()
    attn.after(up.sent)
    attn.second()
    up.after(attn.sent)
    up.fourth()
    attn.after(up.sent)
    attn.third()
    up.after(attn.sent)
    up.fifth()
    attn.after(up.sent)
    attn.fourth()
    up.after(attn.sent)
    up.sixth()
    attn.after(up.sent)
    attn.fifth()
    up.after(attn.sent)
    up.seventh()
    attn.after(up.sent)
    attn.sixth()
    down.after(attn.sent)
    attn.after(down.got)
    attn.seventh()
    (grad_w_down,) = down.result((width,))
    up.after(attn.sent)
    grad_w_up, grad_o = up.result((width, local))
    grad_q, grad_k, grad_v = attn.result((local,) * 3)

    send, keep = collect(
        bias_a, bias_b, bias_c, bias_d, bias_up_a, bias_up_b, bias_up_c, bias_up_d,
        small_second, tie(small_first, up.keep),
    )
    keep = keep + partner(send)
    got = swap(keep, Y)
    keep = jnp.concatenate([keep[8:16] + got[0:8], keep[16:24] + got[16:24]], axis=0)
    bit = 1
    while bit < lax.axis_size("dp"):
        keep = keep + swap(keep, ("dp", bit))
        bit *= 2

    return (
        layer_out,
        grad_tokens,
        grad_q.T,
        grad_k.T,
        grad_v.T,
        keep[0, :local],
        keep[0, 2 * local : 3 * local],
        grad_o,
        keep[11],
        keep[12],
        keep[13],
        grad_w_up,
        keep[1],
        grad_w_down,
        keep[8],
        keep[9],
        keep[10],
    )


def solution(mesh):
    rows = P(("dp", "tensor"), None)
    col, row, vec, rep = P(None, "tensor"), P("tensor", None), P("tensor"), P()
    return jax.shard_map(
        on_device,
        mesh=mesh,
        in_specs=(
            rows, col, col, col, vec, vec, row, rep, rep, rep, col, vec, row, rep, rep, rep, rows,
        ),
        out_specs=(
            rows, rows, col, col, col, vec, vec, row, rep, rep, rep, col, vec, row, rep, rep, rep,
        ),
        check_vma=False,
    )
```

```python
import functools

import jax
import jax.numpy as jnp
from jax import lax
from jax.experimental import pallas as pl
from jax.experimental.pallas import tpu as pltpu
from jax.sharding import PartitionSpec as P

HEAD = 64
SEQ_LEN = 512
BIAS_ROWS = 16
BF = jnp.bfloat16
F32 = jnp.float32
ANY = pl.BlockSpec(memory_space=pl.ANY)
VMEM_BYTES = 26 << 20
BY_B, BY_A, NATURAL, FIRST, SECOND, THIRD, FOURTH, PLACES, SIDE, QUARTERS = 0, 4, 8, 12, 16, 18, 22, 24, 28, 29
ALL_VMEM_BYTES = 60 << 20
UNROLL = 1


def dot(left, right, left_dim, right_dim):
    return lax.dot_general(
        left, right, (((left_dim,), (right_dim,)), ((), ())), preferred_element_type=F32
    )


SMALL = pl.CostEstimate(flops=1000, bytes_accessed=1000, transcendentals=0)


def whole(shape):
    return pl.BlockSpec(shape, lambda *_: (0,) * len(shape))


def params(limit=VMEM_BYTES):
    return pltpu.CompilerParams(vmem_limit_bytes=limit)


def cost(flops, moved):
    return pl.CostEstimate(flops=int(20 * flops), bytes_accessed=int(20 * moved), transcendentals=0)


def run(kernel, name, outs, *ops, scratch=(), estimate=SMALL, plan=None):
    specs = [pl.BlockSpec(memory_space=pltpu.VMEM)] * len(ops)
    if plan is not None:
        ops = (plan, *ops)
        specs.insert(0, pl.BlockSpec(memory_space=pltpu.SMEM))
    return pl.pallas_call(
        kernel,
        in_specs=specs,
        out_specs=[pl.BlockSpec(memory_space=pltpu.VMEM)] * len(outs),
        out_shape=[jax.ShapeDtypeStruct(shape, dtype) for shape, dtype in outs],
        scratch_shapes=scratch,
        compiler_params=params(),
        cost_estimate=estimate,
        name=name,
    )(*ops)


def pack_kernel(plan, wq, wk, wv, wo, wu, wd, *refs):
    vectors, refs = refs[:9], refs[9:]
    out, near, up_near, up_far, down_near, down_far, table, packed, piece, lines, *lists, sem = refs
    local, width = wq.shape
    at = pl.multiple_of(plan[BY_B] * local, local)
    copies = [
        pltpu.make_async_copy(ref, packed.at[pl.ds(i * local, local)], sem.at[0])
        for i, ref in enumerate((wq, wk, wv, wo))
    ]
    copies += [
        pltpu.make_async_copy(ref, line, sem.at[0]) for ref, line in zip(vectors, lists)
    ]
    opposite = pl.multiple_of(plan[QUARTERS + 3] * local, local)
    pieces = [
        pltpu.make_async_copy(ref.at[pl.ds(rows, local)], piece.at[i], sem.at[1])
        for i, (ref, rows) in enumerate(((wu, at), (wu, opposite), (wd, at), (wd, opposite)))
    ]
    for copy in copies:
        copy.start()
    for copy in pieces:
        copy.start()
    packed[4 * local :, :] = jnp.zeros((BIAS_ROWS, width), BF)
    lines[...] = jnp.zeros_like(lines)
    for copy in copies:
        copy.wait()
    bq, bv, bu = lists[:3]
    packed[4 * local : 4 * local + 1, 0:local] = bq[...].reshape(1, local)
    packed[4 * local : 4 * local + 1, local : 2 * local] = bv[...].reshape(1, local)
    packed[4 * local + 1 : 4 * local + 2, :] = bu[...].reshape(1, width)
    outs = [
        pltpu.make_async_copy(
            packed.at[pl.ds(at, local)], near.at[pl.ds(0, local)], sem.at[2]
        ),
        pltpu.make_async_copy(
            packed.at[pl.ds(4 * local, BIAS_ROWS)], near.at[pl.ds(local, BIAS_ROWS)], sem.at[2]
        ),
        pltpu.make_async_copy(packed, out, sem.at[2]),
    ]
    for copy in outs:
        copy.start()
    for i, ref in enumerate(lists[3:]):
        lines[i : i + 1, :] = ref[...].astype(F32).reshape(1, width)
    outs.append(pltpu.make_async_copy(lines, table, sem.at[2]))
    outs[-1].start()
    for copy in pieces:
        copy.wait()
    for i, ref in enumerate((up_near, up_far, down_near, down_far)):
        outs.append(pltpu.make_async_copy(piece.at[i], ref, sem.at[2]))
        outs[-1].start()
    for copy in outs:
        copy.wait()


def pack_weights(plan, w_query, w_key, w_value, w_output, w_up, w_down, vectors):
    local, width = w_output.shape
    shapes = [
        jax.ShapeDtypeStruct((4 * local + BIAS_ROWS, width), BF),
        jax.ShapeDtypeStruct((local + BIAS_ROWS, width), BF),
        *[jax.ShapeDtypeStruct((local, width), BF)] * 4,
        jax.ShapeDtypeStruct((8, width), F32),
    ]
    return pl.pallas_call(
        pack_kernel,
        grid_spec=pltpu.PrefetchScalarGridSpec(
            num_scalar_prefetch=1,
            grid=(1,),
            in_specs=[ANY] * 15,
            out_specs=[ANY] * 7,
            scratch_shapes=[
                pltpu.VMEM(shapes[0].shape, BF),
                pltpu.VMEM((4, *shapes[2].shape), BF),
                pltpu.VMEM(shapes[6].shape, F32),
                *[pltpu.VMEM(v.shape, BF) for v in vectors],
                pltpu.SemaphoreType.DMA((3,)),
            ],
        ),
        out_shape=shapes,
        compiler_params=params(ALL_VMEM_BYTES),
        name="pack_weights",
    )(plan, w_query.T, w_key.T, w_value.T, w_output, w_up, w_down, *vectors)


def join_kernel(base, plan, *refs):
    *pieces, out = refs
    at = 0
    rows = pieces[0].shape[0]
    for ref in pieces:
        if at < 4:
            count = ref.shape[0] // rows
            for i in range(count):
                where = pl.multiple_of(plan[base + at + i] * rows, rows)
                copy_rows(out, where, ref, i * rows, rows)
            at += count
        else:
            out[4 * rows :, :] = ref[...]


def normalize(rows):
    center = rows - jnp.mean(rows, axis=-1, keepdims=True)
    scale = lax.rsqrt(jnp.mean(center * center, axis=-1, keepdims=True) + 1e-12)
    return center * scale, scale


def norm_back(grad, unit, scale):
    return scale * (
        grad
        - jnp.mean(grad, axis=-1, keepdims=True)
        - unit * jnp.mean(grad * unit, axis=-1, keepdims=True)
    )


def by_blocks(rows, body, block=128):
    def step(i, carry):
        body(pl.ds(pl.multiple_of(i * block, block), block))
        return carry

    lax.fori_loop(0, rows // block, step, 0)


def head_rows(head, local, count):
    return [pl.ds(pl.multiple_of(i * local + head * HEAD, HEAD), HEAD) for i in range(count)]


def attention_kernel(first, last, *refs):
    tok, weights, *refs = refs
    if not first:
        part_in, *refs = refs
    if last:
        table, *refs = refs
        qkv, probs, att, bias_up, normed_low, unit, scale, part = refs
    else:
        qkv, probs, att, bias_up, part = refs
    local = att.shape[0]
    body = 4 * local
    rows = weights[body : body + BIAS_ROWS, :].astype(F32)
    bias_up[...] = rows[1:2, :]
    bias = jnp.transpose(rows)
    tokens = tok[...]
    qkv[0:local, :] = (
        dot(weights[0:local, :], tokens, 1, 1) + bias[0:local, 0:1]
    ).astype(BF) * BF(0.125)
    qkv[local : 2 * local, :] = dot(weights[local : 2 * local, :], tokens, 1, 1).astype(BF)
    qkv[2 * local : 3 * local, :] = (
        dot(weights[2 * local : 3 * local, :], tokens, 1, 1) + bias[local : 2 * local, 0:1]
    ).astype(BF)

    def one_head(head, carry):
        spans = head_rows(head, local, 3)
        queries, keys, values = (qkv[span, :] for span in spans)
        scores = dot(keys, queries, 0, 0)
        unnorm = jnp.exp(scores - jnp.max(scores, axis=0, keepdims=True))
        prob = (unnorm * (1.0 / jnp.sum(unnorm, axis=0, keepdims=True))).astype(BF)
        probs[head] = prob
        att[spans[0], :] = dot(values, prob, 1, 0).astype(BF)
        return carry

    lax.fori_loop(0, local // HEAD, one_head, 0, unroll=UNROLL)
    out = dot(att[...], weights[3 * local : 4 * local, :], 0, 0)
    part[...] = out if first else out + part_in[...]
    if last:

        def block(r):
            total = part[r, :] + table[0:1, :] + tok[r, :].astype(F32)
            unit_rows, scale_rows = normalize(total)
            unit[r, :] = unit_rows
            scale[r, :] = scale_rows
            normed_low[r, :] = (unit_rows * table[1:2, :] + table[2:3, :]).astype(BF)

        by_blocks(tok.shape[0], block)


def attention(tokens, pack, part=None, table=None):
    rows, width = tokens.shape
    local = (pack.shape[0] - BIAS_ROWS) // 4
    first, last = part is None, table is not None
    ops = [tokens, pack] + [x for x in (part, table) if x is not None]
    outs = [((3 * local, rows), BF), ((local // HEAD, rows, rows), BF), ((local, rows), BF)]
    outs += [((1, width), F32)]
    if last:
        outs += [((rows, width), BF), ((rows, width), F32), ((rows, 1), F32)]
    else:
        outs += [((rows, width), F32)]
    return run(
        functools.partial(attention_kernel, first, last),
        "attention_last" if last else "attention",
        outs,
        *ops,
        scratch=[pltpu.VMEM((rows, width), F32)] if last else [],
        estimate=cost(2.5e9, 4e6),
    )


def feed_kernel(first, last, *refs):
    low, up, down, bias, *refs = refs
    if not first:
        part_in, *refs = refs
    if last:
        unit, table, cot, act, slope, layer_out, down_low, grad_second, small, part = refs
    else:
        act, slope, part = refs
    rows = dot(low[...], up[...], 1, 0) + bias[...]
    cdf = 0.5 * (1.0 + lax.erf(rows * 0.7071067811865476))
    active = (rows * cdf).astype(BF)
    act[...] = active
    slope[...] = (cdf + (rows * 0.3989422804014327) * jnp.exp(-0.5 * rows * rows)).astype(BF)
    out = dot(active, down[...], 1, 0)
    part[...] = out if first else out + part_in[...]
    if last:
        small[...] = jnp.zeros_like(small)

        def block(r):
            normed = unit[r, :] * table[1:2, :] + table[2:3, :]
            unit2, scale2 = normalize(part[r, :] + table[3:4, :] + normed)
            layer_out[r, :] = (unit2 * table[4:5, :] + table[5:6, :]).astype(BF)
            cots = cot[r, :].astype(F32)
            grad = norm_back(cots * table[4:5, :], unit2, scale2)
            grad_second[r, :] = grad
            down_low[r, :] = grad.astype(BF)
            small[0:1, :] += jnp.sum(grad, axis=0, keepdims=True)
            small[1:2, :] += jnp.sum(cots * unit2, axis=0, keepdims=True)
            small[2:3, :] += jnp.sum(cots, axis=0, keepdims=True)

        by_blocks(low.shape[0], block)


def feed(low, up, down, bias, part=None, extra=None):
    rows, width = low.shape
    hidden = up.shape[1]
    first, last = part is None, extra is not None
    ops = [low, up, down, bias] + ([] if first else [part]) + (extra or [])
    outs = [((rows, hidden), BF)] * 2
    if last:
        outs += [((rows, width), BF), ((rows, width), BF), ((rows, width), F32), ((8, width), F32)]
    else:
        outs += [((rows, width), F32)]
    return run(
        functools.partial(feed_kernel, first, last),
        "feed_last" if last else "feed",
        outs,
        *ops,
        scratch=[pltpu.VMEM((rows, width), F32)] if last else [],
        estimate=cost(2.5e9 if last else 1.5e9, 4e6),
    )


def down_grad_kernel(*refs):
    count = len(refs) // 2
    low = refs[count]
    for act, out in zip(refs[:count], refs[count + 1 :]):
        out[...] = dot(act[...], low[...], 0, 0).astype(BF)


def down_grad(acts, low):
    return run(
        down_grad_kernel,
        "down_grad",
        [((acts[0].shape[1], low.shape[1]), BF)] * len(acts),
        *acts,
        low,
        estimate=cost(1.2e9, 4e6),
    )


def feed_back_kernel(last, *refs):
    slope, down_low, normed_low, grad_in, up, down, *refs = refs
    if last:
        unit, scale, table, grads, bias, grad_first, first_low, small, part = refs
    else:
        grads, bias, part = refs
    grad_up = (dot(down_low[...], down[...], 1, 1) * slope[...].astype(F32)).astype(BF)
    bias[...] = jnp.sum(grad_up.astype(F32), axis=0, keepdims=True)
    grads[...] = dot(normed_low[...], grad_up, 0, 0).astype(BF)
    part[...] = grad_in[...] + dot(grad_up, up[...], 1, 1)
    if last:
        small[...] = jnp.zeros_like(small)

        def block(r):
            grad = part[r, :]
            units = unit[r, :]
            first = norm_back(grad * table[1:2, :], units, scale[r, :])
            grad_first[r, :] = first
            first_low[r, :] = first.astype(BF)
            small[0:1, :] += jnp.sum(first, axis=0, keepdims=True)
            small[1:2, :] += jnp.sum(grad * units, axis=0, keepdims=True)
            small[2:3, :] += jnp.sum(grad, axis=0, keepdims=True)

        by_blocks(part.shape[0], block)


def feed_back(slope, down_low, normed_low, grad_in, up, down, extra=None):
    rows, width = down_low.shape
    hidden = up.shape[1]
    last = extra is not None
    outs = [((width, hidden), BF), ((1, hidden), F32), ((rows, width), F32)]
    if last:
        outs += [((rows, width), BF), ((8, width), F32)]
    return run(
        functools.partial(feed_back_kernel, last),
        "feed_back_last" if last else "feed_back",
        outs,
        slope,
        down_low,
        normed_low,
        grad_in,
        up,
        down,
        *(extra or []),
        scratch=[pltpu.VMEM((rows, width), F32)] if last else [],
        estimate=cost(2.5e9 if last else 2e9, 5e6),
    )


def attention_back_kernel(qkv, probs, first_low, tok, grad_in, weights, grads, bias, out, work):
    local = qkv.shape[0] // 3
    work[3 * local :, :] = dot(weights[3 * local : 4 * local, :], first_low[...], 1, 1).astype(BF)

    def one_head(head, carry):
        spans = head_rows(head, local, 4)
        queries, keys, values = (qkv[span, :] for span in spans[:3])
        grad_att = work[spans[3], :]
        prob = probs[head]
        grad_prob = dot(values, grad_att, 0, 0)
        wide = prob.astype(F32)
        inner = jnp.sum(wide * grad_prob, axis=0, keepdims=True)
        grad_score = (wide * (grad_prob - inner)).astype(BF)
        work[spans[0], :] = (dot(keys, grad_score, 1, 0) * 0.125).astype(BF)
        work[spans[1], :] = dot(queries, grad_score, 1, 1).astype(BF)
        work[spans[2], :] = dot(grad_att, prob, 1, 1).astype(BF)
        return carry

    lax.fori_loop(0, local // HEAD, one_head, 0, unroll=UNROLL)
    joined = work[0 : 3 * local, :]
    grads[...] = dot(joined, tok[...], 1, 0).astype(BF)
    bias[...] = dot(jnp.ones((8, joined.shape[1]), BF), joined, 1, 1)
    out[...] = (grad_in[...] + dot(joined, weights[0 : 3 * local, :], 0, 0)).astype(out.dtype)


def attention_back(saved, first_low, tokens, grad_in, pack, out_dtype):
    qkv, probs, _ = saved
    rows, width = tokens.shape
    joined = qkv.shape[0]
    return run(
        attention_back_kernel,
        "attention_back",
        [((joined, width), BF), ((8, joined), F32), ((rows, width), out_dtype)],
        qkv,
        probs,
        first_low,
        tokens,
        grad_in,
        pack,
        scratch=[pltpu.VMEM((joined // 3 * 4, rows), BF)],
        estimate=cost(3.5e9, 6e6),
    )


def out_grad_kernel(a, b, c, d, low, send, keep):
    for ref, both in ((send, (a, c)), (keep, (b, d))):
        for i, att in enumerate(both):
            ref[i] = dot(att[...], low[...], 1, 0).astype(BF)


def out_grad(atts, low):
    shape = (2, atts[0].shape[0], low.shape[1])
    return run(
        out_grad_kernel, "out_grad", [(shape, BF)] * 2, *atts, low, estimate=cost(6e8, 3e6)
    )


def join(plan, base, *pieces):
    rows = sum(p.shape[0] for p in pieces)
    (out,) = run(
        functools.partial(join_kernel, base), "join", [((rows, pieces[0].shape[1]), BF)], *pieces,
        plan=plan,
    )
    return out


def add_rows(total, at, left, right):
    block = 64

    def body(i, carry):
        r = pl.ds(pl.multiple_of(i * block, block), block)
        to = pl.ds(pl.multiple_of(at + i * block, block), block)
        total[to, :] = left[r, :].astype(F32) + right[r, :].astype(F32)
        return carry

    lax.fori_loop(0, left.shape[0] // block, body, 0)


def copy_rows(target, to, source, at, rows):
    block = next(b for b in (48, 40, 32, 24, 8) if rows % b == 0)

    def body(i, carry):
        here = pl.ds(pl.multiple_of(at + i * block, 8), block)
        there = pl.ds(pl.multiple_of(to + i * block, 8), block)
        target[there, :] = source[here, :].astype(target.dtype)
        return carry

    lax.fori_loop(0, rows // block, body, 0)


def choose(total, plan, base, count, sent, keep):
    rows = sent.shape[0] // count
    for i in range(count):
        for ref, at in ((sent, base + i), (keep, base + count + i)):
            copy_rows(ref, i * rows, total, pl.multiple_of(plan[at] * rows, rows), rows)


def first_kernel(stacked, plan, *refs):
    *parts, sent, keep, total = refs
    rows = sent.shape[0]
    at = 0
    for other, core_other, own, core_own in zip(*[iter(parts)] * 4):
        size = other.shape[0]
        add_rows(total, at, other, core_other)
        add_rows(total, rows + at, own, core_own)
        at += size
    if stacked:
        mine, theirs = parts[-2:]
        size = mine.shape[1]
        add_rows(total, at, mine.at[0], theirs.at[0])
        add_rows(total, rows + at, mine.at[1], theirs.at[1])
    choose(total, plan, FIRST, 2, sent, keep)


def first_stage(plan, parts, stacked):
    width = parts[0].shape[-1]
    rows = parts[0].shape[0] + (stacked[0].shape[1] if stacked else 0)
    return run(
        functools.partial(first_kernel, bool(stacked)),
        "first_stage",
        [((rows, width), BF), ((rows, width), F32)],
        *parts,
        *stacked,
        scratch=[pltpu.VMEM((2 * rows, width), F32)],
        plan=plan,
    )


def next_kernel(base, count, plan, kept, got, sent, keep, total):
    total[...] = kept[...] + got[...].astype(F32)
    choose(total, plan, base, count, sent, keep)


def next_stage(plan, base, count, kept, got):
    rows, width = kept.shape
    return run(
        functools.partial(next_kernel, base, count),
        "next_stage",
        [((rows // 2, width), BF), ((rows // 2, width), F32)],
        kept,
        got,
        scratch=[pltpu.VMEM((rows, width), F32)],
        plan=plan,
    )


def finish_kernel(sizes, plan, mine, theirs, *refs):
    outs, (sums, sem) = refs[:-2], refs[-2:]
    rows = mine.shape[0] // 4
    for h in range(2):
        for i in range(4):
            where = pl.ds(pl.multiple_of(plan[PLACES + i] * rows, rows), rows)
            at = (4 * h + i) * rows
            sums[at : at + rows, :] = jnp.where(
                plan[SIDE] == h, mine[where, :], theirs[where, :]
            ).astype(F32)
    copies, at = [], 0
    for ref, size in zip(outs, sizes):
        copies.append(pltpu.make_async_copy(sums.at[pl.ds(at, size)], ref, sem))
        copies[-1].start()
        at += size
    for copy in copies:
        copy.wait()


def finish(plan, mine, theirs, sizes):
    half, width = mine.shape
    return pl.pallas_call(
        functools.partial(finish_kernel, sizes),
        grid_spec=pltpu.PrefetchScalarGridSpec(
            num_scalar_prefetch=1,
            grid=(1,),
            in_specs=[whole((half, width))] * 2,
            out_specs=[ANY] * len(sizes),
            scratch_shapes=[pltpu.VMEM((2 * half, width), F32), pltpu.SemaphoreType.DMA(())],
        ),
        out_shape=[jax.ShapeDtypeStruct((size, width), F32) for size in sizes],
        compiler_params=params(),
        cost_estimate=SMALL,
        name="finish",
    )(plan, mine, theirs)


def collect_kernel(*refs):
    attn, up, (second, first, send, keep) = refs[:4], refs[4:8], refs[8:]
    span = attn[0].shape[1]
    for ref, other, own in ((send, 0, 2), (keep, 1, 3)):
        ref[...] = jnp.zeros_like(ref)
        ref[0:1, 0:span] = attn[other][0:1, :]
        ref[1:2, :] = up[other][...]
        ref[8:9, 0:span] = attn[own][0:1, :]
        ref[9:10, :] = up[own][...]
        ref[16:19, :] = second[0:3, :]
        ref[19:22, :] = first[0:3, :]


def collect(*parts):
    width = parts[-1].shape[1]
    return run(collect_kernel, "collect", [((24, width), F32)] * 2, *parts)


Y, X, Z_NEAR, Z_FAR = ("tensor", 2), ("dp", 1), ("dp", 2), ("dp", 4)


def tie(value, *others):
    return lax.optimization_barrier((value, others))[0]


def swap(value, even, odd=None):
    groups, width = lax.axis_size("dp"), lax.axis_size("tensor")
    pairs = []
    for group in range(groups):
        for t in range(width):
            axis, bit = even if odd is None or t % 2 == 0 else odd
            to = (group ^ bit, t) if axis == "dp" else (group, t ^ bit)
            pairs.append((group * width + t, to[0] * width + to[1]))
    return lax.ppermute(value, ("dp", "tensor"), pairs)


def partner(value):
    return swap(value, ("tensor", 1))


def make_plan():
    index, t = lax.axis_index("dp"), lax.axis_index("tensor")
    x, near, far, core = index % 2, index // 2 % 2, index // 4 % 2, t % 2
    quarter, place = x + 2 * near, near + 2 * far
    even = [quarter, quarter ^ 1, quarter ^ 2, quarter ^ 3]
    odd = [quarter, quarter ^ 2, quarter ^ 1, quarter ^ 3]
    even += odd + [0, 1, 2, 3]
    odd += even[:4] + [0, 1, 2, 3]
    even += [0, 1, 2, 3]
    odd += [1 - x, 3 - x, x, 2 + x]
    even += [1 - x, x]
    odd += [0, 1]
    even += [1 - near, 3 - near, near, 2 + near]
    odd += [2 - 2 * far, 3 - 2 * far, 2 * far, 2 * far + 1]
    even += [1 - far, far]
    odd += [1 - near, near]
    apart = [i ^ place for i in range(4)]
    even += [i // 2 + 2 * (i % 2) for i in apart]
    odd += apart
    quarters = [quarter ^ i for i in range(4)]
    even += [x, *quarters]
    odd += [x, *quarters]
    both = [jnp.stack([jnp.asarray(i, jnp.int32) for i in plan]) for plan in (even, odd)]
    return jnp.where(core == 0, *both)


class Gather:
    def __init__(self, plan, sent, tail=0):
        self.plan, self.tail = plan, tail
        self.got = swap(sent, Y)

    def after(self, *values):
        self.got = tie(self.got, *values)

    @classmethod
    def of_two(cls, plan, near, far):
        self = cls(plan, near)
        self.far = swap(far, Y)
        return self

    def both(self):
        self.held = self.got
        self.got = [swap(self.held, X), swap(self.held, Z_NEAR)]

    def joined(self):
        return join(self.plan, QUARTERS, self.held, *self.got, self.far)

    def second(self):
        rows = self.got.shape[0] - self.tail
        self.rest = [self.got[rows:]] if self.tail else []
        self.held = self.got[:rows]
        self.got = swap(self.held, X, Z_NEAR)

    def third(self):
        self.held = jnp.concatenate([self.held, self.got], axis=0)
        self.got = swap(self.held, Z_NEAR, X)

    def result(self):
        rows = self.held.shape[0] // 2
        return join(
            self.plan, BY_B, self.held[:rows], self.held[rows:], self.got[:rows], self.got[rows:], *self.rest
        )


class Reduction:
    def __init__(self, plan):
        self.plan = plan

    def after(self, *values):
        self.got = tie(self.got, *values)

    def first(self, parts, stacked=()):
        self.sent, self.keep = first_stage(self.plan, parts, stacked)
        self.got = swap(self.sent, Y, X)

    def second(self):
        self.sent, self.keep = next_stage(self.plan, SECOND, 1, self.keep, self.got)
        self.got = swap(self.sent, X, Y)

    def third(self):
        self.sent, self.keep = next_stage(self.plan, THIRD, 2, self.keep, self.got)
        self.got = swap(self.sent, Z_NEAR, Z_FAR)

    def fourth(self):
        self.sent, self.keep = next_stage(self.plan, FOURTH, 1, self.keep, self.got)
        self.got = swap(self.sent, Z_FAR, Z_NEAR)

    def fifth(self):
        total = (self.keep + self.got.astype(F32)).astype(BF)
        bit = 8
        while bit < lax.axis_size("dp"):
            total = (total.astype(F32) + swap(total, ("dp", bit)).astype(F32)).astype(BF)
            bit *= 2
        self.sent = total
        self.got = swap(self.sent, Z_FAR, Z_NEAR)

    def sixth(self):
        self.sent = jnp.concatenate([self.sent, self.got], axis=0)
        self.got = swap(self.sent, Z_NEAR, Z_FAR)

    def seventh(self):
        self.sent = jnp.concatenate([self.sent, self.got], axis=0)
        self.got = swap(self.sent, X)

    def result(self, sizes):
        return finish(self.plan, self.sent, self.got, sizes)


class Vectors:
    def __init__(self, *parts):
        send, self.keep = collect(*parts)
        self.got = partner(send)

    def after(self, *values):
        self.got = tie(self.got, *values)

    def across(self):
        self.sent = self.keep = self.keep + self.got
        self.got = swap(self.sent, Y)

    def along(self, bit):
        if bit == 1:
            kept, got = self.keep, self.got
            self.keep = jnp.concatenate([kept[8:16] + got[0:8], kept[16:24] + got[16:24]], axis=0)
        else:
            self.keep = self.keep + self.got
        self.sent = self.keep
        self.got = swap(self.sent, ("dp", bit))

    def result(self):
        keep = self.keep + self.got
        bit = 8
        while bit < lax.axis_size("dp"):
            keep = keep + swap(keep, ("dp", bit))
            bit *= 2
        return keep


def on_device(
    tokens,
    w_query,
    w_key,
    w_value,
    b_query,
    b_value,
    w_output,
    b_output,
    first_gain,
    first_shift,
    w_up,
    b_up,
    w_down,
    b_down,
    second_gain,
    second_shift,
    cotangent,
):
    rows, width = tokens.shape
    local = w_query.shape[1]
    assert rows == SEQ_LEN and width == 4 * local and w_up.shape == (width, width)
    plan = make_plan()
    pack_d, near, up_near, up_far, down_near, down_far, table = pack_weights(
        plan, w_query, w_key, w_value, w_output, w_up, w_down,
        (b_query, b_value, b_up, b_output, first_gain, first_shift, b_down, second_gain,
         second_shift),
    )

    far_pack = Gather(plan, near, BIAS_ROWS)
    pack_c = partner(tie(pack_d, near))
    *saved_d, bias_d, part = attention(tokens, pack_d)
    up = Gather.of_two(plan, *tie((up_near, up_far), near))
    *saved_c, bias_c, part = attention(tokens, pack_c, part)
    far_pack.after(part)
    far_pack.second()
    down = Gather.of_two(plan, *tie((down_near, down_far), far_pack.held))
    far_pack.third()
    up_d, down_d = w_up, w_down
    up_c = partner(tie(w_up, far_pack.held))
    pack_b = far_pack.result()
    pack_a = partner(pack_b)
    *saved_b, bias_b, part = attention(tokens, pack_b, part)
    up.after(part)
    up.both()
    down_c = partner(tie(w_down, up.held))
    *saved_a, bias_a, normed_low, unit, scale = attention(
        tokens, pack_a, tie(part, up.held), table
    )
    down.after(normed_low)
    down.both()
    act_d, slope_d, part = feed(tie(normed_low, down.held), up_d, down_d, bias_d)
    up.got, up.far = tie((up.got, up.far), part)
    up_b = up.joined()
    up_a = partner(up_b)
    act_c, slope_c, part = feed(normed_low, up_c, down_c, bias_c, tie(part, up_b))
    down.got, down.far = tie((down.got, down.far), part)
    down_b = down.joined()
    down_a = partner(down_b)
    act_b, slope_b, part = feed(normed_low, up_b, down_b, bias_b, part)
    act_a, slope_a, layer_out, down_low, grad_second, small_second = feed(
        normed_low, up_a, down_a, bias_a, part, [unit, table, cotangent]
    )

    down, up, attn = Reduction(plan), Reduction(plan), Reduction(plan)
    grad_a, grad_b = down_grad([act_a, act_b], down_low)
    core_other = partner(grad_a)
    grad_c, grad_d = down_grad([act_c, act_d], tie(down_low, grad_a))
    core_own = partner(grad_c)
    up_grad_a, bias_up_a, part = feed_back(
        slope_a, down_low, normed_low, tie(grad_second, grad_c), up_a, down_a
    )
    core_up_other = partner(up_grad_a)
    down.first([grad_b, *tie((core_other,), up_grad_a), grad_d, core_own])
    up_grad_b, bias_up_b, part = feed_back(
        slope_b, down_low, normed_low, tie(part, down.sent), up_b, down_b
    )
    up_grad_c, bias_up_c, part = feed_back(
        slope_c, down_low, normed_low, tie(part, core_up_other), up_c, down_c
    )
    core_up_own = partner(up_grad_c)
    up_grad_d, bias_up_d, grad_first, first_low, small_first = feed_back(
        slope_d, down_low, normed_low, part, up_d, down_d, [unit, scale, table]
    )
    out_send, out_keep = out_grad([s[2] for s in (saved_a, saved_b, saved_c, saved_d)], first_low)
    core_out = partner(out_send)
    down.after(out_keep)
    down.second()
    up.first(
        [up_grad_b, core_up_other, up_grad_d, core_up_own], [out_keep, tie(core_out, down.sent)]
    )
    grad_a, bias_a, part = attention_back(
        saved_a[:3], first_low, tokens, tie(grad_first, up.sent), pack_a, F32
    )
    core_other = partner(grad_a)
    down.after(grad_a)
    down.third()
    grad_b, bias_b, part = attention_back(
        saved_b, first_low, tokens, tie(part, down.sent), pack_b, F32
    )
    up.after(grad_b)
    up.second()
    down.after(up.sent)
    down.fourth()
    grad_c, bias_c, part = attention_back(
        saved_c, first_low, tokens, tie(part, down.sent, core_other), pack_c, F32
    )
    core_own = partner(grad_c)
    down.after(grad_c)
    down.fifth()
    up.after(down.sent)
    up.third()
    grad_d, bias_d, grad_tokens = attention_back(
        saved_d, first_low, tokens, tie(part, up.sent), pack_d, BF
    )
    attn.first([grad_b, core_other, grad_d, tie(core_own, grad_d, up.got, down.got)])
    vectors = Vectors(
        bias_a, bias_b, bias_c, bias_d, bias_up_a, bias_up_b, bias_up_c, bias_up_d,
        small_second, tie(small_first, attn.sent),
    )
    down.after(attn.sent)
    down.sixth()
    up.after(down.sent)
    up.fourth()

    attn.after(up.sent)
    attn.second()
    up.after(attn.sent)
    up.fifth()
    down.after(up.sent)
    down.seventh()
    vectors.after(down.sent)
    vectors.across()

    attn.after(vectors.sent)
    attn.third()
    up.after(attn.sent)
    up.sixth()
    vectors.after(up.sent)
    vectors.along(1)

    attn.after(vectors.sent)
    attn.fourth()
    vectors.after(attn.sent)
    vectors.along(2)

    attn.after(vectors.sent)
    attn.fifth()
    up.after(attn.sent)
    up.seventh()
    vectors.after(up.sent)
    vectors.along(4)

    attn.after(vectors.sent)
    attn.sixth()
    down.after(attn.sent)
    (grad_w_down,) = down.result((width,))
    vectors.after(grad_w_down)
    keep = vectors.result()

    attn.after(keep)
    attn.seventh()
    up.after(attn.sent)
    grad_w_up, grad_o = up.result((width, local))
    attn.after(grad_o)
    grad_q, grad_k, grad_v = attn.result((local,) * 3)

    return (
        layer_out,
        grad_tokens,
        grad_q.T,
        grad_k.T,
        grad_v.T,
        keep[0, :local],
        keep[0, 2 * local : 3 * local],
        grad_o,
        keep[11],
        keep[12],
        keep[13],
        grad_w_up,
        keep[1],
        grad_w_down,
        keep[8],
        keep[9],
        keep[10],
    )


def solution(mesh):
    rows = P(("dp", "tensor"), None)
    col, row, vec, rep = P(None, "tensor"), P("tensor", None), P("tensor"), P()
    return jax.shard_map(
        on_device,
        mesh=mesh,
        in_specs=(
            rows, col, col, col, vec, vec, row, rep, rep, rep, col, vec, row, rep, rep, rep, rows,
        ),
        out_specs=(
            rows, rows, col, col, col, vec, vec, row, rep, rep, rep, col, vec, row, rep, rep, rep,
        ),
        check_vma=False,
    )
```

```python
import functools

import jax
import jax.numpy as jnp
from jax import lax
from jax.experimental import pallas as pl
from jax.experimental.pallas import tpu as pltpu
from jax.sharding import PartitionSpec as P

HEAD = 64
SEQ_LEN = 512
BIAS_ROWS = 16
BF = jnp.bfloat16
F32 = jnp.float32
ANY = pl.BlockSpec(memory_space=pl.ANY)
VMEM_BYTES = 26 << 20
BY_B, BY_A, NATURAL, FIRST, SECOND, THIRD, FOURTH, PLACES, SIDE, QUARTERS, SHARD = 0, 4, 8, 12, 16, 18, 22, 24, 28, 29, 33
ALL_VMEM_BYTES = 60 << 20
UNROLL = 1


def dot(left, right, left_dim, right_dim):
    return lax.dot_general(
        left, right, (((left_dim,), (right_dim,)), ((), ())), preferred_element_type=F32
    )


SMALL = pl.CostEstimate(flops=1000, bytes_accessed=1000, transcendentals=0)


def whole(shape):
    return pl.BlockSpec(shape, lambda *_: (0,) * len(shape))


def params(limit=VMEM_BYTES):
    return pltpu.CompilerParams(vmem_limit_bytes=limit)


def cost(flops, moved):
    return pl.CostEstimate(flops=int(20 * flops), bytes_accessed=int(20 * moved), transcendentals=0)


def run(kernel, name, outs, *ops, scratch=(), estimate=SMALL, plan=None):
    specs = [pl.BlockSpec(memory_space=pltpu.VMEM)] * len(ops)
    if plan is not None:
        ops = (plan, *ops)
        specs.insert(0, pl.BlockSpec(memory_space=pltpu.SMEM))
    return pl.pallas_call(
        kernel,
        in_specs=specs,
        out_specs=[pl.BlockSpec(memory_space=pltpu.VMEM)] * len(outs),
        out_shape=[jax.ShapeDtypeStruct(shape, dtype) for shape, dtype in outs],
        scratch_shapes=scratch,
        compiler_params=params(),
        cost_estimate=estimate,
        name=name,
    )(*ops)


def pack_kernel(plan, wq, wk, wv, wo, wu, wd, *refs):
    vectors, refs = refs[:9], refs[9:]
    out, near, up_far, down_far, table, packed, piece, lines, *lists, sem = refs
    local, width = wq.shape
    at = pl.multiple_of(plan[BY_B] * local, local)
    copies = [
        pltpu.make_async_copy(ref, packed.at[pl.ds(i * local, local)], sem.at[0])
        for i, ref in enumerate((wq, wk, wv, wo))
    ]
    copies += [
        pltpu.make_async_copy(ref, line, sem.at[0]) for ref, line in zip(vectors, lists)
    ]
    opposite = pl.multiple_of(plan[QUARTERS + 3] * local, local)
    pieces = [
        pltpu.make_async_copy(ref.at[pl.ds(rows, local)], piece.at[i], sem.at[1])
        for i, (ref, rows) in enumerate(((wu, at), (wu, opposite), (wd, at), (wd, opposite)))
    ]
    for copy in copies:
        copy.start()
    for copy in pieces:
        copy.start()
    packed[4 * local :, :] = jnp.zeros((BIAS_ROWS, width), BF)
    lines[...] = jnp.zeros_like(lines)
    for copy in copies:
        copy.wait()
    bq, bv, bu = lists[:3]
    packed[4 * local : 4 * local + 1, 0:local] = bq[...].reshape(1, local)
    packed[4 * local : 4 * local + 1, local : 2 * local] = bv[...].reshape(1, local)
    packed[4 * local + 1 : 4 * local + 2, :] = bu[...].reshape(1, width)
    outs = [
        pltpu.make_async_copy(
            packed.at[pl.ds(at, local)], near.at[pl.ds(0, local)], sem.at[2]
        ),
        pltpu.make_async_copy(
            packed.at[pl.ds(4 * local, BIAS_ROWS)], near.at[pl.ds(local, BIAS_ROWS)], sem.at[2]
        ),
        pltpu.make_async_copy(packed, out, sem.at[2]),
    ]
    for copy in outs:
        copy.start()
    for i, ref in enumerate(lists[3:]):
        lines[i : i + 1, :] = ref[...].astype(F32).reshape(1, width)
    outs.append(pltpu.make_async_copy(lines, table, sem.at[2]))
    outs[-1].start()
    for copy in pieces:
        copy.wait()
    for i, ref in enumerate((up_far, down_far)):
        for h in range(2):
            part = ref.at[pl.ds(h * local, local)]
            outs.append(pltpu.make_async_copy(piece.at[2 * i + h], part, sem.at[2]))
            outs[-1].start()
    for copy in outs:
        copy.wait()


def pack_weights(plan, w_query, w_key, w_value, w_output, w_up, w_down, vectors):
    local, width = w_output.shape
    shapes = [
        jax.ShapeDtypeStruct((4 * local + BIAS_ROWS, width), BF),
        jax.ShapeDtypeStruct((local + BIAS_ROWS, width), BF),
        *[jax.ShapeDtypeStruct((2 * local, width), BF)] * 2,
        jax.ShapeDtypeStruct((8, width), F32),
    ]
    return pl.pallas_call(
        pack_kernel,
        grid_spec=pltpu.PrefetchScalarGridSpec(
            num_scalar_prefetch=1,
            grid=(1,),
            in_specs=[ANY] * 15,
            out_specs=[ANY] * 5,
            scratch_shapes=[
                pltpu.VMEM(shapes[0].shape, BF),
                pltpu.VMEM((4, local, width), BF),
                pltpu.VMEM(shapes[4].shape, F32),
                *[pltpu.VMEM(v.shape, BF) for v in vectors],
                pltpu.SemaphoreType.DMA((3,)),
            ],
        ),
        out_shape=shapes,
        compiler_params=params(ALL_VMEM_BYTES),
        name="pack_weights",
    )(plan, w_query.T, w_key.T, w_value.T, w_output, w_up, w_down, *vectors)


def join_kernel(base, plan, *refs):
    *pieces, out = refs
    at = 0
    rows = pieces[0].shape[0]
    for ref in pieces:
        if at < 4:
            count = ref.shape[0] // rows
            for i in range(count):
                where = pl.multiple_of(plan[base + at + i] * rows, rows)
                copy_rows(out, where, ref, i * rows, rows)
            at += count
        else:
            out[4 * rows :, :] = ref[...]


def normalize(rows):
    center = rows - jnp.mean(rows, axis=-1, keepdims=True)
    scale = lax.rsqrt(jnp.mean(center * center, axis=-1, keepdims=True) + 1e-12)
    return center * scale, scale


def norm_back(grad, unit, scale):
    return scale * (
        grad
        - jnp.mean(grad, axis=-1, keepdims=True)
        - unit * jnp.mean(grad * unit, axis=-1, keepdims=True)
    )


def by_blocks(rows, body, block=64):
    def step(i, carry):
        body(pl.ds(pl.multiple_of(i * block, block), block))
        return carry

    lax.fori_loop(0, rows // block, step, 0)


def by_halves(rows, body):
    def step(i, carry):
        body(pl.ds(pl.multiple_of(i * (rows // 2), 128), rows // 2))
        return carry

    lax.fori_loop(0, 2, step, 0)


def head_rows(head, local, count):
    return [pl.ds(pl.multiple_of(i * local + head * HEAD, HEAD), HEAD) for i in range(count)]


def attention_kernel(first, last, small, *refs):
    tok, weights, *refs = refs
    if not first:
        part_in, *refs = refs
    if last:
        table, *refs = refs
        qkv, probs, att, bias_up, normed, normed_low, unit, scale, bias, part = refs
    else:
        qkv, probs, att, bias_up, part, bias = refs
    local = att.shape[0]
    body = 4 * local
    rows = weights[body : body + BIAS_ROWS, :].astype(F32)
    bias_up[...] = rows[1:2, :]
    column = jnp.transpose(rows)
    bias[...] = jnp.zeros_like(bias)
    bias[0:local, :] = column[0:local, 0:1]
    bias[2 * local : 3 * local, :] = column[local : 2 * local, 0:1]

    def project(i, carry):
        r = pl.ds(pl.multiple_of(i * local, local), local)
        rows = (dot(weights[r, :], tok[...], 1, 1) + bias[r, :]).astype(BF)
        qkv[r, :] = rows * jnp.where(i == 0, 0.125, 1.0).astype(BF)
        return carry

    lax.fori_loop(0, 3, project, 0, unroll=1 if small else 3)

    def one_head(head, carry):
        spans = head_rows(head, local, 3)
        queries, keys, values = (qkv[span, :] for span in spans)
        scores = dot(keys, queries, 0, 0)
        unnorm = jnp.exp(scores - jnp.max(scores, axis=0, keepdims=True))
        prob = (unnorm * (1.0 / jnp.sum(unnorm, axis=0, keepdims=True))).astype(BF)
        probs[head] = prob
        att[spans[0], :] = dot(values, prob, 1, 0).astype(BF)
        return carry

    lax.fori_loop(0, local // HEAD, one_head, 0, unroll=UNROLL)

    def out_rows(r):
        rows = dot(att[:, r], weights[3 * local : 4 * local, :], 0, 0)
        part[r, :] = rows if first else rows + part_in[r, :]

    by_halves(part.shape[0], out_rows)
    if last:

        def block(r):
            total = part[r, :] + table[0:1, :] + tok[r, :].astype(F32)
            unit_rows, scale_rows = normalize(total)
            unit[r, :] = unit_rows
            scale[r, :] = scale_rows
            rows = unit_rows * table[1:2, :] + table[2:3, :]
            normed[r, :] = rows
            normed_low[r, :] = rows.astype(BF)

        by_blocks(tok.shape[0], block)


def attention(tokens, pack, part=None, table=None, small=False):
    rows, width = tokens.shape
    local = (pack.shape[0] - BIAS_ROWS) // 4
    first, last = part is None, table is not None
    ops = [tokens, pack] + [x for x in (part, table) if x is not None]
    outs = [((3 * local, rows), BF), ((local // HEAD, rows, rows), BF), ((local, rows), BF)]
    outs += [((1, width), F32)]
    if last:
        outs += [((rows, width), F32), ((rows, width), BF), ((rows, width), F32), ((rows, 1), F32)]
    else:
        outs += [((rows, width), F32)]
    return run(
        functools.partial(attention_kernel, first, last, small),
        "attention_last" if last else "attention",
        outs,
        *ops,
        scratch=[pltpu.VMEM((3 * local, 1), F32)] + [pltpu.VMEM((rows, width), F32)] * last,
        estimate=cost(2.5e9, 4e6),
    )


def feed_kernel(last, *refs):
    low, up, down, bias, part_in, *refs = refs
    if last:
        table, cot, act, slope, layer_out, down_low, grad_second, small, part = refs
    else:
        act, slope, part = refs
    rows = dot(low[...], up[...], 1, 0) + bias[...]
    cdf = 0.5 * (1.0 + lax.erf(rows * 0.7071067811865476))
    active = (rows * cdf).astype(BF)
    act[...] = active
    slope[...] = (cdf + (rows * 0.3989422804014327) * jnp.exp(-0.5 * rows * rows)).astype(BF)
    part[...] = part_in[...] + dot(active, down[...], 1, 0)
    if last:
        small[...] = jnp.zeros_like(small)

        def block(r):
            unit2, scale2 = normalize(part[r, :] + table[3:4, :])
            layer_out[r, :] = unit2 * table[4:5, :] + table[5:6, :]
            cots = cot[r, :].astype(F32)
            grad = norm_back(cots * table[4:5, :], unit2, scale2)
            grad_second[r, :] = grad
            down_low[r, :] = grad.astype(BF)
            small[0:1, :] += jnp.sum(grad, axis=0, keepdims=True)
            small[1:2, :] += jnp.sum(cots * unit2, axis=0, keepdims=True)
            small[2:3, :] += jnp.sum(cots, axis=0, keepdims=True)

        by_blocks(low.shape[0], block)


def feed(low, up, down, bias, part, extra=None):
    rows, width = low.shape
    hidden = up.shape[1]
    last = extra is not None
    ops = [low, up, down, bias, part, *(extra or [])]
    outs = [((rows, hidden), BF)] * 2
    if last:
        outs += [((rows, width), F32), ((rows, width), BF), ((rows, width), F32), ((8, width), F32)]
    else:
        outs += [((rows, width), F32)]
    return run(
        functools.partial(feed_kernel, last),
        "feed_last" if last else "feed",
        outs,
        *ops,
        scratch=[pltpu.VMEM((rows, width), F32)] if last else [],
        estimate=cost(2.5e9 if last else 1.5e9, 4e6),
    )


def down_grad_kernel(*refs):
    count = len(refs) // 2
    low = refs[count]
    for act, out in zip(refs[:count], refs[count + 1 :]):

        out[...] = dot(act[...], low[...], 0, 0).astype(BF)


def down_grad(acts, low):
    return run(
        down_grad_kernel,
        "down_grad",
        [((acts[0].shape[1], low.shape[1]), BF)] * len(acts),
        *acts,
        low,
        estimate=cost(1.2e9, 4e6),
    )


def feed_back_kernel(last, *refs):
    slope, down_low, normed_low, grad_in, up, down, *refs = refs
    if last:
        unit, scale, table, grads, bias, grad_first, first_low, small, part = refs
    else:
        grads, bias, part = refs
    grad_up = (dot(down_low[...], down[...], 1, 1) * slope[...].astype(F32)).astype(BF)
    bias[...] = jnp.sum(grad_up.astype(F32), axis=0, keepdims=True)

    def grad_rows(r):
        grads[r, :] = dot(normed_low[:, r], grad_up, 0, 0).astype(BF)

    by_halves(grads.shape[0], grad_rows)
    part[...] = grad_in[...] + dot(grad_up, up[...], 1, 1)
    if last:
        small[...] = jnp.zeros_like(small)

        def block(r):
            grad = part[r, :]
            units = unit[r, :]
            first = norm_back(grad * table[1:2, :], units, scale[r, :])
            grad_first[r, :] = first
            first_low[r, :] = first.astype(BF)
            small[0:1, :] += jnp.sum(first, axis=0, keepdims=True)
            small[1:2, :] += jnp.sum(grad * units, axis=0, keepdims=True)
            small[2:3, :] += jnp.sum(grad, axis=0, keepdims=True)

        by_blocks(part.shape[0], block)


def feed_back(slope, down_low, normed_low, grad_in, up, down, extra=None):
    rows, width = down_low.shape
    hidden = up.shape[1]
    last = extra is not None
    outs = [((width, hidden), BF), ((1, hidden), F32), ((rows, width), F32)]
    if last:
        outs += [((rows, width), BF), ((8, width), F32)]
    return run(
        functools.partial(feed_back_kernel, last),
        "feed_back_last" if last else "feed_back",
        outs,
        slope,
        down_low,
        normed_low,
        grad_in,
        up,
        down,
        *(extra or []),
        scratch=[pltpu.VMEM((rows, width), F32)] if last else [],
        estimate=cost(2.5e9 if last else 2e9, 5e6),
    )


def attention_back_kernel(qkv, probs, first_low, tok, grad_in, weights, grads, bias, out, work):
    local = qkv.shape[0] // 3
    work[3 * local :, :] = dot(weights[3 * local : 4 * local, :], first_low[...], 1, 1).astype(BF)

    def one_head(head, carry):
        spans = head_rows(head, local, 4)
        queries, keys, values = (qkv[span, :] for span in spans[:3])
        grad_att = work[spans[3], :]
        prob = probs[head]
        grad_prob = dot(values, grad_att, 0, 0)
        wide = prob.astype(F32)
        inner = jnp.sum(wide * grad_prob, axis=0, keepdims=True)
        grad_score = (wide * (grad_prob - inner)).astype(BF)
        work[spans[0], :] = (dot(keys, grad_score, 1, 0) * 0.125).astype(BF)
        work[spans[1], :] = dot(queries, grad_score, 1, 1).astype(BF)
        work[spans[2], :] = dot(grad_att, prob, 1, 1).astype(BF)
        return carry

    lax.fori_loop(0, local // HEAD, one_head, 0, unroll=UNROLL)
    joined = work[0 : 3 * local, :]

    def grad_rows(i, carry):
        r = pl.ds(pl.multiple_of(i * local, local), local)
        grads[r, :] = dot(work[r, :], tok[...], 1, 0).astype(BF)
        return carry

    lax.fori_loop(0, 3, grad_rows, 0)
    bias[...] = dot(jnp.ones((8, joined.shape[1]), BF), joined, 1, 1)

    def out_rows(r):
        out[r, :] = grad_in[r, :] + dot(work[0 : 3 * local, r], weights[0 : 3 * local, :], 0, 0)

    by_halves(out.shape[0], out_rows)


def attention_back(saved, first_low, tokens, grad_in, pack):
    qkv, probs, _ = saved
    rows, width = tokens.shape
    joined = qkv.shape[0]
    return run(
        attention_back_kernel,
        "attention_back",
        [((joined, width), BF), ((8, joined), F32), ((rows, width), F32)],
        qkv,
        probs,
        first_low,
        tokens,
        grad_in,
        pack,
        scratch=[pltpu.VMEM((joined // 3 * 4, rows), BF)],
        estimate=cost(3.5e9, 6e6),
    )


def out_grad_kernel(a, b, c, d, low, send, keep):
    for ref, both in ((send, (a, c)), (keep, (b, d))):
        for i, att in enumerate(both):
            ref[i] = dot(att[...], low[...], 1, 0).astype(BF)


def out_grad(atts, low):
    shape = (2, atts[0].shape[0], low.shape[1])
    return run(
        out_grad_kernel, "out_grad", [(shape, BF)] * 2, *atts, low, estimate=cost(6e8, 3e6)
    )


def join(plan, base, *pieces):
    rows = sum(p.shape[0] for p in pieces)
    (out,) = run(
        functools.partial(join_kernel, base), "join", [((rows, pieces[0].shape[1]), BF)], *pieces,
        plan=plan,
    )
    return out


def add_rows(target, to, left, right, at, rows):
    block = next(b for b in (96, 64, 48, 32, 8) if rows % b == 0)

    def body(i, carry):
        here = pl.ds(pl.multiple_of(at + i * block, 8), block)
        there = pl.ds(pl.multiple_of(to + i * block, 8), block)
        total = left[here, :].astype(F32) + right[here, :].astype(F32)
        target[there, :] = total.astype(target.dtype)
        return carry

    lax.fori_loop(0, rows // block, body, 0)


def copy_rows(target, to, source, at, rows):
    block = next(b for b in (48, 40, 32, 24, 8) if rows % b == 0)

    def body(i, carry):
        here = pl.ds(pl.multiple_of(at + i * block, 8), block)
        there = pl.ds(pl.multiple_of(to + i * block, 8), block)
        target[there, :] = source[here, :].astype(target.dtype)
        return carry

    lax.fori_loop(0, rows // block, body, 0)


VECTORS = 16


def send_vectors(value, sent):
    high = value.astype(BF)
    low = (value - high.astype(F32)).astype(BF)
    at = sent.shape[0] - 2 * VECTORS
    sent[at : at + VECTORS, :] = high
    sent[at + VECTORS :, :] = low
    return high.astype(F32) + low.astype(F32)


def got_vectors(got):
    at = got.shape[0] - 2 * VECTORS
    return got[at : at + VECTORS, :].astype(F32) + got[at + VECTORS :, :].astype(F32)


def collect(plan, attn, up, second, first, rows):
    span = attn[0].shape[1]
    rows[...] = jnp.zeros_like(rows)
    for shard in range(4):
        wide, narrow = jnp.zeros((1, rows.shape[1]), F32), jnp.zeros((1, span), F32)
        for apart in range(4):
            here = plan[SHARD] == shard ^ apart
            narrow = jnp.where(here, attn[apart][0:1, :], narrow)
            wide = jnp.where(here, up[apart][...], wide)
        rows[shard : shard + 1, 0:span] = narrow
        rows[4 + shard : 5 + shard, :] = wide
    rows[8:11, :] = second[0:3, :]
    rows[11:14, :] = first[0:3, :]


def choose(total, plan, base, count, sent, keep):
    rows = keep.shape[0] // count
    for i in range(count):
        for ref, at in ((sent, base + i), (keep, base + count + i)):
            copy_rows(ref, i * rows, total, pl.multiple_of(plan[at] * rows, rows), rows)


def first_kernel(segments, vectors, plan, *refs):
    if vectors:
        *ops, sent, keep, kept_vectors, rows = refs
        parts = ops[-10:]
        collect(plan, parts[:4], parts[4:8], parts[8], parts[9], rows)
        kept_vectors[...] = send_vectors(rows[...], sent)
    else:
        *ops, sent, keep = refs
    half = keep.shape[0] // 2
    for slot in range(4):
        target = (sent, keep)[slot // 2]
        for block in ((0, 1), (1, 2, 3), (0, 1, 2), (2, 3))[slot]:

            @pl.when(plan[FIRST + slot] == block)
            def _(slot=slot, block=block, target=target):
                begin, end = (block % 2) * half, (block % 2 + 1) * half
                at = 0
                for left, right, size in segments[block // 2]:
                    low, high = max(begin, at), min(end, at + size)
                    if low < high:
                        to = (slot % 2) * half + low - begin
                        add_rows(target, to, ops[left[0]].at[left[1]], ops[right[0]].at[right[1]], low - at, high - low)
                    at += size


def first_stage(plan, parts, stacked, vectors):
    width = parts[0].shape[-1]
    size = parts[0].shape[0]
    ops = [p[None] for p in parts] + list(stacked)
    segments = [[((0, 0), (1, 0), size)], [((2, 0), (3, 0), size)]]
    rows = size
    if stacked:
        rows += stacked[0].shape[1]
        for i in range(2):
            segments[i].append(((4, i), (5, i), rows - size))
    outs = [((rows, width), BF), ((rows, width), F32)]
    if vectors:
        outs = [((rows + 2 * VECTORS, width), BF), outs[1], ((VECTORS, width), F32)]
    return run(
        functools.partial(first_kernel, segments, bool(vectors)),
        "first_stage",
        outs,
        *ops,
        *vectors,
        scratch=[pltpu.VMEM((VECTORS, width), F32)] if vectors else [],
        plan=plan,
    )


def next_kernel(base, count, plan, kept, got, *refs):
    rows = kept.shape[0]
    if len(refs) > 3:
        had, sent, keep, has, total = refs
        has[...] = send_vectors(had[...] + got_vectors(got), sent)
    else:
        sent, keep, total = refs
    total[...] = kept[...] + got[0:rows, :].astype(F32)
    choose(total, plan, base, count, sent, keep)


def next_stage(plan, base, count, kept, got, vectors=()):
    rows, width = kept.shape
    outs = [((rows // 2, width), BF), ((rows // 2, width), F32)]
    if vectors:
        outs = [((rows // 2 + 2 * VECTORS, width), BF), outs[1], ((VECTORS, width), F32)]
    return run(
        functools.partial(next_kernel, base, count),
        "next_stage",
        outs,
        kept,
        got,
        *vectors,
        scratch=[pltpu.VMEM((rows, width), F32)],
        plan=plan,
    )


def finish_kernel(sizes, plan, mine, theirs, *refs):
    outs, (sums, sem) = refs[:-2], refs[-2:]
    rows = mine.shape[0] // 4
    for h in range(2):
        for i in range(4):
            where = pl.ds(pl.multiple_of(plan[PLACES + i] * rows, rows), rows)
            at = (4 * h + i) * rows
            sums[at : at + rows, :] = jnp.where(
                plan[SIDE] == h, mine[where, :], theirs[where, :]
            ).astype(F32)
    copies, at = [], 0
    for ref, size in zip(outs, sizes):
        copies.append(pltpu.make_async_copy(sums.at[pl.ds(at, size)], ref, sem))
        copies[-1].start()
        at += size
    for copy in copies:
        copy.wait()


def finish(plan, mine, theirs, sizes):
    half, width = mine.shape
    return pl.pallas_call(
        functools.partial(finish_kernel, sizes),
        grid_spec=pltpu.PrefetchScalarGridSpec(
            num_scalar_prefetch=1,
            grid=(1,),
            in_specs=[whole((half, width))] * 2,
            out_specs=[ANY] * len(sizes),
            scratch_shapes=[pltpu.VMEM((2 * half, width), F32), pltpu.SemaphoreType.DMA(())],
        ),
        out_shape=[jax.ShapeDtypeStruct((size, width), F32) for size in sizes],
        compiler_params=params(),
        cost_estimate=SMALL,
        name="finish",
    )(plan, mine, theirs)


Y, X, Z_NEAR, Z_FAR = ("tensor", 2), ("dp", 1), ("dp", 2), ("dp", 4)


def tie(value, *others):
    return lax.optimization_barrier((value, others))[0]


def swap(value, even, odd=None):
    groups, width = lax.axis_size("dp"), lax.axis_size("tensor")
    pairs = []
    for group in range(groups):
        for t in range(width):
            axis, bit = even if odd is None or t % 2 == 0 else odd
            to = (group ^ bit, t) if axis == "dp" else (group, t ^ bit)
            pairs.append((group * width + t, to[0] * width + to[1]))
    return lax.ppermute(value, ("dp", "tensor"), pairs)


def partner(value):
    return swap(value, ("tensor", 1))


def make_plan():
    index, t = lax.axis_index("dp"), lax.axis_index("tensor")
    x, near, far, core = index % 2, index // 2 % 2, index // 4 % 2, t % 2
    quarter, place = x + 2 * near, near + 2 * far
    even = [quarter, quarter ^ 1, quarter ^ 2, quarter ^ 3]
    odd = [quarter, quarter ^ 2, quarter ^ 1, quarter ^ 3]
    even += odd + [0, 1, 2, 3]
    odd += even[:4] + [0, 1, 2, 3]
    even += [0, 1, 2, 3]
    odd += [1 - x, 3 - x, x, 2 + x]
    even += [1 - x, x]
    odd += [0, 1]
    even += [1 - near, 3 - near, near, 2 + near]
    odd += [2 - 2 * far, 3 - 2 * far, 2 * far, 2 * far + 1]
    even += [1 - far, far]
    odd += [1 - near, near]
    apart = [i ^ place for i in range(4)]
    even += [i // 2 + 2 * (i % 2) for i in apart]
    odd += apart
    quarters = [quarter ^ i for i in range(4)]
    even += [x, *quarters, t]
    odd += [x, *quarters, t]
    both = [jnp.stack([jnp.asarray(i, jnp.int32) for i in plan]) for plan in (even, odd)]
    return jnp.where(core == 0, *both)


class Gather:
    def __init__(self, plan, sent, tail=0):
        self.plan, self.tail = plan, tail
        self.got = swap(sent, Y)

    def after(self, *values):
        self.got = tie(self.got, *values)

    @classmethod
    def of_two(cls, plan, sent):
        return cls(plan, sent)

    def both(self):
        rows = self.got.shape[0] // 2
        self.held, self.far = self.got[:rows], self.got[rows:]
        self.got = [swap(self.held, X), swap(self.held, Z_NEAR)]

    def joined(self):
        return join(self.plan, QUARTERS, self.held, *self.got, self.far)

    def second(self):
        rows = self.got.shape[0] - self.tail
        self.rest = [self.got[rows:]] if self.tail else []
        self.held = self.got[:rows]
        self.got = swap(self.held, X, Z_NEAR)

    def third(self):
        self.held = jnp.concatenate([self.held, self.got], axis=0)
        self.got = swap(self.held, Z_NEAR, X)

    def result(self):
        rows = self.held.shape[0] // 2
        return join(
            self.plan, BY_B, self.held[:rows], self.held[rows:], self.got[:rows], self.got[rows:], *self.rest
        )


class Reduction:
    def __init__(self, plan):
        self.plan = plan

    def after(self, *values):
        self.got = tie(self.got, *values)

    def first(self, parts, stacked=(), vectors=()):
        self.sent, self.keep, *self.vectors = first_stage(self.plan, parts, stacked, vectors)
        self.got = swap(self.sent, Y, X)

    def next(self, base, count):
        self.sent, self.keep, *self.vectors = next_stage(
            self.plan, base, count, self.keep, self.got, self.vectors
        )

    def second(self):
        self.next(SECOND, 1)
        self.got = swap(self.sent, X, Y)

    def third(self):
        self.next(THIRD, 2)
        self.got = swap(self.sent, Z_NEAR, Z_FAR)

    def fourth(self):
        self.next(FOURTH, 1)
        self.got = swap(self.sent, Z_FAR, Z_NEAR)

    def fifth(self):
        rows = self.keep.shape[0]
        total = (self.keep + self.got[:rows].astype(F32)).astype(BF)
        if self.vectors:
            high, low = self.got[rows : rows + VECTORS], self.got[rows + VECTORS :]
            self.vectors = [self.vectors[0] + (high.astype(F32) + low.astype(F32))]
        bit = 8
        while bit < lax.axis_size("dp"):
            total = (total.astype(F32) + swap(total, ("dp", bit)).astype(F32)).astype(BF)
            self.vectors = [v + swap(v, ("dp", bit)) for v in self.vectors]
            bit *= 2
        self.sent = total
        self.got = swap(self.sent, Z_FAR, Z_NEAR)

    def sixth(self):
        self.sent = jnp.concatenate([self.sent, self.got], axis=0)
        self.got = swap(self.sent, Z_NEAR, Z_FAR)

    def seventh(self):
        self.sent = jnp.concatenate([self.sent, self.got], axis=0)
        self.got = swap(self.sent, X)

    def result(self, sizes):
        return finish(self.plan, self.sent, self.got, sizes)


def on_device(
    tokens,
    w_query,
    w_key,
    w_value,
    b_query,
    b_value,
    w_output,
    b_output,
    first_gain,
    first_shift,
    w_up,
    b_up,
    w_down,
    b_down,
    second_gain,
    second_shift,
    cotangent,
):
    rows, width = tokens.shape
    local = w_query.shape[1]
    assert rows == SEQ_LEN and width == 4 * local and w_up.shape == (width, width)
    plan = make_plan()
    pack_d, near, up_far, down_far, table = pack_weights(
        plan, w_query, w_key, w_value, w_output, w_up, w_down,
        (b_query, b_value, b_up, b_output, first_gain, first_shift, b_down, second_gain,
         second_shift),
    )

    far_pack = Gather(plan, near, BIAS_ROWS)
    up = Gather.of_two(plan, tie(up_far, near))
    pack_c = partner(tie(pack_d, near))
    down = Gather.of_two(plan, tie(down_far, far_pack.got))
    far_pack.second()
    *saved_d, bias_d, part = attention(tie(tokens, far_pack.held), pack_d, small=True)
    far_pack.after(part)
    far_pack.third()
    *saved_c, bias_c, part = attention(tokens, pack_c, tie(part, far_pack.held), small=True)
    far_pack.after(part)
    pack_b = far_pack.result()
    up.after(pack_b)
    up.both()
    pack_a = partner(pack_b)
    up_d, down_d = w_up, w_down
    up_c = partner(tie(w_up, pack_b))
    *saved_b, bias_b, part = attention(tokens, pack_b, tie(part, up.held))
    down.after(part)
    down.both()
    down_c = partner(tie(w_down, down.held))
    *saved_a, bias_a, normed, normed_low, unit, scale = attention(
        tokens, pack_a, tie(part, down.held), table
    )
    up.got, up.far = tie((up.got, up.far), normed)
    up_b = up.joined()
    up_a = partner(up_b)
    act_d, slope_d, part = feed(normed_low, up_d, down_d, bias_d, tie(normed, up_b))
    act_c, slope_c, part = feed(normed_low, up_c, down_c, bias_c, part)
    down.got, down.far = tie((down.got, down.far), part)
    down_b = down.joined()
    down_a = partner(down_b)
    act_b, slope_b, part = feed(normed_low, up_b, down_b, bias_b, part)
    act_a, slope_a, layer_out, down_low, grad_second, small_second = feed(
        normed_low, up_a, down_a, bias_a, part, [table, cotangent]
    )

    down, up, attn = Reduction(plan), Reduction(plan), Reduction(plan)
    grad_a, grad_b = down_grad([act_a, act_b], down_low)
    core_other = partner(grad_a)
    grad_c, grad_d = down_grad([act_c, act_d], tie(down_low, grad_a))
    core_own = partner(grad_c)
    up_grad_a, bias_up_a, part = feed_back(
        slope_a, down_low, normed_low, tie(grad_second, grad_c), up_a, down_a
    )
    core_up_other = partner(up_grad_a)
    down.first([grad_b, *tie((core_other,), up_grad_a), grad_d, core_own])
    up_grad_b, bias_up_b, part = feed_back(
        slope_b, down_low, normed_low, tie(part, down.sent), up_b, down_b
    )
    up_grad_c, bias_up_c, part = feed_back(
        slope_c, down_low, normed_low, tie(part, core_up_other), up_c, down_c
    )
    core_up_own = partner(up_grad_c)
    up_grad_d, bias_up_d, grad_first, first_low, small_first = feed_back(
        slope_d, down_low, normed_low, part, up_d, down_d, [unit, scale, table]
    )
    out_send, out_keep = out_grad([s[2] for s in (saved_a, saved_b, saved_c, saved_d)], first_low)
    core_out = partner(out_send)
    down.after(out_keep)
    down.second()
    grad_a, bias_a, part = attention_back(
        saved_a[:3], first_low, tokens, tie(grad_first, down.sent), pack_a
    )
    core_other = partner(grad_a)
    up.first([up_grad_b, core_up_other, up_grad_d, core_up_own], [out_keep, tie(core_out, grad_a)])
    down.after(up.sent)
    down.third()
    grad_b, bias_b, part = attention_back(
        saved_b, first_low, tokens, tie(part, down.sent), pack_b
    )
    grad_c, bias_c, part = attention_back(
        saved_c, first_low, tokens, tie(part, core_other), pack_c
    )
    core_own = partner(grad_c)
    down.after(grad_c)
    down.fourth()
    up.after(down.sent)
    up.second()
    grad_d, bias_d, grad_tokens = attention_back(
        saved_d, first_low, tokens, tie(part, up.sent), pack_d
    )
    down.after(grad_tokens)
    down.fifth()
    attn.first(
        [grad_b, core_other, grad_d, tie(core_own, down.sent, up.got)],
        vectors=[
            bias_d, bias_c, bias_b, bias_a, bias_up_d, bias_up_c, bias_up_b, bias_up_a,
            small_second, small_first,
        ],
    )

    up.after(attn.sent)
    up.third()
    down.after(up.sent)
    down.sixth()

    attn.after(down.sent)
    attn.second()
    up.after(attn.sent)
    up.fourth()
    down.after(up.sent)
    down.seventh()

    attn.after(down.sent)
    attn.third()
    up.after(attn.sent)
    up.fifth()

    attn.after(up.sent)
    attn.fourth()
    up.after(attn.sent)
    up.sixth()
    down.after(up.sent)
    (grad_w_down,) = down.result((width,))

    attn.after(grad_w_down)
    attn.fifth()
    (sums,) = attn.vectors
    others = partner(sums)
    up.after(attn.sent)
    up.seventh()

    attn.after(up.sent)
    attn.sixth()
    sums = sums + tie(others, attn.sent)
    shard = lax.axis_index("tensor")
    attn_vectors = lax.dynamic_index_in_dim(sums, shard, 0, keepdims=False)
    up_vector = lax.dynamic_index_in_dim(sums, 4 + shard, 0, keepdims=False)

    attn.after(attn_vectors, up_vector)
    attn.seventh()
    up.after(attn.sent)
    grad_w_up, grad_o = up.result((width, local))
    attn.after(grad_o)
    grad_q, grad_k, grad_v = attn.result((local,) * 3)

    return (
        tie(layer_out, attn.got).astype(BF),
        grad_tokens.astype(BF),
        grad_q.T,
        grad_k.T,
        grad_v.T,
        attn_vectors[:local],
        attn_vectors[2 * local : 3 * local],
        grad_o,
        sums[11],
        sums[12],
        sums[13],
        grad_w_up,
        up_vector,
        grad_w_down,
        sums[8],
        sums[9],
        sums[10],
    )


def solution(mesh):
    rows = P(("dp", "tensor"), None)
    col, row, vec, rep = P(None, "tensor"), P("tensor", None), P("tensor"), P()
    return jax.shard_map(
        on_device,
        mesh=mesh,
        in_specs=(
            rows, col, col, col, vec, vec, row, rep, rep, rep, col, vec, row, rep, rep, rep, rows,
        ),
        out_specs=(
            rows, rows, col, col, col, vec, vec, row, rep, rep, rep, col, vec, row, rep, rep, rep,
        ),
        check_vma=False,
    )
```

```python
import functools

import jax
import jax.numpy as jnp
from jax import lax
from jax.experimental import pallas as pl
from jax.experimental.pallas import tpu as pltpu
from jax.sharding import PartitionSpec as P

HEAD = 64
SEQ_LEN = 512
BIAS_ROWS = 16
BF = jnp.bfloat16
F32 = jnp.float32
ANY = pl.BlockSpec(memory_space=pl.ANY)
VMEM_BYTES = 26 << 20
BY_B, BY_A, NATURAL, FIRST, SECOND, THIRD, FOURTH, PLACES, SIDE, QUARTERS, SHARD = 0, 4, 8, 12, 16, 18, 22, 24, 28, 29, 33
ALL_VMEM_BYTES = 60 << 20
UNROLL = 1


def dot(left, right, left_dim, right_dim):
    return lax.dot_general(
        left, right, (((left_dim,), (right_dim,)), ((), ())), preferred_element_type=F32
    )


SMALL = pl.CostEstimate(flops=1000, bytes_accessed=1000, transcendentals=0)


def whole(shape):
    return pl.BlockSpec(shape, lambda *_: (0,) * len(shape))


def params(limit=VMEM_BYTES):
    return pltpu.CompilerParams(vmem_limit_bytes=limit)


def cost(flops, moved):
    return pl.CostEstimate(flops=int(20 * flops), bytes_accessed=int(20 * moved), transcendentals=0)


def run(kernel, name, outs, *ops, scratch=(), estimate=SMALL, plan=None):
    specs = [pl.BlockSpec(memory_space=pltpu.VMEM)] * len(ops)
    if plan is not None:
        ops = (plan, *ops)
        specs.insert(0, pl.BlockSpec(memory_space=pltpu.SMEM))
    return pl.pallas_call(
        kernel,
        in_specs=specs,
        out_specs=[pl.BlockSpec(memory_space=pltpu.VMEM)] * len(outs),
        out_shape=[jax.ShapeDtypeStruct(shape, dtype) for shape, dtype in outs],
        scratch_shapes=scratch,
        compiler_params=params(),
        cost_estimate=estimate,
        name=name,
    )(*ops)


def near_kernel(plan, wq, wk, wv, wo, bq, bv, bu, out, *lines):
    sem = lines[-1]
    local, width = wq.shape
    for i, ref in enumerate((wq, wk, wv, wo)):

        @pl.when(plan[BY_B] == i)
        def _(ref=ref):
            pltpu.make_async_copy(ref, out.at[pl.ds(0, local)], sem.at[0]).start()

    copies = [
        pltpu.make_async_copy(ref, line, sem.at[1]) for ref, line in zip((bq, bv, bu), lines)
    ]
    for copy in copies:
        copy.start()
    out[local:, :] = jnp.zeros((BIAS_ROWS, width), BF)
    for copy in copies:
        copy.wait()
    q, v, u = lines[:3]
    out[local : local + 1, 0:local] = q[...].reshape(1, local)
    out[local : local + 1, local : 2 * local] = v[...].reshape(1, local)
    out[local + 1 : local + 2, :] = u[...].reshape(1, width)
    pltpu.make_async_copy(wq, out.at[pl.ds(0, local)], sem.at[0]).wait()


def pack_near(plan, w_query, w_key, w_value, w_output, biases):
    local, width = w_output.shape
    (out,) = pl.pallas_call(
        near_kernel,
        in_specs=[pl.BlockSpec(memory_space=pltpu.SMEM)] + [ANY] * 7,
        out_specs=[pl.BlockSpec(memory_space=pltpu.VMEM)],
        out_shape=[jax.ShapeDtypeStruct((local + BIAS_ROWS, width), BF)],
        scratch_shapes=[
            *[pltpu.VMEM(v.shape, BF) for v in biases],
            pltpu.SemaphoreType.DMA((2,)),
        ],
        compiler_params=params(ALL_VMEM_BYTES),
        name="pack_near",
    )(plan, w_query.T, w_key.T, w_value.T, w_output, *biases)
    return out


def pack_kernel(plan, wq, wk, wv, wo, wu, wd, near, *refs):
    vectors, refs = refs[:6], refs[6:]
    out, up_far, down_far, table, packed, piece, lines, *lists, sem = refs
    local, width = wq.shape
    at = pl.multiple_of(plan[BY_B] * local, local)
    opposite = pl.multiple_of(plan[QUARTERS + 3] * local, local)
    pieces = [
        pltpu.make_async_copy(ref.at[pl.ds(rows, local)], piece.at[i], sem.at[1])
        for i, (ref, rows) in enumerate(((wu, at), (wu, opposite), (wd, at), (wd, opposite)))
    ]
    copies = [
        pltpu.make_async_copy(ref, packed.at[pl.ds(i * local, local)], sem.at[0])
        for i, ref in enumerate((wq, wk, wv, wo))
    ]
    copies.append(
        pltpu.make_async_copy(
            near.at[pl.ds(local, BIAS_ROWS)], packed.at[pl.ds(4 * local, BIAS_ROWS)], sem.at[0]
        )
    )
    copies += [
        pltpu.make_async_copy(ref, line, sem.at[0]) for ref, line in zip(vectors, lists)
    ]
    for copy in pieces:
        copy.start()
    for copy in copies:
        copy.start()
    lines[...] = jnp.zeros_like(lines)
    outs = []
    for copy in pieces:
        copy.wait()
    for i, ref in enumerate((up_far, down_far)):
        for h in range(2):
            part = ref.at[pl.ds(h * local, local)]
            outs.append(pltpu.make_async_copy(piece.at[2 * i + h], part, sem.at[2]))
            outs[-1].start()
    for copy in copies:
        copy.wait()
    outs.append(pltpu.make_async_copy(packed, out, sem.at[2]))
    outs[-1].start()
    for i, ref in enumerate(lists):
        lines[i : i + 1, :] = ref[...].astype(F32).reshape(1, width)
    outs.append(pltpu.make_async_copy(lines, table, sem.at[2]))
    outs[-1].start()
    for copy in outs:
        copy.wait()


def pack_weights(plan, w_query, w_key, w_value, w_output, w_up, w_down, near, vectors):
    local, width = w_output.shape
    shapes = [
        jax.ShapeDtypeStruct((4 * local + BIAS_ROWS, width), BF),
        *[jax.ShapeDtypeStruct((2 * local, width), BF)] * 2,
        jax.ShapeDtypeStruct((8, width), F32),
    ]
    return pl.pallas_call(
        pack_kernel,
        grid_spec=pltpu.PrefetchScalarGridSpec(
            num_scalar_prefetch=1,
            grid=(1,),
            in_specs=[ANY] * 13,
            out_specs=[ANY] * 4,
            scratch_shapes=[
                pltpu.VMEM(shapes[0].shape, BF),
                pltpu.VMEM((4, local, width), BF),
                pltpu.VMEM(shapes[3].shape, F32),
                *[pltpu.VMEM(v.shape, BF) for v in vectors],
                pltpu.SemaphoreType.DMA((3,)),
            ],
        ),
        out_shape=shapes,
        compiler_params=params(ALL_VMEM_BYTES),
        name="pack_weights",
    )(plan, w_query.T, w_key.T, w_value.T, w_output, w_up, w_down, near, *vectors)


def join_kernel(base, plan, *refs):
    *pieces, out = refs
    at = 0
    rows = pieces[0].shape[0]
    for ref in pieces:
        if at < 4:
            count = ref.shape[0] // rows
            for i in range(count):
                where = pl.multiple_of(plan[base + at + i] * rows, rows)
                copy_rows(out, where, ref, i * rows, rows)
            at += count
        else:
            out[4 * rows :, :] = ref[...]


def normalize(rows):
    center = rows - jnp.mean(rows, axis=-1, keepdims=True)
    scale = lax.rsqrt(jnp.mean(center * center, axis=-1, keepdims=True) + 1e-12)
    return center * scale, scale


def norm_back(grad, unit, scale):
    return scale * (
        grad
        - jnp.mean(grad, axis=-1, keepdims=True)
        - unit * jnp.mean(grad * unit, axis=-1, keepdims=True)
    )


def by_blocks(rows, body, block=128):
    def step(i, carry):
        body(pl.ds(pl.multiple_of(i * block, block), block))
        return carry

    lax.fori_loop(0, rows // block, step, 0)


def by_halves(rows, body):
    def step(i, carry):
        body(pl.ds(pl.multiple_of(i * (rows // 2), 128), rows // 2))
        return carry

    lax.fori_loop(0, 2, step, 0)


def head_rows(head, local, count):
    return [pl.ds(pl.multiple_of(i * local + head * HEAD, HEAD), HEAD) for i in range(count)]


def attention_kernel(first, last, small, *refs):
    tok, weights, *refs = refs
    if not first:
        part_in, *refs = refs
    if last:
        table, *refs = refs
        qkv, probs, att, bias_up, normed, normed_low, unit, scale, bias, part = refs
    else:
        qkv, probs, att, bias_up, part, bias = refs
    local = att.shape[0]
    body = 4 * local
    rows = weights[body : body + BIAS_ROWS, :].astype(F32)
    bias_up[...] = rows[1:2, :]
    column = jnp.transpose(rows)
    bias[...] = jnp.zeros_like(bias)
    bias[0:local, :] = column[0:local, 0:1]
    bias[2 * local : 3 * local, :] = column[local : 2 * local, 0:1]

    def project(i, carry):
        r = pl.ds(pl.multiple_of(i * local, local), local)
        rows = (dot(weights[r, :], tok[...], 1, 1) + bias[r, :]).astype(BF)
        qkv[r, :] = rows * jnp.where(i == 0, 0.125, 1.0).astype(BF)
        return carry

    lax.fori_loop(0, 3, project, 0, unroll=1 if small else 3)

    def one_head(head, carry):
        spans = head_rows(head, local, 3)
        queries, keys, values = (qkv[span, :] for span in spans)
        scores = dot(keys, queries, 0, 0)
        unnorm = jnp.exp(scores - jnp.max(scores, axis=0, keepdims=True))
        prob = (unnorm * (1.0 / jnp.sum(unnorm, axis=0, keepdims=True))).astype(BF)
        probs[head] = prob
        att[spans[0], :] = dot(values, prob, 1, 0).astype(BF)
        return carry

    lax.fori_loop(0, local // HEAD, one_head, 0, unroll=UNROLL)

    def out_rows(r):
        rows = dot(att[:, r], weights[3 * local : 4 * local, :], 0, 0)
        part[r, :] = rows if first else rows + part_in[r, :]

    by_halves(part.shape[0], out_rows)
    if last:

        def block(r):
            total = part[r, :] + table[0:1, :] + tok[r, :].astype(F32)
            unit_rows, scale_rows = normalize(total)
            unit[r, :] = unit_rows
            scale[r, :] = scale_rows
            rows = unit_rows * table[1:2, :] + table[2:3, :]
            normed[r, :] = rows
            normed_low[r, :] = rows.astype(BF)

        by_blocks(tok.shape[0], block)


def attention(tokens, pack, part=None, table=None, small=False):
    rows, width = tokens.shape
    local = (pack.shape[0] - BIAS_ROWS) // 4
    first, last = part is None, table is not None
    ops = [tokens, pack] + [x for x in (part, table) if x is not None]
    outs = [((3 * local, rows), BF), ((local // HEAD, rows, rows), BF), ((local, rows), BF)]
    outs += [((1, width), F32)]
    if last:
        outs += [((rows, width), F32), ((rows, width), BF), ((rows, width), F32), ((rows, 1), F32)]
    else:
        outs += [((rows, width), F32)]
    return run(
        functools.partial(attention_kernel, first, last, small),
        "attention_last" if last else "attention",
        outs,
        *ops,
        scratch=[pltpu.VMEM((3 * local, 1), F32)] + [pltpu.VMEM((rows, width), F32)] * last,
        estimate=cost(2.5e9, 4e6),
    )


def feed_kernel(last, *refs):
    low, up, down, bias, part_in, *refs = refs
    if last:
        table, cot, act, slope, layer_out, down_low, grad_second, small, part = refs
    else:
        act, slope, part = refs
    rows = dot(low[...], up[...], 1, 0) + bias[...]
    cdf = 0.5 * (1.0 + lax.erf(rows * 0.7071067811865476))
    active = (rows * cdf).astype(BF)
    act[...] = active
    slope[...] = (cdf + (rows * 0.3989422804014327) * jnp.exp(-0.5 * rows * rows)).astype(BF)
    part[...] = part_in[...] + dot(active, down[...], 1, 0)
    if last:
        small[...] = jnp.zeros_like(small)

        def block(r):
            unit2, scale2 = normalize(part[r, :] + table[3:4, :])
            layer_out[r, :] = unit2 * table[4:5, :] + table[5:6, :]
            cots = cot[r, :].astype(F32)
            grad = norm_back(cots * table[4:5, :], unit2, scale2)
            grad_second[r, :] = grad
            down_low[r, :] = grad.astype(BF)
            small[0:1, :] += jnp.sum(grad, axis=0, keepdims=True)
            small[1:2, :] += jnp.sum(cots * unit2, axis=0, keepdims=True)
            small[2:3, :] += jnp.sum(cots, axis=0, keepdims=True)

        by_blocks(low.shape[0], block)


def feed(low, up, down, bias, part, extra=None):
    rows, width = low.shape
    hidden = up.shape[1]
    last = extra is not None
    ops = [low, up, down, bias, part, *(extra or [])]
    outs = [((rows, hidden), BF)] * 2
    if last:
        outs += [((rows, width), F32), ((rows, width), BF), ((rows, width), F32), ((8, width), F32)]
    else:
        outs += [((rows, width), F32)]
    return run(
        functools.partial(feed_kernel, last),
        "feed_last" if last else "feed",
        outs,
        *ops,
        scratch=[pltpu.VMEM((rows, width), F32)] if last else [],
        estimate=cost(2.5e9 if last else 1.5e9, 4e6),
    )


def down_grad_kernel(*refs):
    count = len(refs) // 2
    low = refs[count]
    for act, out in zip(refs[:count], refs[count + 1 :]):

        out[...] = dot(act[...], low[...], 0, 0).astype(BF)


def down_grad(acts, low):
    return run(
        down_grad_kernel,
        "down_grad",
        [((acts[0].shape[1], low.shape[1]), BF)] * len(acts),
        *acts,
        low,
        estimate=cost(1.2e9, 4e6),
    )


def feed_back_kernel(last, *refs):
    slope, down_low, normed_low, grad_in, up, down, *refs = refs
    if last:
        unit, scale, table, grads, bias, grad_first, first_low, small, part = refs
    else:
        grads, bias, part = refs
    grad_up = (dot(down_low[...], down[...], 1, 1) * slope[...].astype(F32)).astype(BF)
    bias[...] = jnp.sum(grad_up.astype(F32), axis=0, keepdims=True)

    def grad_rows(r):
        grads[r, :] = dot(normed_low[:, r], grad_up, 0, 0).astype(BF)

    by_halves(grads.shape[0], grad_rows)
    part[...] = grad_in[...] + dot(grad_up, up[...], 1, 1)
    if last:
        small[...] = jnp.zeros_like(small)

        def block(r):
            grad = part[r, :]
            units = unit[r, :]
            first = norm_back(grad * table[1:2, :], units, scale[r, :])
            grad_first[r, :] = first
            first_low[r, :] = first.astype(BF)
            small[0:1, :] += jnp.sum(first, axis=0, keepdims=True)
            small[1:2, :] += jnp.sum(grad * units, axis=0, keepdims=True)
            small[2:3, :] += jnp.sum(grad, axis=0, keepdims=True)

        by_blocks(part.shape[0], block)


def feed_back(slope, down_low, normed_low, grad_in, up, down, extra=None):
    rows, width = down_low.shape
    hidden = up.shape[1]
    last = extra is not None
    outs = [((width, hidden), BF), ((1, hidden), F32), ((rows, width), F32)]
    if last:
        outs += [((rows, width), BF), ((8, width), F32)]
    return run(
        functools.partial(feed_back_kernel, last),
        "feed_back_last" if last else "feed_back",
        outs,
        slope,
        down_low,
        normed_low,
        grad_in,
        up,
        down,
        *(extra or []),
        scratch=[pltpu.VMEM((rows, width), F32)] if last else [],
        estimate=cost(2.5e9 if last else 2e9, 5e6),
    )


def attention_back_kernel(qkv, probs, first_low, tok, grad_in, weights, grads, bias, out, work):
    local = qkv.shape[0] // 3
    work[3 * local :, :] = dot(weights[3 * local : 4 * local, :], first_low[...], 1, 1).astype(BF)

    def one_head(head, carry):
        spans = head_rows(head, local, 4)
        queries, keys, values = (qkv[span, :] for span in spans[:3])
        grad_att = work[spans[3], :]
        prob = probs[head]
        grad_prob = dot(values, grad_att, 0, 0)
        wide = prob.astype(F32)
        inner = jnp.sum(wide * grad_prob, axis=0, keepdims=True)
        grad_score = (wide * (grad_prob - inner)).astype(BF)
        work[spans[0], :] = (dot(keys, grad_score, 1, 0) * 0.125).astype(BF)
        work[spans[1], :] = dot(queries, grad_score, 1, 1).astype(BF)
        work[spans[2], :] = dot(grad_att, prob, 1, 1).astype(BF)
        return carry

    lax.fori_loop(0, local // HEAD, one_head, 0, unroll=UNROLL)
    joined = work[0 : 3 * local, :]
    grads[...] = dot(joined, tok[...], 1, 0).astype(BF)
    bias[...] = dot(jnp.ones((8, joined.shape[1]), BF), joined, 1, 1)

    def out_rows(r):
        out[r, :] = grad_in[r, :] + dot(work[0 : 3 * local, r], weights[0 : 3 * local, :], 0, 0)

    by_halves(out.shape[0], out_rows)


def attention_back(saved, first_low, tokens, grad_in, pack):
    qkv, probs, _ = saved
    rows, width = tokens.shape
    joined = qkv.shape[0]
    return run(
        attention_back_kernel,
        "attention_back",
        [((joined, width), BF), ((8, joined), F32), ((rows, width), F32)],
        qkv,
        probs,
        first_low,
        tokens,
        grad_in,
        pack,
        scratch=[pltpu.VMEM((joined // 3 * 4, rows), BF)],
        estimate=cost(3.5e9, 6e6),
    )


def out_grad_kernel(a, b, c, d, low, send, keep):
    for ref, both in ((send, (a, c)), (keep, (b, d))):
        for i, att in enumerate(both):
            ref[i] = dot(att[...], low[...], 1, 0).astype(BF)


def out_grad(atts, low):
    shape = (2, atts[0].shape[0], low.shape[1])
    return run(
        out_grad_kernel, "out_grad", [(shape, BF)] * 2, *atts, low, estimate=cost(6e8, 3e6)
    )


def join(plan, base, *pieces):
    rows = sum(p.shape[0] for p in pieces)
    (out,) = run(
        functools.partial(join_kernel, base), "join", [((rows, pieces[0].shape[1]), BF)], *pieces,
        plan=plan,
    )
    return out


def add_rows(target, to, left, right, at, rows):
    block = next(b for b in (32, 24, 8) if rows % b == 0)

    def body(i, carry):
        here = pl.ds(pl.multiple_of(at + i * block, 8), block)
        there = pl.ds(pl.multiple_of(to + i * block, 8), block)
        total = left[here, :].astype(F32) + right[here, :].astype(F32)
        target[there, :] = total.astype(target.dtype)
        return carry

    lax.fori_loop(0, rows // block, body, 0)


def copy_rows(target, to, source, at, rows):
    block = next(b for b in (32, 24, 16, 8) if rows % b == 0)

    def body(i, carry):
        here = pl.ds(pl.multiple_of(at + i * block, 8), block)
        there = pl.ds(pl.multiple_of(to + i * block, 8), block)
        target[there, :] = source[here, :].astype(target.dtype)
        return carry

    lax.fori_loop(0, rows // block, body, 0)


VECTORS = 16


def send_vectors(value, sent):
    high = value.astype(BF)
    low = (value - high.astype(F32)).astype(BF)
    at = sent.shape[0] - 2 * VECTORS
    sent[at : at + VECTORS, :] = high
    sent[at + VECTORS :, :] = low
    return high.astype(F32) + low.astype(F32)


def got_vectors(got):
    at = got.shape[0] - 2 * VECTORS
    return got[at : at + VECTORS, :].astype(F32) + got[at + VECTORS :, :].astype(F32)


def collect(plan, attn, up, second, first, rows):
    span = attn[0].shape[1]
    rows[...] = jnp.zeros_like(rows)
    for shard in range(4):
        wide, narrow = jnp.zeros((1, rows.shape[1]), F32), jnp.zeros((1, span), F32)
        for apart in range(4):
            here = plan[SHARD] == shard ^ apart
            narrow = jnp.where(here, attn[apart][0:1, :], narrow)
            wide = jnp.where(here, up[apart][...], wide)
        rows[shard : shard + 1, 0:span] = narrow
        rows[4 + shard : 5 + shard, :] = wide
    rows[8:11, :] = second[0:3, :]
    rows[11:14, :] = first[0:3, :]


def choose(total, plan, base, count, sent, keep):
    rows = keep.shape[0] // count
    for i in range(count):
        for ref, at in ((sent, base + i), (keep, base + count + i)):
            copy_rows(ref, i * rows, total, pl.multiple_of(plan[at] * rows, rows), rows)


def first_kernel(segments, vectors, plan, *refs):
    if vectors:
        *ops, sent, keep, kept_vectors, rows = refs
        parts = ops[-10:]
        collect(plan, parts[:4], parts[4:8], parts[8], parts[9], rows)
        kept_vectors[...] = send_vectors(rows[...], sent)
    else:
        *ops, sent, keep = refs
    half = keep.shape[0] // 2
    for slot in range(4):
        target = (sent, keep)[slot // 2]
        for block in ((0, 1), (1, 2, 3), (0, 1, 2), (2, 3))[slot]:

            @pl.when(plan[FIRST + slot] == block)
            def _(slot=slot, block=block, target=target):
                begin, end = (block % 2) * half, (block % 2 + 1) * half
                at = 0
                for left, right, size in segments[block // 2]:
                    low, high = max(begin, at), min(end, at + size)
                    if low < high:
                        to = (slot % 2) * half + low - begin
                        add_rows(target, to, ops[left[0]].at[left[1]], ops[right[0]].at[right[1]], low - at, high - low)
                    at += size


def first_stage(plan, parts, stacked, vectors):
    width = parts[0].shape[-1]
    size = parts[0].shape[0]
    ops = [p[None] for p in parts] + list(stacked)
    segments = [[((0, 0), (1, 0), size)], [((2, 0), (3, 0), size)]]
    rows = size
    if stacked:
        rows += stacked[0].shape[1]
        for i in range(2):
            segments[i].append(((4, i), (5, i), rows - size))
    outs = [((rows, width), BF), ((rows, width), F32)]
    if vectors:
        outs = [((rows + 2 * VECTORS, width), BF), outs[1], ((VECTORS, width), F32)]
    return run(
        functools.partial(first_kernel, segments, bool(vectors)),
        "first_stage",
        outs,
        *ops,
        *vectors,
        scratch=[pltpu.VMEM((VECTORS, width), F32)] if vectors else [],
        plan=plan,
    )


def next_kernel(base, count, plan, kept, got, *refs):
    rows = kept.shape[0]
    if len(refs) > 3:
        had, sent, keep, has, total = refs
        has[...] = send_vectors(had[...] + got_vectors(got), sent)
    else:
        sent, keep, total = refs
    total[...] = kept[...] + got[0:rows, :].astype(F32)
    choose(total, plan, base, count, sent, keep)


def next_stage(plan, base, count, kept, got, vectors=()):
    rows, width = kept.shape
    outs = [((rows // 2, width), BF), ((rows // 2, width), F32)]
    if vectors:
        outs = [((rows // 2 + 2 * VECTORS, width), BF), outs[1], ((VECTORS, width), F32)]
    return run(
        functools.partial(next_kernel, base, count),
        "next_stage",
        outs,
        kept,
        got,
        *vectors,
        scratch=[pltpu.VMEM((rows, width), F32)],
        plan=plan,
    )


def finish_kernel(sizes, plan, mine, theirs, *refs):
    outs, (sums, sem) = refs[:-2], refs[-2:]
    rows = mine.shape[0] // 4
    copies = []
    for i in range(8):
        where = pl.ds(pl.multiple_of(plan[PLACES + i % 4] * rows, rows), rows)
        begin, end = i * rows, (i + 1) * rows
        sums[begin:end, :] = jnp.where(
            plan[SIDE] == i // 4, mine[where, :], theirs[where, :]
        ).astype(F32)
        at = 0
        for ref, size in zip(outs, sizes):
            low, high = max(begin, at), min(end, at + size)
            if low < high:
                source, target = sums.at[pl.ds(low, high - low)], ref.at[pl.ds(low - at, high - low)]
                copies.append(pltpu.make_async_copy(source, target, sem))
                copies[-1].start()
            at += size
    for copy in copies:
        copy.wait()


def finish(plan, mine, theirs, sizes):
    half, width = mine.shape
    return pl.pallas_call(
        functools.partial(finish_kernel, sizes),
        grid_spec=pltpu.PrefetchScalarGridSpec(
            num_scalar_prefetch=1,
            grid=(1,),
            in_specs=[whole((half, width))] * 2,
            out_specs=[ANY] * len(sizes),
            scratch_shapes=[pltpu.VMEM((2 * half, width), F32), pltpu.SemaphoreType.DMA(())],
        ),
        out_shape=[jax.ShapeDtypeStruct((size, width), F32) for size in sizes],
        compiler_params=params(),
        cost_estimate=SMALL,
        name="finish",
    )(plan, mine, theirs)


Y, X, Z_NEAR, Z_FAR = ("tensor", 2), ("dp", 1), ("dp", 2), ("dp", 4)


def tie(value, *others):
    return lax.optimization_barrier((value, others))[0]


def swap(value, even, odd=None):
    groups, width = lax.axis_size("dp"), lax.axis_size("tensor")
    pairs = []
    for group in range(groups):
        for t in range(width):
            axis, bit = even if odd is None or t % 2 == 0 else odd
            to = (group ^ bit, t) if axis == "dp" else (group, t ^ bit)
            pairs.append((group * width + t, to[0] * width + to[1]))
    return lax.ppermute(value, ("dp", "tensor"), pairs)


def partner(value):
    return swap(value, ("tensor", 1))


def make_plan():
    index, t = lax.axis_index("dp"), lax.axis_index("tensor")
    x, near, far, core = index % 2, index // 2 % 2, index // 4 % 2, t % 2
    quarter, place = x + 2 * near, near + 2 * far
    even = [quarter, quarter ^ 1, quarter ^ 2, quarter ^ 3]
    odd = [quarter, quarter ^ 2, quarter ^ 1, quarter ^ 3]
    even += odd + [0, 1, 2, 3]
    odd += even[:4] + [0, 1, 2, 3]
    even += [0, 1, 2, 3]
    odd += [1 - x, 3 - x, x, 2 + x]
    even += [1 - x, x]
    odd += [0, 1]
    even += [1 - near, 3 - near, near, 2 + near]
    odd += [2 - 2 * far, 3 - 2 * far, 2 * far, 2 * far + 1]
    even += [1 - far, far]
    odd += [1 - near, near]
    apart = [i ^ place for i in range(4)]
    even += [i // 2 + 2 * (i % 2) for i in apart]
    odd += apart
    quarters = [quarter ^ i for i in range(4)]
    even += [x, *quarters, t]
    odd += [x, *quarters, t]
    both = [jnp.stack([jnp.asarray(i, jnp.int32) for i in plan]) for plan in (even, odd)]
    return jnp.where(core == 0, *both)


class Gather:
    def __init__(self, plan, sent, tail=0):
        self.plan, self.tail = plan, tail
        self.got = swap(sent, Y)

    def after(self, *values):
        self.got = tie(self.got, *values)

    @classmethod
    def of_two(cls, plan, sent):
        return cls(plan, sent)

    def both(self):
        rows = self.got.shape[0] // 2
        self.held, self.far = self.got[:rows], self.got[rows:]
        self.got = [swap(self.held, X), swap(self.held, Z_NEAR)]

    def joined(self):
        return join(self.plan, QUARTERS, self.held, *self.got, self.far)

    def second(self):
        rows = self.got.shape[0] - self.tail
        self.rest = [self.got[rows:]] if self.tail else []
        self.held = self.got[:rows]
        self.got = swap(self.held, X, Z_NEAR)

    def third(self):
        self.held = jnp.concatenate([self.held, self.got], axis=0)
        self.got = swap(self.held, Z_NEAR, X)

    def result(self):
        rows = self.held.shape[0] // 2
        return join(
            self.plan, BY_B, self.held[:rows], self.held[rows:], self.got[:rows], self.got[rows:], *self.rest
        )


class Reduction:
    def __init__(self, plan):
        self.plan = plan

    def after(self, *values):
        self.got = tie(self.got, *values)

    def first(self, parts, stacked=(), vectors=()):
        self.sent, self.keep, *self.vectors = first_stage(self.plan, parts, stacked, vectors)
        self.got = swap(self.sent, Y, X)

    def next(self, base, count):
        self.sent, self.keep, *self.vectors = next_stage(
            self.plan, base, count, self.keep, self.got, self.vectors
        )

    def second(self):
        self.next(SECOND, 1)
        self.got = swap(self.sent, X, Y)

    def third(self):
        self.next(THIRD, 2)
        self.got = swap(self.sent, Z_NEAR, Z_FAR)

    def fourth(self):
        self.next(FOURTH, 1)
        self.got = swap(self.sent, Z_FAR, Z_NEAR)

    def fifth(self):
        rows = self.keep.shape[0]
        total = (self.keep + self.got[:rows].astype(F32)).astype(BF)
        if self.vectors:
            high, low = self.got[rows : rows + VECTORS], self.got[rows + VECTORS :]
            self.vectors = [self.vectors[0] + (high.astype(F32) + low.astype(F32))]
        bit = 8
        while bit < lax.axis_size("dp"):
            total = (total.astype(F32) + swap(total, ("dp", bit)).astype(F32)).astype(BF)
            self.vectors = [v + swap(v, ("dp", bit)) for v in self.vectors]
            bit *= 2
        self.sent = total
        self.got = swap(self.sent, Z_FAR, Z_NEAR)

    def sixth(self):
        self.sent = jnp.concatenate([self.sent, self.got], axis=0)
        self.got = swap(self.sent, Z_NEAR, Z_FAR)

    def seventh(self):
        self.sent = jnp.concatenate([self.sent, self.got], axis=0)
        self.got = swap(self.sent, X)

    def result(self, sizes):
        return finish(self.plan, self.sent, self.got, sizes)


def on_device(
    tokens,
    w_query,
    w_key,
    w_value,
    b_query,
    b_value,
    w_output,
    b_output,
    first_gain,
    first_shift,
    w_up,
    b_up,
    w_down,
    b_down,
    second_gain,
    second_shift,
    cotangent,
):
    rows, width = tokens.shape
    local = w_query.shape[1]
    assert rows == SEQ_LEN and width == 4 * local and w_up.shape == (width, width)
    plan = make_plan()
    near = pack_near(plan, w_query, w_key, w_value, w_output, (b_query, b_value, b_up))
    pack_d, up_far, down_far, table = pack_weights(
        tie(plan, near), w_query, w_key, w_value, w_output, w_up, w_down, near,
        (b_output, first_gain, first_shift, b_down, second_gain, second_shift),
    )

    far_pack = Gather(plan, near, BIAS_ROWS)
    up = Gather.of_two(plan, tie(up_far, near))
    pack_c = partner(tie(pack_d, near))
    down = Gather.of_two(plan, tie(down_far, far_pack.got))
    far_pack.second()
    *saved_d, bias_d, part = attention(tie(tokens, far_pack.held), pack_d, small=True)
    far_pack.after(part)
    far_pack.third()
    *saved_c, bias_c, part = attention(tokens, pack_c, tie(part, far_pack.held), small=True)
    far_pack.after(part)
    pack_b = far_pack.result()
    up.after(pack_b)
    up.both()
    pack_a = partner(pack_b)
    up_d, down_d = w_up, w_down
    up_c = partner(tie(w_up, pack_b))
    *saved_b, bias_b, part = attention(tokens, pack_b, tie(part, up.held))
    down.after(part)
    down.both()
    down_c = partner(tie(w_down, down.held))
    *saved_a, bias_a, normed, normed_low, unit, scale = attention(
        tokens, pack_a, tie(part, down.held), table
    )
    up.got, up.far = tie((up.got, up.far), normed)
    up_b = up.joined()
    up_a = partner(up_b)
    act_d, slope_d, part = feed(normed_low, up_d, down_d, bias_d, tie(normed, up_b))
    act_c, slope_c, part = feed(normed_low, up_c, down_c, bias_c, part)
    down.got, down.far = tie((down.got, down.far), part)
    down_b = down.joined()
    down_a = partner(down_b)
    act_b, slope_b, part = feed(normed_low, up_b, down_b, bias_b, part)
    act_a, slope_a, layer_out, down_low, grad_second, small_second = feed(
        normed_low, up_a, down_a, bias_a, part, [table, cotangent]
    )

    down, up, attn = Reduction(plan), Reduction(plan), Reduction(plan)
    grad_a, grad_b = down_grad([act_a, act_b], down_low)
    core_other = partner(grad_a)
    grad_c, grad_d = down_grad([act_c, act_d], tie(down_low, grad_a))
    core_own = partner(grad_c)
    up_grad_a, bias_up_a, part = feed_back(
        slope_a, down_low, normed_low, tie(grad_second, grad_c), up_a, down_a
    )
    core_up_other = partner(up_grad_a)
    down.first([grad_b, *tie((core_other,), up_grad_a), grad_d, core_own])
    up_grad_b, bias_up_b, part = feed_back(
        slope_b, down_low, normed_low, tie(part, down.sent), up_b, down_b
    )
    up_grad_c, bias_up_c, part = feed_back(
        slope_c, down_low, normed_low, tie(part, core_up_other), up_c, down_c
    )
    core_up_own = partner(up_grad_c)
    up_grad_d, bias_up_d, grad_first, first_low, small_first = feed_back(
        slope_d, down_low, normed_low, part, up_d, down_d, [unit, scale, table]
    )
    out_send, out_keep = out_grad([s[2] for s in (saved_a, saved_b, saved_c, saved_d)], first_low)
    core_out = partner(out_send)
    down.after(out_keep)
    down.second()
    grad_a, bias_a, part = attention_back(
        saved_a[:3], first_low, tokens, tie(grad_first, down.sent), pack_a
    )
    core_other = partner(grad_a)
    up.first([up_grad_b, core_up_other, up_grad_d, core_up_own], [out_keep, tie(core_out, grad_a)])
    down.after(up.sent)
    down.third()
    grad_b, bias_b, part = attention_back(
        saved_b, first_low, tokens, tie(part, down.sent), pack_b
    )
    grad_c, bias_c, part = attention_back(
        saved_c, first_low, tokens, tie(part, core_other), pack_c
    )
    core_own = partner(grad_c)
    down.after(grad_c)
    down.fourth()
    up.after(down.sent)
    up.second()
    grad_d, bias_d, grad_tokens = attention_back(
        saved_d, first_low, tokens, tie(part, up.sent), pack_d
    )
    down.after(grad_tokens)
    down.fifth()
    attn.first(
        [grad_b, core_other, grad_d, tie(core_own, down.sent, up.got)],
        vectors=[
            bias_d, bias_c, bias_b, bias_a, bias_up_d, bias_up_c, bias_up_b, bias_up_a,
            small_second, small_first,
        ],
    )

    up.after(attn.sent)
    up.third()
    down.after(up.sent)
    down.sixth()

    attn.after(down.sent)
    attn.second()
    up.after(attn.sent)
    up.fourth()
    down.after(up.sent)
    down.seventh()

    attn.after(down.sent)
    attn.third()
    up.after(attn.sent)
    up.fifth()

    attn.after(up.sent)
    attn.fourth()
    up.after(attn.sent)
    up.sixth()
    down.after(up.sent)
    (grad_w_down,) = down.result((width,))

    attn.after(grad_w_down)
    attn.fifth()
    (sums,) = attn.vectors
    others = partner(sums)
    up.after(attn.sent)
    up.seventh()

    attn.after(up.sent)
    attn.sixth()
    sums = sums + tie(others, attn.sent)
    shard = lax.axis_index("tensor")
    attn_vectors = lax.dynamic_index_in_dim(sums, shard, 0, keepdims=False)
    up_vector = lax.dynamic_index_in_dim(sums, 4 + shard, 0, keepdims=False)

    attn.after(attn_vectors, up_vector)
    attn.seventh()
    up.after(attn.sent)
    grad_w_up, grad_o = up.result((width, local))
    attn.after(grad_o)
    grad_q, grad_k, grad_v = attn.result((local,) * 3)

    return (
        tie(layer_out, attn.sent).astype(BF),
        tie(grad_tokens, attn.sent).astype(BF),
        grad_q.T,
        grad_k.T,
        grad_v.T,
        attn_vectors[:local],
        attn_vectors[2 * local : 3 * local],
        grad_o,
        sums[11],
        sums[12],
        sums[13],
        grad_w_up,
        up_vector,
        grad_w_down,
        sums[8],
        sums[9],
        sums[10],
    )


def solution(mesh):
    rows = P(("dp", "tensor"), None)
    col, row, vec, rep = P(None, "tensor"), P("tensor", None), P("tensor"), P()
    return jax.shard_map(
        on_device,
        mesh=mesh,
        in_specs=(
            rows, col, col, col, vec, vec, row, rep, rep, rep, col, vec, row, rep, rep, rep, rows,
        ),
        out_specs=(
            rows, rows, col, col, col, vec, vec, row, rep, rep, rep, col, vec, row, rep, rep, rep,
        ),
        check_vma=False,
    )
```

```python
import functools

import jax
import jax.numpy as jnp
from jax import lax
from jax.experimental import pallas as pl
from jax.experimental.pallas import tpu as pltpu
from jax.sharding import PartitionSpec as P

HEAD = 64
SEQ_LEN = 512
BIAS_ROWS = 16
BF = jnp.bfloat16
F32 = jnp.float32
ANY = pl.BlockSpec(memory_space=pl.ANY)
VMEM_BYTES = 26 << 20
BY_B, BY_A, NATURAL, FIRST, SECOND, THIRD, FOURTH, PLACES, SIDE, QUARTERS, SHARD = 0, 4, 8, 12, 16, 18, 22, 24, 28, 29, 33
ALL_VMEM_BYTES = 60 << 20
UNROLL = 1


def dot(left, right, left_dim, right_dim):
    return lax.dot_general(
        left, right, (((left_dim,), (right_dim,)), ((), ())), preferred_element_type=F32
    )


SMALL = pl.CostEstimate(flops=1000, bytes_accessed=1000, transcendentals=0)


def whole(shape):
    return pl.BlockSpec(shape, lambda *_: (0,) * len(shape))


def params(limit=VMEM_BYTES):
    return pltpu.CompilerParams(vmem_limit_bytes=limit)


def cost(flops, moved):
    return pl.CostEstimate(flops=int(20 * flops), bytes_accessed=int(20 * moved), transcendentals=0)


def run(kernel, name, outs, *ops, scratch=(), estimate=SMALL, plan=None):
    specs = [pl.BlockSpec(memory_space=pltpu.VMEM)] * len(ops)
    if plan is not None:
        ops = (plan, *ops)
        specs.insert(0, pl.BlockSpec(memory_space=pltpu.SMEM))
    return pl.pallas_call(
        kernel,
        in_specs=specs,
        out_specs=[pl.BlockSpec(memory_space=pltpu.VMEM)] * len(outs),
        out_shape=[jax.ShapeDtypeStruct(shape, dtype) for shape, dtype in outs],
        scratch_shapes=scratch,
        compiler_params=params(),
        cost_estimate=estimate,
        name=name,
    )(*ops)


def near_kernel(plan, wq, wk, wv, wo, bq, bv, bu, out, *lines):
    sem = lines[-1]
    local, width = wq.shape
    for i, ref in enumerate((wq, wk, wv, wo)):

        @pl.when(plan[BY_B] == i)
        def _(ref=ref):
            pltpu.make_async_copy(ref, out.at[pl.ds(0, local)], sem.at[0]).start()

    copies = [
        pltpu.make_async_copy(ref, line, sem.at[1]) for ref, line in zip((bq, bv, bu), lines)
    ]
    for copy in copies:
        copy.start()
    out[local:, :] = jnp.zeros((BIAS_ROWS, width), BF)
    for copy in copies:
        copy.wait()
    q, v, u = lines[:3]
    out[local : local + 1, 0:local] = q[...].reshape(1, local)
    out[local : local + 1, local : 2 * local] = v[...].reshape(1, local)
    out[local + 1 : local + 2, :] = u[...].reshape(1, width)
    pltpu.make_async_copy(wq, out.at[pl.ds(0, local)], sem.at[0]).wait()


def pack_near(plan, w_query, w_key, w_value, w_output, biases):
    local, width = w_output.shape
    (out,) = pl.pallas_call(
        near_kernel,
        in_specs=[pl.BlockSpec(memory_space=pltpu.SMEM)] + [ANY] * 7,
        out_specs=[pl.BlockSpec(memory_space=pltpu.VMEM)],
        out_shape=[jax.ShapeDtypeStruct((local + BIAS_ROWS, width), BF)],
        scratch_shapes=[
            *[pltpu.VMEM(v.shape, BF) for v in biases],
            pltpu.SemaphoreType.DMA((2,)),
        ],
        compiler_params=params(ALL_VMEM_BYTES),
        name="pack_near",
    )(plan, w_query.T, w_key.T, w_value.T, w_output, *biases)
    return out


def pack_kernel(plan, wq, wk, wv, wo, wu, wd, near, *refs):
    vectors, refs = refs[:6], refs[6:]
    out, up_far, down_far, table, packed, piece, lines, *lists, sem = refs
    local, width = wq.shape
    at = pl.multiple_of(plan[BY_B] * local, local)
    opposite = pl.multiple_of(plan[QUARTERS + 3] * local, local)
    pieces = [
        pltpu.make_async_copy(ref.at[pl.ds(rows, local)], piece.at[i], sem.at[1])
        for i, (ref, rows) in enumerate(((wu, at), (wu, opposite), (wd, at), (wd, opposite)))
    ]
    copies = [
        pltpu.make_async_copy(ref, packed.at[pl.ds(i * local, local)], sem.at[0])
        for i, ref in enumerate((wq, wk, wv, wo))
    ]
    copies.append(
        pltpu.make_async_copy(
            near.at[pl.ds(local, BIAS_ROWS)], packed.at[pl.ds(4 * local, BIAS_ROWS)], sem.at[0]
        )
    )
    copies += [
        pltpu.make_async_copy(ref, line, sem.at[0]) for ref, line in zip(vectors, lists)
    ]
    for copy in pieces:
        copy.start()
    for copy in copies:
        copy.start()
    lines[...] = jnp.zeros_like(lines)
    outs = []
    for copy in pieces:
        copy.wait()
    for i, ref in enumerate((up_far, down_far)):
        for h in range(2):
            part = ref.at[pl.ds(h * local, local)]
            outs.append(pltpu.make_async_copy(piece.at[2 * i + h], part, sem.at[2]))
            outs[-1].start()
    for copy in copies:
        copy.wait()
    outs.append(pltpu.make_async_copy(packed, out, sem.at[2]))
    outs[-1].start()
    for i, ref in enumerate(lists):
        lines[i : i + 1, :] = ref[...].astype(F32).reshape(1, width)
    outs.append(pltpu.make_async_copy(lines, table, sem.at[2]))
    outs[-1].start()
    for copy in outs:
        copy.wait()


def pack_weights(plan, w_query, w_key, w_value, w_output, w_up, w_down, near, vectors):
    local, width = w_output.shape
    shapes = [
        jax.ShapeDtypeStruct((4 * local + BIAS_ROWS, width), BF),
        *[jax.ShapeDtypeStruct((2 * local, width), BF)] * 2,
        jax.ShapeDtypeStruct((8, width), F32),
    ]
    return pl.pallas_call(
        pack_kernel,
        grid_spec=pltpu.PrefetchScalarGridSpec(
            num_scalar_prefetch=1,
            grid=(1,),
            in_specs=[ANY] * 13,
            out_specs=[ANY] * 4,
            scratch_shapes=[
                pltpu.VMEM(shapes[0].shape, BF),
                pltpu.VMEM((4, local, width), BF),
                pltpu.VMEM(shapes[3].shape, F32),
                *[pltpu.VMEM(v.shape, BF) for v in vectors],
                pltpu.SemaphoreType.DMA((3,)),
            ],
        ),
        out_shape=shapes,
        compiler_params=params(ALL_VMEM_BYTES),
        name="pack_weights",
    )(plan, w_query.T, w_key.T, w_value.T, w_output, w_up, w_down, near, *vectors)


def join_kernel(base, plan, *refs):
    *pieces, out = refs
    at = 0
    rows = pieces[0].shape[0]
    for ref in pieces:
        if at < 4:
            count = ref.shape[0] // rows
            for i in range(count):
                where = pl.multiple_of(plan[base + at + i] * rows, rows)
                copy_rows(out, where, ref, i * rows, rows)
            at += count
        else:
            out[4 * rows :, :] = ref[...]


def normalize(rows):
    center = rows - jnp.mean(rows, axis=-1, keepdims=True)
    scale = lax.rsqrt(jnp.mean(center * center, axis=-1, keepdims=True) + 1e-12)
    return center * scale, scale


def norm_back(grad, unit, scale):
    return scale * (
        grad
        - jnp.mean(grad, axis=-1, keepdims=True)
        - unit * jnp.mean(grad * unit, axis=-1, keepdims=True)
    )


def by_blocks(rows, body, block=128):
    def step(i, carry):
        body(pl.ds(pl.multiple_of(i * block, block), block))
        return carry

    lax.fori_loop(0, rows // block, step, 0)


def by_halves(rows, body):
    def step(i, carry):
        body(pl.ds(pl.multiple_of(i * (rows // 2), 128), rows // 2))
        return carry

    lax.fori_loop(0, 2, step, 0)


def head_rows(head, local, count):
    return [pl.ds(pl.multiple_of(i * local + head * HEAD, HEAD), HEAD) for i in range(count)]


def attention_kernel(first, last, small, *refs):
    tok, weights, *refs = refs
    if not first:
        part_in, *refs = refs
    if last:
        table, *refs = refs
        qkv, probs, att, bias_up, normed, normed_low, unit, scale, bias, part = refs
    else:
        qkv, probs, att, bias_up, part, bias = refs
    local = att.shape[0]
    body = 4 * local
    rows = weights[body : body + BIAS_ROWS, :].astype(F32)
    bias_up[...] = rows[1:2, :]
    column = jnp.transpose(rows)
    bias[...] = jnp.zeros_like(bias)
    bias[0:local, :] = column[0:local, 0:1]
    bias[2 * local : 3 * local, :] = column[local : 2 * local, 0:1]

    def project(i, carry):
        r = pl.ds(pl.multiple_of(i * local, local), local)
        rows = (dot(weights[r, :], tok[...], 1, 1) + bias[r, :]).astype(BF)
        qkv[r, :] = rows * jnp.where(i == 0, 0.125, 1.0).astype(BF)
        return carry

    lax.fori_loop(0, 3, project, 0, unroll=1 if small else 3)

    def one_head(head, carry):
        spans = head_rows(head, local, 3)
        queries, keys, values = (qkv[span, :] for span in spans)
        scores = dot(keys, queries, 0, 0)
        unnorm = jnp.exp(scores - jnp.max(scores, axis=0, keepdims=True))
        prob = (unnorm * (1.0 / jnp.sum(unnorm, axis=0, keepdims=True))).astype(BF)
        probs[head] = prob
        att[spans[0], :] = dot(values, prob, 1, 0).astype(BF)
        return carry

    lax.fori_loop(0, local // HEAD, one_head, 0, unroll=UNROLL)

    def out_rows(r):
        rows = dot(att[:, r], weights[3 * local : 4 * local, :], 0, 0)
        part[r, :] = rows if first else rows + part_in[r, :]

    by_halves(part.shape[0], out_rows)
    if last:

        def block(r):
            total = part[r, :] + table[0:1, :] + tok[r, :].astype(F32)
            unit_rows, scale_rows = normalize(total)
            unit[r, :] = unit_rows
            scale[r, :] = scale_rows
            rows = unit_rows * table[1:2, :] + table[2:3, :]
            normed[r, :] = rows
            normed_low[r, :] = rows.astype(BF)

        by_blocks(tok.shape[0], block)


def attention(tokens, pack, part=None, table=None, small=False):
    rows, width = tokens.shape
    local = (pack.shape[0] - BIAS_ROWS) // 4
    first, last = part is None, table is not None
    ops = [tokens, pack] + [x for x in (part, table) if x is not None]
    outs = [((3 * local, rows), BF), ((local // HEAD, rows, rows), BF), ((local, rows), BF)]
    outs += [((1, width), F32)]
    if last:
        outs += [((rows, width), F32), ((rows, width), BF), ((rows, width), F32), ((rows, 1), F32)]
    else:
        outs += [((rows, width), F32)]
    return run(
        functools.partial(attention_kernel, first, last, small),
        "attention_last" if last else "attention",
        outs,
        *ops,
        scratch=[pltpu.VMEM((3 * local, 1), F32)] + [pltpu.VMEM((rows, width), F32)] * last,
        estimate=cost(2.5e9, 4e6),
    )


def feed_kernel(last, *refs):
    low, up, down, bias, part_in, *refs = refs
    if last:
        table, cot, act, slope, layer_out, down_low, grad_second, small, part = refs
    else:
        act, slope, part = refs
    rows = dot(low[...], up[...], 1, 0) + bias[...]
    cdf = 0.5 * (1.0 + lax.erf(rows * 0.7071067811865476))
    active = (rows * cdf).astype(BF)
    act[...] = active
    slope[...] = (cdf + (rows * 0.3989422804014327) * jnp.exp(-0.5 * rows * rows)).astype(BF)
    part[...] = part_in[...] + dot(active, down[...], 1, 0)
    if last:
        small[...] = jnp.zeros_like(small)

        def block(r):
            unit2, scale2 = normalize(part[r, :] + table[3:4, :])
            layer_out[r, :] = unit2 * table[4:5, :] + table[5:6, :]
            cots = cot[r, :].astype(F32)
            grad = norm_back(cots * table[4:5, :], unit2, scale2)
            grad_second[r, :] = grad
            down_low[r, :] = grad.astype(BF)
            small[0:1, :] += jnp.sum(grad, axis=0, keepdims=True)
            small[1:2, :] += jnp.sum(cots * unit2, axis=0, keepdims=True)
            small[2:3, :] += jnp.sum(cots, axis=0, keepdims=True)

        by_blocks(low.shape[0], block)


def feed(low, up, down, bias, part, extra=None):
    rows, width = low.shape
    hidden = up.shape[1]
    last = extra is not None
    ops = [low, up, down, bias, part, *(extra or [])]
    outs = [((rows, hidden), BF)] * 2
    if last:
        outs += [((rows, width), F32), ((rows, width), BF), ((rows, width), F32), ((8, width), F32)]
    else:
        outs += [((rows, width), F32)]
    return run(
        functools.partial(feed_kernel, last),
        "feed_last" if last else "feed",
        outs,
        *ops,
        scratch=[pltpu.VMEM((rows, width), F32)] if last else [],
        estimate=cost(2.5e9 if last else 1.5e9, 4e6),
    )


def down_grad_kernel(*refs):
    count = len(refs) // 2
    low = refs[count]
    for act, out in zip(refs[:count], refs[count + 1 :]):

        out[...] = dot(act[...], low[...], 0, 0).astype(BF)


def down_grad(acts, low):
    return run(
        down_grad_kernel,
        "down_grad",
        [((acts[0].shape[1], low.shape[1]), BF)] * len(acts),
        *acts,
        low,
        estimate=cost(1.2e9, 4e6),
    )


def feed_back_kernel(last, *refs):
    slope, down_low, normed_low, grad_in, up, down, *refs = refs
    if last:
        unit, scale, table, grads, bias, grad_first, first_low, small, part = refs
    else:
        grads, bias, part = refs
    grad_up = (dot(down_low[...], down[...], 1, 1) * slope[...].astype(F32)).astype(BF)
    bias[...] = jnp.sum(grad_up.astype(F32), axis=0, keepdims=True)

    def grad_rows(r):
        grads[r, :] = dot(normed_low[:, r], grad_up, 0, 0).astype(BF)

    by_halves(grads.shape[0], grad_rows)
    part[...] = grad_in[...] + dot(grad_up, up[...], 1, 1)
    if last:
        small[...] = jnp.zeros_like(small)

        def block(r):
            grad = part[r, :]
            units = unit[r, :]
            first = norm_back(grad * table[1:2, :], units, scale[r, :])
            grad_first[r, :] = first
            first_low[r, :] = first.astype(BF)
            small[0:1, :] += jnp.sum(first, axis=0, keepdims=True)
            small[1:2, :] += jnp.sum(grad * units, axis=0, keepdims=True)
            small[2:3, :] += jnp.sum(grad, axis=0, keepdims=True)

        by_blocks(part.shape[0], block)


def feed_back(slope, down_low, normed_low, grad_in, up, down, extra=None):
    rows, width = down_low.shape
    hidden = up.shape[1]
    last = extra is not None
    outs = [((width, hidden), BF), ((1, hidden), F32), ((rows, width), F32)]
    if last:
        outs += [((rows, width), BF), ((8, width), F32)]
    return run(
        functools.partial(feed_back_kernel, last),
        "feed_back_last" if last else "feed_back",
        outs,
        slope,
        down_low,
        normed_low,
        grad_in,
        up,
        down,
        *(extra or []),
        scratch=[pltpu.VMEM((rows, width), F32)] if last else [],
        estimate=cost(2.5e9 if last else 2e9, 5e6),
    )


def attention_back_kernel(qkv, probs, first_low, tok, grad_in, weights, grads, bias, out, work):
    local = qkv.shape[0] // 3
    work[3 * local :, :] = dot(weights[3 * local : 4 * local, :], first_low[...], 1, 1).astype(BF)

    def one_head(head, carry):
        spans = head_rows(head, local, 4)
        queries, keys, values = (qkv[span, :] for span in spans[:3])
        grad_att = work[spans[3], :]
        prob = probs[head]
        grad_prob = dot(values, grad_att, 0, 0)
        wide = prob.astype(F32)
        inner = jnp.sum(wide * grad_prob, axis=0, keepdims=True)
        grad_score = (wide * (grad_prob - inner)).astype(BF)
        work[spans[0], :] = (dot(keys, grad_score, 1, 0) * 0.125).astype(BF)
        work[spans[1], :] = dot(queries, grad_score, 1, 1).astype(BF)
        work[spans[2], :] = dot(grad_att, prob, 1, 1).astype(BF)
        return carry

    lax.fori_loop(0, local // HEAD, one_head, 0, unroll=UNROLL)
    joined = work[0 : 3 * local, :]
    grads[...] = dot(joined, tok[...], 1, 0).astype(BF)
    bias[...] = dot(jnp.ones((8, joined.shape[1]), BF), joined, 1, 1)

    def out_rows(r):
        out[r, :] = grad_in[r, :] + dot(work[0 : 3 * local, r], weights[0 : 3 * local, :], 0, 0)

    by_halves(out.shape[0], out_rows)


def attention_back(saved, first_low, tokens, grad_in, pack):
    qkv, probs, _ = saved
    rows, width = tokens.shape
    joined = qkv.shape[0]
    return run(
        attention_back_kernel,
        "attention_back",
        [((joined, width), BF), ((8, joined), F32), ((rows, width), F32)],
        qkv,
        probs,
        first_low,
        tokens,
        grad_in,
        pack,
        scratch=[pltpu.VMEM((joined // 3 * 4, rows), BF)],
        estimate=cost(3.5e9, 6e6),
    )


def out_grad_kernel(a, b, c, d, low, send, keep):
    for ref, both in ((send, (a, c)), (keep, (b, d))):
        for i, att in enumerate(both):
            ref[i] = dot(att[...], low[...], 1, 0).astype(BF)


def out_grad(atts, low):
    shape = (2, atts[0].shape[0], low.shape[1])
    return run(
        out_grad_kernel, "out_grad", [(shape, BF)] * 2, *atts, low, estimate=cost(6e8, 3e6)
    )


def join(plan, base, *pieces):
    rows = sum(p.shape[0] for p in pieces)
    (out,) = run(
        functools.partial(join_kernel, base), "join", [((rows, pieces[0].shape[1]), BF)], *pieces,
        plan=plan,
    )
    return out


def add_rows(target, to, left, right, at, rows):
    block = next(b for b in (32, 24, 8) if rows % b == 0)

    def body(i, carry):
        here = pl.ds(pl.multiple_of(at + i * block, 8), block)
        there = pl.ds(pl.multiple_of(to + i * block, 8), block)
        total = left[here, :].astype(F32) + right[here, :].astype(F32)
        target[there, :] = total.astype(target.dtype)
        return carry

    lax.fori_loop(0, rows // block, body, 0)


def copy_rows(target, to, source, at, rows):
    block = next(b for b in (32, 24, 16, 8) if rows % b == 0)

    def body(i, carry):
        here = pl.ds(pl.multiple_of(at + i * block, 8), block)
        there = pl.ds(pl.multiple_of(to + i * block, 8), block)
        target[there, :] = source[here, :].astype(target.dtype)
        return carry

    lax.fori_loop(0, rows // block, body, 0)


VECTORS = 16


def send_vectors(value, sent):
    high = value.astype(BF)
    low = (value - high.astype(F32)).astype(BF)
    at = sent.shape[0] - 2 * VECTORS
    sent[at : at + VECTORS, :] = high
    sent[at + VECTORS :, :] = low
    return high.astype(F32) + low.astype(F32)


def got_vectors(got):
    at = got.shape[0] - 2 * VECTORS
    return got[at : at + VECTORS, :].astype(F32) + got[at + VECTORS :, :].astype(F32)


def collect(plan, attn, up, second, first, rows):
    span = attn[0].shape[1]
    rows[...] = jnp.zeros_like(rows)
    for shard in range(4):
        wide, narrow = jnp.zeros((1, rows.shape[1]), F32), jnp.zeros((1, span), F32)
        for apart in range(4):
            here = plan[SHARD] == shard ^ apart
            narrow = jnp.where(here, attn[apart][0:1, :], narrow)
            wide = jnp.where(here, up[apart][...], wide)
        rows[shard : shard + 1, 0:span] = narrow
        rows[4 + shard : 5 + shard, :] = wide
    rows[8:11, :] = second[0:3, :]
    rows[11:14, :] = first[0:3, :]


def choose(total, plan, base, count, sent, keep):
    rows = keep.shape[0] // count
    for i in range(count):
        for ref, at in ((sent, base + i), (keep, base + count + i)):
            copy_rows(ref, i * rows, total, pl.multiple_of(plan[at] * rows, rows), rows)


def first_kernel(segments, vectors, plan, *refs):
    if vectors:
        *ops, sent, keep, kept_vectors, rows = refs
        parts = ops[-10:]
        collect(plan, parts[:4], parts[4:8], parts[8], parts[9], rows)
        kept_vectors[...] = send_vectors(rows[...], sent)
    else:
        *ops, sent, keep = refs
    half = keep.shape[0] // 2
    for slot in range(4):
        target = (sent, keep)[slot // 2]
        for block in ((0, 1), (1, 2, 3), (0, 1, 2), (2, 3))[slot]:

            @pl.when(plan[FIRST + slot] == block)
            def _(slot=slot, block=block, target=target):
                begin, end = (block % 2) * half, (block % 2 + 1) * half
                at = 0
                for left, right, size in segments[block // 2]:
                    low, high = max(begin, at), min(end, at + size)
                    if low < high:
                        to = (slot % 2) * half + low - begin
                        add_rows(target, to, ops[left[0]].at[left[1]], ops[right[0]].at[right[1]], low - at, high - low)
                    at += size


def first_stage(plan, parts, stacked, vectors):
    width = parts[0].shape[-1]
    size = parts[0].shape[0]
    ops = [p[None] for p in parts] + list(stacked)
    segments = [[((0, 0), (1, 0), size)], [((2, 0), (3, 0), size)]]
    rows = size
    if stacked:
        rows += stacked[0].shape[1]
        for i in range(2):
            segments[i].append(((4, i), (5, i), rows - size))
    outs = [((rows, width), BF), ((rows, width), F32)]
    if vectors:
        outs = [((rows + 2 * VECTORS, width), BF), outs[1], ((VECTORS, width), F32)]
    return run(
        functools.partial(first_kernel, segments, bool(vectors)),
        "first_stage",
        outs,
        *ops,
        *vectors,
        scratch=[pltpu.VMEM((VECTORS, width), F32)] if vectors else [],
        plan=plan,
    )


def next_kernel(base, count, plan, kept, got, *refs):
    rows = kept.shape[0]
    if len(refs) > 3:
        had, sent, keep, has, total = refs
        has[...] = send_vectors(had[...] + got_vectors(got), sent)
    else:
        sent, keep, total = refs
    total[...] = kept[...] + got[0:rows, :].astype(F32)
    choose(total, plan, base, count, sent, keep)


def next_stage(plan, base, count, kept, got, vectors=()):
    rows, width = kept.shape
    outs = [((rows // 2, width), BF), ((rows // 2, width), F32)]
    if vectors:
        outs = [((rows // 2 + 2 * VECTORS, width), BF), outs[1], ((VECTORS, width), F32)]
    return run(
        functools.partial(next_kernel, base, count),
        "next_stage",
        outs,
        kept,
        got,
        *vectors,
        scratch=[pltpu.VMEM((rows, width), F32)],
        plan=plan,
    )


def finish_kernel(sizes, plan, mine, theirs, *refs):
    outs, (sums, sem) = refs[:-2], refs[-2:]
    rows = mine.shape[0] // 4
    copies = []
    for i in range(8):
        where = pl.ds(pl.multiple_of(plan[PLACES + i % 4] * rows, rows), rows)
        begin, end = i * rows, (i + 1) * rows
        sums[begin:end, :] = jnp.where(
            plan[SIDE] == i // 4, mine[where, :], theirs[where, :]
        ).astype(F32)
        at = 0
        for ref, size in zip(outs, sizes):
            low, high = max(begin, at), min(end, at + size)
            if low < high:
                source, target = sums.at[pl.ds(low, high - low)], ref.at[pl.ds(low - at, high - low)]
                copies.append(pltpu.make_async_copy(source, target, sem))
                copies[-1].start()
            at += size
    for copy in copies:
        copy.wait()


def finish(plan, mine, theirs, sizes):
    half, width = mine.shape
    return pl.pallas_call(
        functools.partial(finish_kernel, sizes),
        grid_spec=pltpu.PrefetchScalarGridSpec(
            num_scalar_prefetch=1,
            grid=(1,),
            in_specs=[whole((half, width))] * 2,
            out_specs=[ANY] * len(sizes),
            scratch_shapes=[pltpu.VMEM((2 * half, width), F32), pltpu.SemaphoreType.DMA(())],
        ),
        out_shape=[jax.ShapeDtypeStruct((size, width), F32) for size in sizes],
        compiler_params=params(),
        cost_estimate=SMALL,
        name="finish",
    )(plan, mine, theirs)


Y, X, Z_NEAR, Z_FAR = ("tensor", 2), ("dp", 1), ("dp", 2), ("dp", 4)


def tie(value, *others):
    return lax.optimization_barrier((value, others))[0]


def swap(value, even, odd=None):
    groups, width = lax.axis_size("dp"), lax.axis_size("tensor")
    pairs = []
    for group in range(groups):
        for t in range(width):
            axis, bit = even if odd is None or t % 2 == 0 else odd
            to = (group ^ bit, t) if axis == "dp" else (group, t ^ bit)
            pairs.append((group * width + t, to[0] * width + to[1]))
    return lax.ppermute(value, ("dp", "tensor"), pairs)


def partner(value):
    return swap(value, ("tensor", 1))


def make_plan():
    index, t = lax.axis_index("dp"), lax.axis_index("tensor")
    x, near, far, core = index % 2, index // 2 % 2, index // 4 % 2, t % 2
    quarter, place = x + 2 * near, near + 2 * far
    even = [quarter, quarter ^ 1, quarter ^ 2, quarter ^ 3]
    odd = [quarter, quarter ^ 2, quarter ^ 1, quarter ^ 3]
    even += odd + [0, 1, 2, 3]
    odd += even[:4] + [0, 1, 2, 3]
    even += [0, 1, 2, 3]
    odd += [1 - x, 3 - x, x, 2 + x]
    even += [1 - x, x]
    odd += [0, 1]
    even += [1 - near, 3 - near, near, 2 + near]
    odd += [2 - 2 * far, 3 - 2 * far, 2 * far, 2 * far + 1]
    even += [1 - far, far]
    odd += [1 - near, near]
    apart = [i ^ place for i in range(4)]
    even += [i // 2 + 2 * (i % 2) for i in apart]
    odd += apart
    quarters = [quarter ^ i for i in range(4)]
    even += [x, *quarters, t]
    odd += [x, *quarters, t]
    both = [jnp.stack([jnp.asarray(i, jnp.int32) for i in plan]) for plan in (even, odd)]
    return jnp.where(core == 0, *both)


class Gather:
    def __init__(self, plan, sent, tail=0):
        self.plan, self.tail = plan, tail
        self.got = swap(sent, Y)

    def after(self, *values):
        self.got = tie(self.got, *values)

    @classmethod
    def of_two(cls, plan, sent):
        return cls(plan, sent)

    def both(self):
        rows = self.got.shape[0] // 2
        self.held, self.far = self.got[:rows], self.got[rows:]
        self.got = [swap(self.held, X), swap(self.held, Z_NEAR)]

    def joined(self):
        return join(self.plan, QUARTERS, self.held, *self.got, self.far)

    def second(self):
        rows = self.got.shape[0] - self.tail
        self.rest = [self.got[rows:]] if self.tail else []
        self.held = self.got[:rows]
        self.got = swap(self.held, X, Z_NEAR)

    def third(self):
        self.held = jnp.concatenate([self.held, self.got], axis=0)
        self.got = swap(self.held, Z_NEAR, X)

    def result(self):
        rows = self.held.shape[0] // 2
        return join(
            self.plan, BY_B, self.held[:rows], self.held[rows:], self.got[:rows], self.got[rows:], *self.rest
        )


class Reduction:
    def __init__(self, plan):
        self.plan = plan

    def after(self, *values):
        self.got = tie(self.got, *values)

    def first(self, parts, stacked=(), vectors=()):
        self.sent, self.keep, *self.vectors = first_stage(self.plan, parts, stacked, vectors)
        self.got = swap(self.sent, Y, X)

    def next(self, base, count):
        self.sent, self.keep, *self.vectors = next_stage(
            self.plan, base, count, self.keep, self.got, self.vectors
        )

    def second(self):
        self.next(SECOND, 1)
        self.got = swap(self.sent, X, Y)

    def third(self):
        self.next(THIRD, 2)
        self.got = swap(self.sent, Z_NEAR, Z_FAR)

    def fourth(self):
        self.next(FOURTH, 1)
        self.got = swap(self.sent, Z_FAR, Z_NEAR)

    def fifth(self):
        rows = self.keep.shape[0]
        total = (self.keep + self.got[:rows].astype(F32)).astype(BF)
        if self.vectors:
            high, low = self.got[rows : rows + VECTORS], self.got[rows + VECTORS :]
            self.vectors = [self.vectors[0] + (high.astype(F32) + low.astype(F32))]
        bit = 8
        while bit < lax.axis_size("dp"):
            total = (total.astype(F32) + swap(total, ("dp", bit)).astype(F32)).astype(BF)
            self.vectors = [v + swap(v, ("dp", bit)) for v in self.vectors]
            bit *= 2
        self.sent = total
        self.got = swap(self.sent, Z_FAR, Z_NEAR)

    def sixth(self):
        self.sent = jnp.concatenate([self.sent, self.got], axis=0)
        self.got = swap(self.sent, Z_NEAR, Z_FAR)

    def seventh(self):
        self.sent = jnp.concatenate([self.sent, self.got], axis=0)
        self.got = swap(self.sent, X)

    def result(self, sizes):
        return finish(self.plan, self.sent, self.got, sizes)


def on_device(
    tokens,
    w_query,
    w_key,
    w_value,
    b_query,
    b_value,
    w_output,
    b_output,
    first_gain,
    first_shift,
    w_up,
    b_up,
    w_down,
    b_down,
    second_gain,
    second_shift,
    cotangent,
):
    rows, width = tokens.shape
    local = w_query.shape[1]
    assert rows == SEQ_LEN and width == 4 * local and w_up.shape == (width, width)
    plan = make_plan()
    near = pack_near(plan, w_query, w_key, w_value, w_output, (b_query, b_value, b_up))
    pack_d, up_far, down_far, table = pack_weights(
        tie(plan, near), w_query, w_key, w_value, w_output, w_up, w_down, near,
        (b_output, first_gain, first_shift, b_down, second_gain, second_shift),
    )

    far_pack = Gather(plan, near, BIAS_ROWS)
    up = Gather.of_two(plan, tie(up_far, near))
    pack_c = partner(tie(pack_d, near))
    far_pack.second()
    *saved_d, bias_d, part = attention(tie(tokens, far_pack.held), pack_d, small=True)
    far_pack.after(part)
    far_pack.third()
    down = Gather.of_two(plan, tie(down_far, far_pack.held))
    *saved_c, bias_c, part = attention(tokens, pack_c, tie(part, far_pack.held), small=True)
    far_pack.after(part)
    pack_b = far_pack.result()
    up.after(pack_b)
    up.both()
    pack_a = partner(pack_b)
    up_d, down_d = w_up, w_down
    up_c = partner(tie(w_up, pack_b))
    *saved_b, bias_b, part = attention(tokens, pack_b, tie(part, up.held))
    down.after(part)
    down.both()
    down_c = partner(tie(w_down, down.held))
    *saved_a, bias_a, normed, normed_low, unit, scale = attention(
        tokens, pack_a, tie(part, down.held), table
    )
    up.got, up.far = tie((up.got, up.far), normed)
    up_b = up.joined()
    up_a = partner(up_b)
    act_d, slope_d, part = feed(normed_low, up_d, down_d, bias_d, tie(normed, up_b))
    act_c, slope_c, part = feed(normed_low, up_c, down_c, bias_c, part)
    down.got, down.far = tie((down.got, down.far), part)
    down_b = down.joined()
    down_a = partner(down_b)
    act_b, slope_b, part = feed(normed_low, up_b, down_b, bias_b, part)
    act_a, slope_a, layer_out, down_low, grad_second, small_second = feed(
        normed_low, up_a, down_a, bias_a, part, [table, cotangent]
    )

    down, up, attn = Reduction(plan), Reduction(plan), Reduction(plan)
    grad_a, grad_b = down_grad([act_a, act_b], down_low)
    core_other = partner(grad_a)
    grad_c, grad_d = down_grad([act_c, act_d], tie(down_low, grad_a))
    core_own = partner(grad_c)
    up_grad_a, bias_up_a, part = feed_back(
        slope_a, down_low, normed_low, tie(grad_second, grad_c), up_a, down_a
    )
    core_up_other = partner(up_grad_a)
    down.first([grad_b, *tie((core_other,), up_grad_a), grad_d, core_own])
    up_grad_b, bias_up_b, part = feed_back(
        slope_b, down_low, normed_low, tie(part, down.sent), up_b, down_b
    )
    up_grad_c, bias_up_c, part = feed_back(
        slope_c, down_low, normed_low, tie(part, core_up_other), up_c, down_c
    )
    core_up_own = partner(up_grad_c)
    up_grad_d, bias_up_d, grad_first, first_low, small_first = feed_back(
        slope_d, down_low, normed_low, part, up_d, down_d, [unit, scale, table]
    )
    out_send, out_keep = out_grad([s[2] for s in (saved_a, saved_b, saved_c, saved_d)], first_low)
    core_out = partner(out_send)
    down.after(out_keep)
    down.second()
    grad_a, bias_a, part = attention_back(
        saved_a[:3], first_low, tokens, tie(grad_first, down.sent), pack_a
    )
    core_other = partner(grad_a)
    up.first([up_grad_b, core_up_other, up_grad_d, core_up_own], [out_keep, tie(core_out, grad_a)])
    down.after(up.sent)
    down.third()
    grad_b, bias_b, part = attention_back(
        saved_b, first_low, tokens, tie(part, down.sent), pack_b
    )
    grad_c, bias_c, part = attention_back(
        saved_c, first_low, tokens, tie(part, core_other), pack_c
    )
    core_own = partner(grad_c)
    up.after(grad_c)
    up.second()
    down.after(up.sent)
    down.fourth()
    grad_d, bias_d, grad_tokens = attention_back(
        saved_d, first_low, tokens, tie(part, down.sent), pack_d
    )
    down.after(grad_tokens)
    down.fifth()
    attn.first(
        [grad_b, core_other, grad_d, tie(core_own, down.sent, up.got)],
        vectors=[
            bias_d, bias_c, bias_b, bias_a, bias_up_d, bias_up_c, bias_up_b, bias_up_a,
            small_second, small_first,
        ],
    )

    up.after(attn.sent)
    up.third()
    down.after(up.sent)
    down.sixth()
    attn.after(down.sent)
    attn.second()
    up.after(attn.sent)
    up.fourth()
    down.after(up.sent)
    down.seventh()
    attn.after(down.sent)
    attn.third()
    up.after(attn.sent)
    up.fifth()
    attn.after(up.sent)
    attn.fourth()
    up.after(attn.sent)
    up.sixth()
    attn.after(up.sent)
    attn.fifth()
    (sums,) = attn.vectors
    others = partner(sums)
    up.after(attn.sent)
    up.seventh()
    down.after(up.sent)
    (grad_w_down,) = down.result((width,))
    attn.after(grad_w_down)
    attn.sixth()
    sums = sums + tie(others, attn.sent)
    shard = lax.axis_index("tensor")
    attn_vectors = lax.dynamic_index_in_dim(sums, shard, 0, keepdims=False)
    up_vector = lax.dynamic_index_in_dim(sums, 4 + shard, 0, keepdims=False)
    attn.after(attn_vectors, up_vector)
    attn.seventh()
    up.after(attn.sent)
    grad_w_up, grad_o = up.result((width, local))
    attn.after(grad_o)
    grad_q, grad_k, grad_v = attn.result((local,) * 3)

    return (
        tie(layer_out, attn.sent).astype(BF),
        tie(grad_tokens, attn.sent).astype(BF),
        grad_q.T,
        grad_k.T,
        grad_v.T,
        attn_vectors[:local],
        attn_vectors[2 * local : 3 * local],
        grad_o,
        sums[11],
        sums[12],
        sums[13],
        grad_w_up,
        up_vector,
        grad_w_down,
        sums[8],
        sums[9],
        sums[10],
    )


def solution(mesh):
    rows = P(("dp", "tensor"), None)
    col, row, vec, rep = P(None, "tensor"), P("tensor", None), P("tensor"), P()
    return jax.shard_map(
        on_device,
        mesh=mesh,
        in_specs=(
            rows, col, col, col, vec, vec, row, rep, rep, rep, col, vec, row, rep, rep, rep, rows,
        ),
        out_specs=(
            rows, rows, col, col, col, vec, vec, row, rep, rep, rep, col, vec, row, rep, rep, rep,
        ),
        check_vma=False,
    )
```

```python
import functools

import jax
import jax.numpy as jnp
from jax import lax
from jax.experimental import pallas as pl
from jax.experimental.pallas import tpu as pltpu
from jax.sharding import PartitionSpec as P

HEAD = 64
SEQ_LEN = 512
BIAS_ROWS = 16
BF = jnp.bfloat16
F32 = jnp.float32
ANY = pl.BlockSpec(memory_space=pl.ANY)
VMEM_BYTES = 26 << 20
BY_B, BY_A, NATURAL, FIRST, SECOND, THIRD, FOURTH, PLACES, SIDE, QUARTERS, SHARD = 0, 4, 8, 12, 16, 18, 22, 24, 28, 29, 33
ALL_VMEM_BYTES = 60 << 20
UNROLL = 1


def dot(left, right, left_dim, right_dim):
    return lax.dot_general(
        left, right, (((left_dim,), (right_dim,)), ((), ())), preferred_element_type=F32
    )


SMALL = pl.CostEstimate(flops=1000, bytes_accessed=1000, transcendentals=0)


def whole(shape):
    return pl.BlockSpec(shape, lambda *_: (0,) * len(shape))


def params(limit=VMEM_BYTES):
    return pltpu.CompilerParams(vmem_limit_bytes=limit)


def cost(flops, moved):
    return pl.CostEstimate(flops=int(20 * flops), bytes_accessed=int(20 * moved), transcendentals=0)


def run(kernel, name, outs, *ops, scratch=(), estimate=SMALL, plan=None):
    specs = [pl.BlockSpec(memory_space=pltpu.VMEM)] * len(ops)
    if plan is not None:
        ops = (plan, *ops)
        specs.insert(0, pl.BlockSpec(memory_space=pltpu.SMEM))
    return pl.pallas_call(
        kernel,
        in_specs=specs,
        out_specs=[pl.BlockSpec(memory_space=pltpu.VMEM)] * len(outs),
        out_shape=[jax.ShapeDtypeStruct(shape, dtype) for shape, dtype in outs],
        scratch_shapes=scratch,
        compiler_params=params(),
        cost_estimate=estimate,
        name=name,
    )(*ops)


def near_kernel(plan, wq, wk, wv, wo, bq, bv, bu, out, *lines):
    sem = lines[-1]
    local, width = wq.shape
    for i, ref in enumerate((wq, wk, wv, wo)):

        @pl.when(plan[BY_B] == i)
        def _(ref=ref):
            pltpu.make_async_copy(ref, out.at[pl.ds(0, local)], sem.at[0]).start()

    copies = [
        pltpu.make_async_copy(ref, line, sem.at[1]) for ref, line in zip((bq, bv, bu), lines)
    ]
    for copy in copies:
        copy.start()
    out[local:, :] = jnp.zeros((BIAS_ROWS, width), BF)
    for copy in copies:
        copy.wait()
    q, v, u = lines[:3]
    out[local : local + 1, 0:local] = q[...].reshape(1, local)
    out[local : local + 1, local : 2 * local] = v[...].reshape(1, local)
    out[local + 1 : local + 2, :] = u[...].reshape(1, width)
    pltpu.make_async_copy(wq, out.at[pl.ds(0, local)], sem.at[0]).wait()


def pack_near(plan, w_query, w_key, w_value, w_output, biases):
    local, width = w_output.shape
    (out,) = pl.pallas_call(
        near_kernel,
        in_specs=[pl.BlockSpec(memory_space=pltpu.SMEM)] + [ANY] * 7,
        out_specs=[pl.BlockSpec(memory_space=pltpu.VMEM)],
        out_shape=[jax.ShapeDtypeStruct((local + BIAS_ROWS, width), BF)],
        scratch_shapes=[
            *[pltpu.VMEM(v.shape, BF) for v in biases],
            pltpu.SemaphoreType.DMA((2,)),
        ],
        compiler_params=params(ALL_VMEM_BYTES),
        name="pack_near",
    )(plan, w_query.T, w_key.T, w_value.T, w_output, *biases)
    return out


def pack_kernel(plan, wq, wk, wv, wo, wu, wd, near, *refs):
    vectors, refs = refs[:6], refs[6:]
    out, up_far, down_far, table, packed, piece, lines, *lists, sem = refs
    local, width = wq.shape
    at = pl.multiple_of(plan[BY_B] * local, local)
    opposite = pl.multiple_of(plan[QUARTERS + 3] * local, local)
    pieces = [
        pltpu.make_async_copy(ref.at[pl.ds(rows, local)], piece.at[i], sem.at[1])
        for i, (ref, rows) in enumerate(((wu, at), (wu, opposite), (wd, at), (wd, opposite)))
    ]
    copies = [
        pltpu.make_async_copy(ref, packed.at[pl.ds(i * local, local)], sem.at[0])
        for i, ref in enumerate((wq, wk, wv, wo))
    ]
    copies.append(
        pltpu.make_async_copy(
            near.at[pl.ds(local, BIAS_ROWS)], packed.at[pl.ds(4 * local, BIAS_ROWS)], sem.at[0]
        )
    )
    copies += [
        pltpu.make_async_copy(ref, line, sem.at[0]) for ref, line in zip(vectors, lists)
    ]
    for copy in pieces:
        copy.start()
    for copy in copies:
        copy.start()
    lines[...] = jnp.zeros_like(lines)
    outs = []
    for copy in pieces:
        copy.wait()
    for i, ref in enumerate((up_far, down_far)):
        for h in range(2):
            part = ref.at[pl.ds(h * local, local)]
            outs.append(pltpu.make_async_copy(piece.at[2 * i + h], part, sem.at[2]))
            outs[-1].start()
    for copy in copies:
        copy.wait()
    outs.append(pltpu.make_async_copy(packed, out, sem.at[2]))
    outs[-1].start()
    for i, ref in enumerate(lists):
        lines[i : i + 1, :] = ref[...].astype(F32).reshape(1, width)
    outs.append(pltpu.make_async_copy(lines, table, sem.at[2]))
    outs[-1].start()
    for copy in outs:
        copy.wait()


def pack_weights(plan, w_query, w_key, w_value, w_output, w_up, w_down, near, vectors):
    local, width = w_output.shape
    shapes = [
        jax.ShapeDtypeStruct((4 * local + BIAS_ROWS, width), BF),
        *[jax.ShapeDtypeStruct((2 * local, width), BF)] * 2,
        jax.ShapeDtypeStruct((8, width), F32),
    ]
    return pl.pallas_call(
        pack_kernel,
        grid_spec=pltpu.PrefetchScalarGridSpec(
            num_scalar_prefetch=1,
            grid=(1,),
            in_specs=[ANY] * 13,
            out_specs=[ANY] * 4,
            scratch_shapes=[
                pltpu.VMEM(shapes[0].shape, BF),
                pltpu.VMEM((4, local, width), BF),
                pltpu.VMEM(shapes[3].shape, F32),
                *[pltpu.VMEM(v.shape, BF) for v in vectors],
                pltpu.SemaphoreType.DMA((3,)),
            ],
        ),
        out_shape=shapes,
        compiler_params=params(ALL_VMEM_BYTES),
        name="pack_weights",
    )(plan, w_query.T, w_key.T, w_value.T, w_output, w_up, w_down, near, *vectors)


def join_kernel(base, plan, *refs):
    *pieces, out = refs
    at = 0
    rows = pieces[0].shape[0]
    for ref in pieces:
        if at < 4:
            count = ref.shape[0] // rows
            for i in range(count):
                where = pl.multiple_of(plan[base + at + i] * rows, rows)
                copy_rows(out, where, ref, i * rows, rows)
            at += count
        else:
            out[4 * rows :, :] = ref[...]


def normalize(rows):
    center = rows - jnp.mean(rows, axis=-1, keepdims=True)
    scale = lax.rsqrt(jnp.mean(center * center, axis=-1, keepdims=True) + 1e-12)
    return center * scale, scale


def norm_back(grad, unit, scale):
    return scale * (
        grad
        - jnp.mean(grad, axis=-1, keepdims=True)
        - unit * jnp.mean(grad * unit, axis=-1, keepdims=True)
    )


def by_blocks(rows, body, block=128):
    def step(i, carry):
        body(pl.ds(pl.multiple_of(i * block, block), block))
        return carry

    lax.fori_loop(0, rows // block, step, 0)


def by_halves(rows, body):
    def step(i, carry):
        body(pl.ds(pl.multiple_of(i * (rows // 2), 128), rows // 2))
        return carry

    lax.fori_loop(0, 2, step, 0)


def head_rows(head, local, count):
    return [pl.ds(pl.multiple_of(i * local + head * HEAD, HEAD), HEAD) for i in range(count)]


def attention_kernel(first, last, small, *refs):
    tok, weights, *refs = refs
    if not first:
        part_in, *refs = refs
    if last:
        table, *refs = refs
        qkv, probs, att, bias_up, normed, normed_low, unit, scale, bias, part = refs
    else:
        qkv, probs, att, bias_up, part, bias = refs
    local = att.shape[0]
    body = 4 * local
    rows = weights[body : body + BIAS_ROWS, :].astype(F32)
    bias_up[...] = rows[1:2, :]
    column = jnp.transpose(rows)
    bias[...] = jnp.zeros_like(bias)
    bias[0:local, :] = column[0:local, 0:1]
    bias[2 * local : 3 * local, :] = column[local : 2 * local, 0:1]

    def project(i, carry):
        r = pl.ds(pl.multiple_of(i * local, local), local)
        rows = (dot(weights[r, :], tok[...], 1, 1) + bias[r, :]).astype(BF)
        qkv[r, :] = rows * jnp.where(i == 0, 0.125, 1.0).astype(BF)
        return carry

    lax.fori_loop(0, 3, project, 0, unroll=1 if small else 3)

    def one_head(head, carry):
        spans = head_rows(head, local, 3)
        queries, keys, values = (qkv[span, :] for span in spans)
        scores = dot(keys, queries, 0, 0)
        unnorm = jnp.exp(scores - jnp.max(scores, axis=0, keepdims=True))
        prob = (unnorm * (1.0 / jnp.sum(unnorm, axis=0, keepdims=True))).astype(BF)
        probs[head] = prob
        att[spans[0], :] = dot(values, prob, 1, 0).astype(BF)
        return carry

    lax.fori_loop(0, local // HEAD, one_head, 0, unroll=UNROLL)

    def out_rows(r):
        rows = dot(att[:, r], weights[3 * local : 4 * local, :], 0, 0)
        part[r, :] = rows if first else rows + part_in[r, :]

    by_halves(part.shape[0], out_rows)
    if last:

        def block(r):
            total = part[r, :] + table[0:1, :] + tok[r, :].astype(F32)
            unit_rows, scale_rows = normalize(total)
            unit[r, :] = unit_rows
            scale[r, :] = scale_rows
            rows = unit_rows * table[1:2, :] + table[2:3, :]
            normed[r, :] = rows
            normed_low[r, :] = rows.astype(BF)

        by_blocks(tok.shape[0], block)


def attention(tokens, pack, part=None, table=None, small=False):
    rows, width = tokens.shape
    local = (pack.shape[0] - BIAS_ROWS) // 4
    first, last = part is None, table is not None
    ops = [tokens, pack] + [x for x in (part, table) if x is not None]
    outs = [((3 * local, rows), BF), ((local // HEAD, rows, rows), BF), ((local, rows), BF)]
    outs += [((1, width), F32)]
    if last:
        outs += [((rows, width), F32), ((rows, width), BF), ((rows, width), F32), ((rows, 1), F32)]
    else:
        outs += [((rows, width), F32)]
    return run(
        functools.partial(attention_kernel, first, last, small),
        "attention_last" if last else "attention",
        outs,
        *ops,
        scratch=[pltpu.VMEM((3 * local, 1), F32)] + [pltpu.VMEM((rows, width), F32)] * last,
        estimate=cost(2.5e9, 4e6),
    )


def feed_kernel(last, *refs):
    low, up, down, bias, part_in, *refs = refs
    if last:
        table, cot, act, slope, layer_out, down_low, grad_second, small, part = refs
    else:
        act, slope, part = refs
    rows = dot(low[...], up[...], 1, 0) + bias[...]
    cdf = 0.5 * (1.0 + lax.erf(rows * 0.7071067811865476))
    active = (rows * cdf).astype(BF)
    act[...] = active
    slope[...] = (cdf + (rows * 0.3989422804014327) * jnp.exp(-0.5 * rows * rows)).astype(BF)
    part[...] = part_in[...] + dot(active, down[...], 1, 0)
    if last:
        small[...] = jnp.zeros_like(small)

        def block(r):
            unit2, scale2 = normalize(part[r, :] + table[3:4, :])
            layer_out[r, :] = unit2 * table[4:5, :] + table[5:6, :]
            cots = cot[r, :].astype(F32)
            grad = norm_back(cots * table[4:5, :], unit2, scale2)
            grad_second[r, :] = grad
            down_low[r, :] = grad.astype(BF)
            small[0:1, :] += jnp.sum(grad, axis=0, keepdims=True)
            small[1:2, :] += jnp.sum(cots * unit2, axis=0, keepdims=True)
            small[2:3, :] += jnp.sum(cots, axis=0, keepdims=True)

        by_blocks(low.shape[0], block)


def feed(low, up, down, bias, part, extra=None):
    rows, width = low.shape
    hidden = up.shape[1]
    last = extra is not None
    ops = [low, up, down, bias, part, *(extra or [])]
    outs = [((rows, hidden), BF)] * 2
    if last:
        outs += [((rows, width), F32), ((rows, width), BF), ((rows, width), F32), ((8, width), F32)]
    else:
        outs += [((rows, width), F32)]
    return run(
        functools.partial(feed_kernel, last),
        "feed_last" if last else "feed",
        outs,
        *ops,
        scratch=[pltpu.VMEM((rows, width), F32)] if last else [],
        estimate=cost(2.5e9 if last else 1.5e9, 4e6),
    )


def down_grad_kernel(*refs):
    count = len(refs) // 2
    low = refs[count]
    for act, out in zip(refs[:count], refs[count + 1 :]):

        out[...] = dot(act[...], low[...], 0, 0).astype(BF)


def down_grad(acts, low):
    return run(
        down_grad_kernel,
        "down_grad",
        [((acts[0].shape[1], low.shape[1]), BF)] * len(acts),
        *acts,
        low,
        estimate=cost(1.2e9, 4e6),
    )


def feed_back_kernel(last, *refs):
    slope, down_low, normed_low, grad_in, up, down, *refs = refs
    if last:
        unit, scale, table, grads, bias, grad_first, first_low, small, part = refs
    else:
        grads, bias, part = refs
    grad_up = (dot(down_low[...], down[...], 1, 1) * slope[...].astype(F32)).astype(BF)
    bias[...] = jnp.sum(grad_up.astype(F32), axis=0, keepdims=True)

    def grad_rows(r):
        grads[r, :] = dot(normed_low[:, r], grad_up, 0, 0).astype(BF)

    if last:
        by_halves(grads.shape[0], grad_rows)
    else:
        grad_rows(slice(None))
    part[...] = grad_in[...] + dot(grad_up, up[...], 1, 1)
    if last:
        small[...] = jnp.zeros_like(small)

        def block(r):
            grad = part[r, :]
            units = unit[r, :]
            first = norm_back(grad * table[1:2, :], units, scale[r, :])
            grad_first[r, :] = first
            first_low[r, :] = first.astype(BF)
            small[0:1, :] += jnp.sum(first, axis=0, keepdims=True)
            small[1:2, :] += jnp.sum(grad * units, axis=0, keepdims=True)
            small[2:3, :] += jnp.sum(grad, axis=0, keepdims=True)

        by_blocks(part.shape[0], block)


def feed_back(slope, down_low, normed_low, grad_in, up, down, extra=None):
    rows, width = down_low.shape
    hidden = up.shape[1]
    last = extra is not None
    outs = [((width, hidden), BF), ((1, hidden), F32), ((rows, width), F32)]
    if last:
        outs += [((rows, width), BF), ((8, width), F32)]
    return run(
        functools.partial(feed_back_kernel, last),
        "feed_back_last" if last else "feed_back",
        outs,
        slope,
        down_low,
        normed_low,
        grad_in,
        up,
        down,
        *(extra or []),
        scratch=[pltpu.VMEM((rows, width), F32)] if last else [],
        estimate=cost(2.5e9 if last else 2e9, 5e6),
    )


def attention_back_kernel(qkv, probs, first_low, tok, grad_in, weights, grads, bias, out, work):
    local = qkv.shape[0] // 3
    work[3 * local :, :] = dot(weights[3 * local : 4 * local, :], first_low[...], 1, 1).astype(BF)

    def one_head(head, carry):
        spans = head_rows(head, local, 4)
        queries, keys, values = (qkv[span, :] for span in spans[:3])
        grad_att = work[spans[3], :]
        prob = probs[head]
        grad_prob = dot(values, grad_att, 0, 0)
        wide = prob.astype(F32)
        inner = jnp.sum(wide * grad_prob, axis=0, keepdims=True)
        grad_score = (wide * (grad_prob - inner)).astype(BF)
        work[spans[0], :] = (dot(keys, grad_score, 1, 0) * 0.125).astype(BF)
        work[spans[1], :] = dot(queries, grad_score, 1, 1).astype(BF)
        work[spans[2], :] = dot(grad_att, prob, 1, 1).astype(BF)
        return carry

    lax.fori_loop(0, local // HEAD, one_head, 0, unroll=UNROLL)
    joined = work[0 : 3 * local, :]
    grads[...] = dot(joined, tok[...], 1, 0).astype(BF)
    bias[...] = dot(jnp.ones((8, joined.shape[1]), BF), joined, 1, 1)

    def out_rows(r):
        out[r, :] = grad_in[r, :] + dot(work[0 : 3 * local, r], weights[0 : 3 * local, :], 0, 0)

    by_halves(out.shape[0], out_rows)


def attention_back(saved, first_low, tokens, grad_in, pack):
    qkv, probs, _ = saved
    rows, width = tokens.shape
    joined = qkv.shape[0]
    return run(
        attention_back_kernel,
        "attention_back",
        [((joined, width), BF), ((8, joined), F32), ((rows, width), F32)],
        qkv,
        probs,
        first_low,
        tokens,
        grad_in,
        pack,
        scratch=[pltpu.VMEM((joined // 3 * 4, rows), BF)],
        estimate=cost(3.5e9, 6e6),
    )


def out_grad_kernel(a, b, c, d, low, send, keep):
    for ref, both in ((send, (a, c)), (keep, (b, d))):
        for i, att in enumerate(both):
            ref[i] = dot(att[...], low[...], 1, 0).astype(BF)


def out_grad(atts, low):
    shape = (2, atts[0].shape[0], low.shape[1])
    return run(
        out_grad_kernel, "out_grad", [(shape, BF)] * 2, *atts, low, estimate=cost(6e8, 3e6)
    )


def join(plan, base, *pieces):
    rows = sum(p.shape[0] for p in pieces)
    (out,) = run(
        functools.partial(join_kernel, base), "join", [((rows, pieces[0].shape[1]), BF)], *pieces,
        plan=plan,
    )
    return out


def add_rows(target, to, left, right, at, rows):
    block = next(b for b in (32, 24, 8) if rows % b == 0)

    def body(i, carry):
        here = pl.ds(pl.multiple_of(at + i * block, 8), block)
        there = pl.ds(pl.multiple_of(to + i * block, 8), block)
        total = left[here, :].astype(F32) + right[here, :].astype(F32)
        target[there, :] = total.astype(target.dtype)
        return carry

    lax.fori_loop(0, rows // block, body, 0)


def copy_rows(target, to, source, at, rows):
    block = next(b for b in (32, 24, 16, 8) if rows % b == 0)

    def body(i, carry):
        here = pl.ds(pl.multiple_of(at + i * block, 8), block)
        there = pl.ds(pl.multiple_of(to + i * block, 8), block)
        target[there, :] = source[here, :].astype(target.dtype)
        return carry

    lax.fori_loop(0, rows // block, body, 0)


VECTORS = 16


def send_vectors(value, sent):
    high = value.astype(BF)
    low = (value - high.astype(F32)).astype(BF)
    at = sent.shape[0] - 2 * VECTORS
    sent[at : at + VECTORS, :] = high
    sent[at + VECTORS :, :] = low
    return high.astype(F32) + low.astype(F32)


def got_vectors(got):
    at = got.shape[0] - 2 * VECTORS
    return got[at : at + VECTORS, :].astype(F32) + got[at + VECTORS :, :].astype(F32)


def collect(plan, attn, up, second, first, rows):
    span = attn[0].shape[1]
    rows[...] = jnp.zeros_like(rows)
    for shard in range(4):
        wide, narrow = jnp.zeros((1, rows.shape[1]), F32), jnp.zeros((1, span), F32)
        for apart in range(4):
            here = plan[SHARD] == shard ^ apart
            narrow = jnp.where(here, attn[apart][0:1, :], narrow)
            wide = jnp.where(here, up[apart][...], wide)
        rows[shard : shard + 1, 0:span] = narrow
        rows[4 + shard : 5 + shard, :] = wide
    rows[8:11, :] = second[0:3, :]
    rows[11:14, :] = first[0:3, :]


def choose(total, plan, base, count, sent, keep):
    rows = keep.shape[0] // count
    for i in range(count):
        for ref, at in ((sent, base + i), (keep, base + count + i)):
            copy_rows(ref, i * rows, total, pl.multiple_of(plan[at] * rows, rows), rows)


def first_kernel(segments, vectors, plan, *refs):
    if vectors:
        *ops, sent, keep, kept_vectors, rows = refs
        parts = ops[-10:]
        collect(plan, parts[:4], parts[4:8], parts[8], parts[9], rows)
        kept_vectors[...] = send_vectors(rows[...], sent)
    else:
        *ops, sent, keep = refs
    half = keep.shape[0] // 2
    for slot in range(4):
        target = (sent, keep)[slot // 2]
        for block in ((0, 1), (1, 2, 3), (0, 1, 2), (2, 3))[slot]:

            @pl.when(plan[FIRST + slot] == block)
            def _(slot=slot, block=block, target=target):
                begin, end = (block % 2) * half, (block % 2 + 1) * half
                at = 0
                for left, right, size in segments[block // 2]:
                    low, high = max(begin, at), min(end, at + size)
                    if low < high:
                        to = (slot % 2) * half + low - begin
                        add_rows(target, to, ops[left[0]].at[left[1]], ops[right[0]].at[right[1]], low - at, high - low)
                    at += size


def first_stage(plan, parts, stacked, vectors):
    width = parts[0].shape[-1]
    size = parts[0].shape[0]
    ops = [p[None] for p in parts] + list(stacked)
    segments = [[((0, 0), (1, 0), size)], [((2, 0), (3, 0), size)]]
    rows = size
    if stacked:
        rows += stacked[0].shape[1]
        for i in range(2):
            segments[i].append(((4, i), (5, i), rows - size))
    outs = [((rows, width), BF), ((rows, width), F32)]
    if vectors:
        outs = [((rows + 2 * VECTORS, width), BF), outs[1], ((VECTORS, width), F32)]
    return run(
        functools.partial(first_kernel, segments, bool(vectors)),
        "first_stage",
        outs,
        *ops,
        *vectors,
        scratch=[pltpu.VMEM((VECTORS, width), F32)] if vectors else [],
        plan=plan,
    )


def next_kernel(base, count, plan, kept, got, *refs):
    rows = kept.shape[0]
    if len(refs) > 3:
        had, sent, keep, has, total = refs
        has[...] = send_vectors(had[...] + got_vectors(got), sent)
    else:
        sent, keep, total = refs
    total[...] = kept[...] + got[0:rows, :].astype(F32)
    choose(total, plan, base, count, sent, keep)


def next_stage(plan, base, count, kept, got, vectors=()):
    rows, width = kept.shape
    outs = [((rows // 2, width), BF), ((rows // 2, width), F32)]
    if vectors:
        outs = [((rows // 2 + 2 * VECTORS, width), BF), outs[1], ((VECTORS, width), F32)]
    return run(
        functools.partial(next_kernel, base, count),
        "next_stage",
        outs,
        kept,
        got,
        *vectors,
        scratch=[pltpu.VMEM((rows, width), F32)],
        plan=plan,
    )


def finish_kernel(sizes, plan, mine, theirs, *refs):
    outs, (sums, sem) = refs[:-2], refs[-2:]
    rows = mine.shape[0] // 4
    copies = []
    for i in range(8):
        where = pl.ds(pl.multiple_of(plan[PLACES + i % 4] * rows, rows), rows)
        begin, end = i * rows, (i + 1) * rows
        sums[begin:end, :] = jnp.where(
            plan[SIDE] == i // 4, mine[where, :], theirs[where, :]
        ).astype(F32)
        at = 0
        for ref, size in zip(outs, sizes):
            low, high = max(begin, at), min(end, at + size)
            if low < high:
                source, target = sums.at[pl.ds(low, high - low)], ref.at[pl.ds(low - at, high - low)]
                copies.append(pltpu.make_async_copy(source, target, sem))
                copies[-1].start()
            at += size
    for copy in copies:
        copy.wait()


def finish(plan, mine, theirs, sizes):
    half, width = mine.shape
    return pl.pallas_call(
        functools.partial(finish_kernel, sizes),
        grid_spec=pltpu.PrefetchScalarGridSpec(
            num_scalar_prefetch=1,
            grid=(1,),
            in_specs=[whole((half, width))] * 2,
            out_specs=[ANY] * len(sizes),
            scratch_shapes=[pltpu.VMEM((2 * half, width), F32), pltpu.SemaphoreType.DMA(())],
        ),
        out_shape=[jax.ShapeDtypeStruct((size, width), F32) for size in sizes],
        compiler_params=params(),
        cost_estimate=SMALL,
        name="finish",
    )(plan, mine, theirs)


Y, X, Z_NEAR, Z_FAR = ("tensor", 2), ("dp", 1), ("dp", 2), ("dp", 4)


def tie(value, *others):
    return lax.optimization_barrier((value, others))[0]


def swap(value, even, odd=None):
    groups, width = lax.axis_size("dp"), lax.axis_size("tensor")
    pairs = []
    for group in range(groups):
        for t in range(width):
            axis, bit = even if odd is None or t % 2 == 0 else odd
            to = (group ^ bit, t) if axis == "dp" else (group, t ^ bit)
            pairs.append((group * width + t, to[0] * width + to[1]))
    return lax.ppermute(value, ("dp", "tensor"), pairs)


def partner(value):
    return swap(value, ("tensor", 1))


def make_plan():
    index, t = lax.axis_index("dp"), lax.axis_index("tensor")
    x, near, far, core = index % 2, index // 2 % 2, index // 4 % 2, t % 2
    quarter, place = x + 2 * near, near + 2 * far
    even = [quarter, quarter ^ 1, quarter ^ 2, quarter ^ 3]
    odd = [quarter, quarter ^ 2, quarter ^ 1, quarter ^ 3]
    even += odd + [0, 1, 2, 3]
    odd += even[:4] + [0, 1, 2, 3]
    even += [0, 1, 2, 3]
    odd += [1 - x, 3 - x, x, 2 + x]
    even += [1 - x, x]
    odd += [0, 1]
    even += [1 - near, 3 - near, near, 2 + near]
    odd += [2 - 2 * far, 3 - 2 * far, 2 * far, 2 * far + 1]
    even += [1 - far, far]
    odd += [1 - near, near]
    apart = [i ^ place for i in range(4)]
    even += [i // 2 + 2 * (i % 2) for i in apart]
    odd += apart
    quarters = [quarter ^ i for i in range(4)]
    even += [x, *quarters, t]
    odd += [x, *quarters, t]
    both = [jnp.stack([jnp.asarray(i, jnp.int32) for i in plan]) for plan in (even, odd)]
    return jnp.where(core == 0, *both)


class Gather:
    def __init__(self, plan, sent, tail=0):
        self.plan, self.tail = plan, tail
        self.got = swap(sent, Y)

    def after(self, *values):
        self.got = tie(self.got, *values)

    @classmethod
    def of_two(cls, plan, sent):
        return cls(plan, sent)

    def both(self):
        rows = self.got.shape[0] // 2
        self.held, self.far = self.got[:rows], self.got[rows:]
        self.got = [swap(self.held, X), swap(self.held, Z_NEAR)]

    def joined(self):
        return join(self.plan, QUARTERS, self.held, *self.got, self.far)

    def second(self):
        rows = self.got.shape[0] - self.tail
        self.rest = [self.got[rows:]] if self.tail else []
        self.held = self.got[:rows]
        self.got = swap(self.held, X, Z_NEAR)

    def third(self):
        self.held = jnp.concatenate([self.held, self.got], axis=0)
        self.got = swap(self.held, Z_NEAR, X)

    def result(self):
        rows = self.held.shape[0] // 2
        return join(
            self.plan, BY_B, self.held[:rows], self.held[rows:], self.got[:rows], self.got[rows:], *self.rest
        )


class Reduction:
    def __init__(self, plan):
        self.plan = plan

    def after(self, *values):
        self.got = tie(self.got, *values)

    def first(self, parts, stacked=(), vectors=()):
        self.sent, self.keep, *self.vectors = first_stage(self.plan, parts, stacked, vectors)
        self.got = swap(self.sent, Y, X)

    def next(self, base, count):
        self.sent, self.keep, *self.vectors = next_stage(
            self.plan, base, count, self.keep, self.got, self.vectors
        )

    def second(self):
        self.next(SECOND, 1)
        self.got = swap(self.sent, X, Y)

    def third(self):
        self.next(THIRD, 2)
        self.got = swap(self.sent, Z_NEAR, Z_FAR)

    def fourth(self):
        self.next(FOURTH, 1)
        self.got = swap(self.sent, Z_FAR, Z_NEAR)

    def fifth(self):
        rows = self.keep.shape[0]
        total = (self.keep + self.got[:rows].astype(F32)).astype(BF)
        if self.vectors:
            high, low = self.got[rows : rows + VECTORS], self.got[rows + VECTORS :]
            self.vectors = [self.vectors[0] + (high.astype(F32) + low.astype(F32))]
        bit = 8
        while bit < lax.axis_size("dp"):
            total = (total.astype(F32) + swap(total, ("dp", bit)).astype(F32)).astype(BF)
            self.vectors = [v + swap(v, ("dp", bit)) for v in self.vectors]
            bit *= 2
        self.sent = total
        self.got = swap(self.sent, Z_FAR, Z_NEAR)

    def sixth(self):
        self.sent = jnp.concatenate([self.sent, self.got], axis=0)
        self.got = swap(self.sent, Z_NEAR, Z_FAR)

    def seventh(self):
        self.sent = jnp.concatenate([self.sent, self.got], axis=0)
        self.got = swap(self.sent, X)

    def result(self, sizes):
        return finish(self.plan, self.sent, self.got, sizes)


def on_device(
    tokens,
    w_query,
    w_key,
    w_value,
    b_query,
    b_value,
    w_output,
    b_output,
    first_gain,
    first_shift,
    w_up,
    b_up,
    w_down,
    b_down,
    second_gain,
    second_shift,
    cotangent,
):
    rows, width = tokens.shape
    local = w_query.shape[1]
    assert rows == SEQ_LEN and width == 4 * local and w_up.shape == (width, width)
    plan = make_plan()
    near = pack_near(plan, w_query, w_key, w_value, w_output, (b_query, b_value, b_up))
    pack_d, up_far, down_far, table = pack_weights(
        tie(plan, near), w_query, w_key, w_value, w_output, w_up, w_down, near,
        (b_output, first_gain, first_shift, b_down, second_gain, second_shift),
    )

    far_pack = Gather(plan, near, BIAS_ROWS)
    up = Gather.of_two(plan, tie(up_far, near))
    pack_c = partner(tie(pack_d, near))
    far_pack.second()
    *saved_d, bias_d, part = attention(tie(tokens, far_pack.held), pack_d, small=True)
    far_pack.after(part)
    far_pack.third()
    down = Gather.of_two(plan, tie(down_far, far_pack.held))
    *saved_c, bias_c, part = attention(tokens, pack_c, tie(part, far_pack.held), small=True)
    far_pack.after(part)
    pack_b = far_pack.result()
    up.after(pack_b)
    up.both()
    pack_a = partner(pack_b)
    up_d, down_d = w_up, w_down
    up_c = partner(tie(w_up, pack_b))
    *saved_b, bias_b, part = attention(tokens, pack_b, tie(part, up.held))
    down.after(part)
    down.both()
    down_c = partner(tie(w_down, down.held))
    *saved_a, bias_a, normed, normed_low, unit, scale = attention(
        tokens, pack_a, tie(part, down.held), table
    )
    up.got, up.far = tie((up.got, up.far), normed)
    up_b = up.joined()
    up_a = partner(up_b)
    act_d, slope_d, part = feed(normed_low, up_d, down_d, bias_d, tie(normed, up_b))
    act_c, slope_c, part = feed(normed_low, up_c, down_c, bias_c, part)
    down.got, down.far = tie((down.got, down.far), part)
    down_b = down.joined()
    down_a = partner(down_b)
    act_b, slope_b, part = feed(normed_low, up_b, down_b, bias_b, part)
    act_a, slope_a, layer_out, down_low, grad_second, small_second = feed(
        normed_low, up_a, down_a, bias_a, part, [table, cotangent]
    )

    down, up, attn = Reduction(plan), Reduction(plan), Reduction(plan)
    grad_a, grad_b = down_grad([act_a, act_b], down_low)
    core_other = partner(grad_a)
    grad_c, grad_d = down_grad([act_c, act_d], tie(down_low, grad_a))
    core_own = partner(grad_c)
    up_grad_a, bias_up_a, part = feed_back(
        slope_a, down_low, normed_low, tie(grad_second, grad_c), up_a, down_a
    )
    core_up_other = partner(up_grad_a)
    down.first([grad_b, *tie((core_other,), up_grad_a), grad_d, core_own])
    up_grad_b, bias_up_b, part = feed_back(
        slope_b, down_low, normed_low, tie(part, down.sent), up_b, down_b
    )
    up_grad_c, bias_up_c, part = feed_back(
        slope_c, down_low, normed_low, tie(part, core_up_other), up_c, down_c
    )
    core_up_own = partner(up_grad_c)
    up_grad_d, bias_up_d, grad_first, first_low, small_first = feed_back(
        slope_d, down_low, normed_low, part, up_d, down_d, [unit, scale, table]
    )
    out_send, out_keep = out_grad([s[2] for s in (saved_a, saved_b, saved_c, saved_d)], first_low)
    core_out = partner(out_send)
    down.after(out_keep)
    down.second()
    grad_a, bias_a, part = attention_back(
        saved_a[:3], first_low, tokens, tie(grad_first, down.sent), pack_a
    )
    core_other = partner(grad_a)
    up.first([up_grad_b, core_up_other, up_grad_d, core_up_own], [out_keep, tie(core_out, grad_a)])
    down.after(up.sent)
    down.third()
    grad_b, bias_b, part = attention_back(
        saved_b, first_low, tokens, tie(part, down.sent), pack_b
    )
    grad_c, bias_c, part = attention_back(
        saved_c, first_low, tokens, tie(part, core_other), pack_c
    )
    core_own = partner(grad_c)
    up.after(grad_c)
    up.second()
    down.after(up.sent)
    down.fourth()
    grad_d, bias_d, grad_tokens = attention_back(
        saved_d, first_low, tokens, tie(part, down.sent), pack_d
    )
    down.after(grad_tokens)
    down.fifth()
    attn.first(
        [grad_b, core_other, grad_d, tie(core_own, down.sent, up.got)],
        vectors=[
            bias_d, bias_c, bias_b, bias_a, bias_up_d, bias_up_c, bias_up_b, bias_up_a,
            small_second, small_first,
        ],
    )

    up.after(attn.sent)
    up.third()
    down.after(up.sent)
    down.sixth()
    attn.after(down.sent)
    attn.second()
    up.after(attn.sent)
    up.fourth()
    down.after(up.sent)
    down.seventh()
    attn.after(down.sent)
    attn.third()
    up.after(attn.sent)
    up.fifth()
    attn.after(up.sent)
    attn.fourth()
    up.after(attn.sent)
    up.sixth()
    attn.after(up.sent)
    attn.fifth()
    (sums,) = attn.vectors
    others = partner(sums)
    up.after(attn.sent)
    up.seventh()
    down.after(up.sent)
    (grad_w_down,) = down.result((width,))
    attn.after(grad_w_down)
    attn.sixth()
    sums = sums + tie(others, attn.sent)
    shard = lax.axis_index("tensor")
    attn_vectors = lax.dynamic_index_in_dim(sums, shard, 0, keepdims=False)
    up_vector = lax.dynamic_index_in_dim(sums, 4 + shard, 0, keepdims=False)
    attn.after(attn_vectors, up_vector)
    attn.seventh()
    up.after(attn.sent)
    grad_w_up, grad_o = up.result((width, local))
    attn.after(grad_o)
    grad_q, grad_k, grad_v = attn.result((local,) * 3)

    return (
        tie(layer_out, attn.sent).astype(BF),
        tie(grad_tokens, attn.sent).astype(BF),
        grad_q.T,
        grad_k.T,
        grad_v.T,
        attn_vectors[:local],
        attn_vectors[2 * local : 3 * local],
        grad_o,
        sums[11],
        sums[12],
        sums[13],
        grad_w_up,
        up_vector,
        grad_w_down,
        sums[8],
        sums[9],
        sums[10],
    )


def solution(mesh):
    rows = P(("dp", "tensor"), None)
    col, row, vec, rep = P(None, "tensor"), P("tensor", None), P("tensor"), P()
    return jax.shard_map(
        on_device,
        mesh=mesh,
        in_specs=(
            rows, col, col, col, vec, vec, row, rep, rep, rep, col, vec, row, rep, rep, rep, rows,
        ),
        out_specs=(
            rows, rows, col, col, col, vec, vec, row, rep, rep, rep, col, vec, row, rep, rep, rep,
        ),
        check_vma=False,
    )
```
